32 devices in a mesh: shard: 4 (over z), ctx: 2 (over x), tp: 4 (over y, core).
Axes of the slice: x: 2, y: 2, z: 4, core: 2. Of those that a mesh axis runs over, the one named last changes fastest.
Arguments:
- tokens: bfloat16 [2, 10240, 768], P(None, ('shard', 'ctx')), may hold values from -6 to 6
- cotangent: bfloat16 [2, 10240, 768], P(None, ('shard', 'ctx')), may hold values from -6 to 6
- block_path: int32 [2, 3, 80], P(None, None, 'shard'), may hold values from 0 to 12, as said below
- labels: int32 [2, 80], P(None, ('shard', 'ctx')), may hold values from 0 to 13
- w_attn_in: bfloat16 [3, 768, 768], P(None, 'shard', 'tp'), may hold values from -0.21875 to 0.21875
- attn_bias: bfloat16 [2, 768], P(None, 'tp'), may hold values from -3 to 3
- w_attn_out: bfloat16 [768, 768], P('tp', 'shard'), may hold values from -6 to 6
- w_up: bfloat16 [768, 3072], P('shard', 'tp'), may hold values from -0.21875 to 0.21875
- up_bias: bfloat16 [3072], P('tp'), may hold values from -3 to 3
- w_down: bfloat16 [3072, 768], P('tp', 'shard'), may hold values from -0.109375 to 0.109375
- norm_gain: bfloat16 [2, 768], replicated, may hold values from 0.25 to 1.75
- layer_bias: bfloat16 [4, 768], replicated, may hold values from -3 to 3
- stu_proj: bfloat16 [768, 128], P('shard'), may hold values from -0.21875 to 0.21875
- stu_bias: bfloat16 [2, 128], replicated, may hold values from -1.1953125 to 1.1953125
- pool_query: bfloat16 [128], replicated, may hold values from -6 to 6
- stu_dense: bfloat16 [128, 128], replicated, may hold values from -2 to 2
- stu_head: bfloat16 [128, 14], replicated, may hold values from -1 to 1
- class_bias: bfloat16 [14], replicated, may hold values from -3 to 3
Outputs:
- block_out: bfloat16 [2, 10240, 768], P(None, ('shard', 'ctx'))
- tokens_grad: float32 [2, 10240, 768], P(None, ('shard', 'ctx'))
- grad_w_attn_in: float32 [3, 768, 768], P(None, 'shard', 'tp')
- grad_attn_bias: float32 [2, 768], P(None, 'tp')
- grad_w_attn_out: float32 [768, 768], P('tp', 'shard')
- grad_w_up: float32 [768, 3072], P('shard', 'tp')
- grad_up_bias: float32 [3072], P('tp')
- grad_w_down: float32 [3072, 768], P('tp', 'shard')
- grad_norm_gain: float32 [2, 768], replicated
- grad_layer_bias: float32 [4, 768], replicated
- grad_stu_proj: float32 [768, 128], P('shard')
- grad_stu_bias: float32 [2, 128], replicated
- grad_pool_query: float32 [128], replicated
- grad_stu_dense: float32 [128, 128], replicated
- grad_stu_head: float32 [128, 14], replicated
- grad_class_bias: float32 [14], replicated
The draws below stay inside these ranges and needn't reach their ends.
Inputs may be any that keep to these rules, and one draw needn't show every extreme that they name: `block_path`: in each micro-batch and shard index, ctx indices 2 t and 2 t + 1 hold the 20 blocks of one tree: the even one its eight trunk blocks and two of its four branch blocks, the odd one the other two branch blocks and its eight leaf blocks, in any order; every branch has two leaves. A trunk block's path is (trunk, trunk, trunk), a branch block's (trunk, branch, branch), a leaf block's (trunk, branch, leaf); node ids of different trees of a shard index differ.
All inputs are finite; a program needn't handle non-finite values.
Results may differ from the reference program's by a relative error of at most 0.028.
Values may be sent and summed in bfloat16 or wider, within the bound.
No kernel may reach another device: no remote copies, remote signals or barrier semaphores. Data moves between devices by JAX's collectives and lax.ppermute only.
A program may use at most 192 MiB of HBM per device.

```python
import jax
import jax.numpy as jnp
from jax import lax

D = 768
HEAD_DIM = 64
FF = 3072
STU = 128
POOL_HEADS = 2
CLASSES = 14
BLOCK = 128
BLK_DEV = 10
MB = 2
TREES_GROUP = 1
NBLOCKS = 80
TOKENS = 10240
N_TP = 4


def draw_block_path(key, part):
    per_micro = NBLOCKS // 20
    tree_total = MB * per_micro
    tree_keys = jax.random.split(key, tree_total)

    def one_tree(tree_key):
        key_a, key_b, key_c, key_d = jax.random.split(tree_key, 4)
        branches = jax.random.permutation(key_a, jnp.arange(4, dtype=jnp.int32)) + 1
        owners = jax.random.permutation(key_b, jnp.array([0, 0, 1, 1, 2, 2, 3, 3], dtype=jnp.int32)) + 1
        first_half = jnp.concatenate([jnp.zeros((8,), jnp.int32), branches[:2]])
        second_half = jnp.concatenate([branches[2:], jnp.arange(5, 13, dtype=jnp.int32)])
        nodes = jnp.concatenate([jax.random.permutation(key_c, first_half), jax.random.permutation(key_d, second_half)])
        leaf_parent = owners[jnp.clip(nodes - 5, 0, 7)]
        middle = jnp.where(nodes >= 5, leaf_parent, nodes)
        return jnp.stack([jnp.zeros_like(nodes), middle, nodes])
    paths = jax.vmap(one_tree)(tree_keys)
    offset = jnp.arange(tree_total, dtype=jnp.int32) % per_micro % TREES_GROUP * 13
    paths = paths + offset[:, None, None]
    paths = paths.reshape(MB, per_micro, 3, 20).transpose(0, 2, 1, 3).reshape(MB, 3, NBLOCKS)
    return paths.astype(jnp.int32)


def plant(entries, stream_key, smallest, top_value):
    shape = entries.shape
    place = [jax.random.randint(jax.random.fold_in(stream_key, axis), (), 0, shape[axis]) for axis in range(len(shape))]
    entries = entries.at[tuple(place)].set(smallest)
    longest = shape.index(max(shape))
    place[longest] = (place[longest] + 1) % shape[longest]
    return entries.at[tuple(place)].set(top_value)


def shard_levels(own_key, shape, pieces, smallest, largest):
    loudness, own = 1.0, jax.random.fold_in(own_key, 6)
    for dim, blocks in pieces:
        heights = jnp.exp(jax.random.uniform(jax.random.fold_in(own, dim), (blocks,), jnp.float32, smallest / len(pieces), largest / len(pieces)))
        loudness = loudness * jnp.repeat(heights, shape[dim] // blocks).reshape([-1 if axis == dim else 1 for axis in range(len(shape))])
    return loudness


def scatter_about(stream_key, shape, deviation, limit, pieces=(), kind=jnp.bfloat16):
    drawn = deviation * jax.random.normal(stream_key, shape, jnp.float32)
    if pieces:
        drawn = drawn * shard_levels(stream_key, shape, pieces, -0.22, 0.18)
    return jnp.clip(drawn, -limit, limit).astype(kind)


def setup_inputs(seed: int = 0) -> dict:
    keys = jax.random.split(jax.random.key(seed), 19)
    tokens = scatter_about(keys[0], (MB, TOKENS, D), 1.0, 6.0, ((1, 8),))
    cotangent = scatter_about(keys[1], (MB, TOKENS, D), 1.0, 6.0, ((1, 8),))
    block_path = draw_block_path(jax.random.fold_in(keys[18], 71), 0)
    labels = plant(jax.random.randint(keys[3], (MB, NBLOCKS), 0, CLASSES), jax.random.fold_in(keys[3], 1), 0, CLASSES - 1).astype(jnp.int32)
    w_attn_in = scatter_about(keys[4], (3, D, D), D ** -0.5, 0.21875, ((1, 4), (2, 4)))
    attn_bias = scatter_about(keys[5], (2, D), 0.5, 3.0, ((1, 4),))
    w_attn_out = scatter_about(keys[6], (D, D), (max(1, D // (4 * BLOCK))) ** -0.5, 6.0, ((0, 4), (1, 4)))
    w_up = scatter_about(keys[7], (D, FF), D ** -0.5, 0.21875, ((0, 4), (1, 4)))
    up_bias = scatter_about(keys[8], (FF,), 0.5, 3.0, ((0, 4),))
    w_down = scatter_about(keys[9], (FF, D), FF ** -0.5, 0.109375, ((0, 4), (1, 4)))
    norm_gain = jnp.clip(1.0 + 0.15 * jax.random.normal(keys[10], (2, D), jnp.float32), 0.25, 1.75).astype(jnp.bfloat16)
    layer_bias = scatter_about(keys[11], (4, D), 0.5, 3.0)
    stu_proj = scatter_about(keys[12], (D, STU), D ** -0.5, 0.21875, ((0, 4),))
    stu_bias = scatter_about(keys[13], (2, STU), 0.2, 1.1953125)
    pool_query = scatter_about(keys[14], (STU,), 1.0, 6.0)
    stu_dense = scatter_about(keys[15], (STU, STU), (STU // 16) ** -0.5, 2.0)
    stu_head = scatter_about(keys[16], (STU, CLASSES), (STU // 4) ** -0.5, 1.0)
    class_bias = scatter_about(keys[17], (CLASSES,), 0.5, 3.0)
    return {"tokens": tokens, "cotangent": cotangent, "block_path": block_path, "labels": labels, "w_attn_in": w_attn_in, "attn_bias": attn_bias, "w_attn_out": w_attn_out, "w_up": w_up, "up_bias": up_bias, "w_down": w_down, "norm_gain": norm_gain, "layer_bias": layer_bias, "stu_proj": stu_proj, "stu_bias": stu_bias, "pool_query": pool_query, "stu_dense": stu_dense, "stu_head": stu_head, "class_bias": class_bias}


@jax.custom_vjp
def low(v):
    return lax.optimization_barrier(v.astype(jnp.bfloat16)).astype(jnp.float32)

@jax.custom_vjp
def low_back(v):
    return v

def low_keep(v):
    return (low(v), None)

def low_pass(kept, grad):
    return (grad,)

def back_keep(v):
    return (v, None)

def back_low(kept, grad):
    return (low(grad),)
low.defvjp(low_keep, low_pass)
low_back.defvjp(back_keep, back_low)
NORM_EPSILON = 1e-05
MASK_VALUE = -1e+30

def to_float(array):
    return array.astype(jnp.float32)

def full_dot(left, right):
    return jnp.dot(left, right, precision=lax.Precision.HIGHEST, preferred_element_type=jnp.float32)

def layer_norm(resid, gain, shift):
    center = resid - lax.optimization_barrier(jnp.mean(resid, axis=-1, keepdims=True))
    inverse = lax.rsqrt(lax.optimization_barrier(jnp.mean(center * center, axis=-1, keepdims=True)) + NORM_EPSILON)
    return center * inverse * gain + shift

def tree_forward(params, tree_x, tree_path, tree_label):
    in_weight, qv_bias, out_weight, up_weight, up_shift, down_weight, norm_gains, shifts, proj_weight, stu_shift, pool_vec, dense_weight, head_weight, cls_shift = params
    tok_count = tree_x.shape[0]
    block_count = tree_path.shape[1]
    block_len = tok_count // block_count
    model_width = tree_x.shape[1]
    group_width = model_width // N_TP
    group_heads = group_width // HEAD_DIM
    head_scale = HEAD_DIM ** (-0.5)
    key_nodes = tree_path[2]
    block_vis = jnp.any(tree_path[:, :, None] == key_nodes[None, None, :], axis=0)
    token_vis = jnp.repeat(jnp.repeat(block_vis, block_len, axis=0), block_len, axis=1)
    attn_total = jnp.zeros((tok_count, model_width), jnp.float32)
    for head_group in range(N_TP):
        first_col = head_group * group_width
        last_col = first_col + group_width
        rows_in = low_back(tree_x)
        queries = low(low_back(full_dot(rows_in, in_weight[0][:, first_col:last_col]) + qv_bias[0][first_col:last_col]))
        key_rows = low(low_back(full_dot(rows_in, in_weight[1][:, first_col:last_col])))
        value_rows = low(low_back(full_dot(rows_in, in_weight[2][:, first_col:last_col]) + qv_bias[1][first_col:last_col]))
        query_heads = queries.reshape(tok_count, group_heads, HEAD_DIM)
        key_heads = key_rows.reshape(tok_count, group_heads, HEAD_DIM)
        value_heads = value_rows.reshape(tok_count, group_heads, HEAD_DIM)
        scores = low_back(head_scale * jnp.einsum('qhd,khd->hqk', query_heads, key_heads, precision=lax.Precision.HIGHEST))
        scores = jnp.where(token_vis[None], scores, MASK_VALUE)
        attn_probs = jax.nn.softmax(scores, axis=-1)
        attended = jnp.einsum('hqk,khd->qhd', low(attn_probs), value_heads, precision=lax.Precision.HIGHEST)
        attended = low(low_back(attended.reshape(tok_count, group_width)))
        attn_total = attn_total + low(full_dot(attended, out_weight[first_col:last_col, :]))
    hidden_one = layer_norm(tree_x + (low_back(attn_total) + shifts[0]), norm_gains[0], shifts[2])
    hidden_low = low(hidden_one)
    ff_width = up_weight.shape[1] // N_TP
    ffn_total = jnp.zeros((tok_count, model_width), jnp.float32)
    for ff_group in range(N_TP):
        first_col = ff_group * ff_width
        last_col = first_col + ff_width
        rows_up = low_back(hidden_low)
        pre_act = low_back(full_dot(rows_up, up_weight[:, first_col:last_col]) + up_shift[first_col:last_col])
        active = low(jax.nn.gelu(pre_act, approximate=False))
        ffn_total = ffn_total + low(full_dot(active, down_weight[first_col:last_col, :]))
    hidden_two = layer_norm(hidden_one + low_back(ffn_total) + shifts[1], norm_gains[1], shifts[3])
    student = low_back(full_dot(low(hidden_two), proj_weight) + stu_shift[0])
    pool_dim = student.shape[1] // POOL_HEADS
    student_heads = student.reshape(tok_count, POOL_HEADS, pool_dim)
    pool_score = lax.optimization_barrier(jnp.sum(student_heads * pool_vec.reshape(1, POOL_HEADS, pool_dim), axis=-1)) * pool_dim ** (-0.5)
    leaf_mask = tree_path[2] != tree_path[1]
    member = jnp.repeat(block_vis, block_len, axis=1)
    weight_logits = jnp.where(member[:, None, :], pool_score.T[None], MASK_VALUE)
    pool_weights = jax.nn.softmax(weight_logits, axis=-1)
    pooled = jnp.einsum('pht,thd->phd', pool_weights, student_heads, precision=lax.Precision.HIGHEST)
    pooled = pooled.reshape(block_count, POOL_HEADS * pool_dim)
    dense_out = jnp.tanh(full_dot(pooled, dense_weight) + stu_shift[1])
    logits = full_dot(dense_out, head_weight) + cls_shift
    picked = jnp.take_along_axis(logits, tree_label[:, None].astype(jnp.int32), axis=1)[:, 0]
    cross = jax.nn.logsumexp(logits, axis=1) - picked
    tree_loss = jnp.sum(jnp.where(leaf_mask, cross, 0.0))
    return (hidden_two, tree_loss)

def reference(tokens, cotangent, block_path, labels, w_attn_in, attn_bias, w_attn_out, w_up, up_bias, w_down, norm_gain, layer_bias, stu_proj, stu_bias, pool_query, stu_dense, stu_head, class_bias):
    params = tuple((to_float(array) for array in (w_attn_in, attn_bias, w_attn_out, w_up, up_bias, w_down, norm_gain, layer_bias, stu_proj, stu_bias, pool_query, stu_dense, stu_head, class_bias)))
    micro_count, total_tok, model_width = tokens.shape
    tree_blocks = 2 * BLK_DEV
    tree_tok = tree_blocks * BLOCK
    tree_count = total_tok // tree_tok
    tree_rows = to_float(tokens).reshape(micro_count * tree_count, tree_tok, model_width)
    tree_cot = to_float(cotangent).reshape(micro_count * tree_count, tree_tok, model_width)
    tree_paths = block_path.reshape(micro_count, 3, tree_count, tree_blocks).transpose(0, 2, 1, 3).reshape(micro_count * tree_count, 3, tree_blocks)
    tree_labels = labels.reshape(micro_count * tree_count, tree_blocks)

    def forward(weights, rows):

        def one_tree(loss_sum, scan_item):
            tree_x, tree_path, tree_label = scan_item
            hidden_two, tree_loss = tree_forward(weights, tree_x, tree_path, tree_label)
            return (loss_sum + tree_loss, hidden_two)
        loss_total, outputs = lax.scan(jax.checkpoint(one_tree), jnp.zeros((), jnp.float32), (rows, tree_paths, tree_labels))
        return (outputs, loss_total)
    (outputs, loss_total), pullback = jax.vjp(forward, params, tree_rows)
    grad_params, grad_rows = pullback((tree_cot, jnp.ones((), jnp.float32)))
    block_out = outputs.reshape(micro_count, total_tok, model_width).astype(jnp.bfloat16)
    tokens_grad = grad_rows.reshape(micro_count, total_tok, model_width)
    return (block_out, tokens_grad, grad_params[0], grad_params[1], grad_params[2], grad_params[3], grad_params[4], grad_params[5], grad_params[6], grad_params[7], grad_params[8], grad_params[9], grad_params[10], grad_params[11], grad_params[12], grad_params[13])
```

```python
import functools

import jax
import jax.numpy as jnp
from jax import lax
from jax.experimental import pallas as pl
from jax.experimental.pallas import tpu as pltpu
from jax.sharding import Mesh
from jax.sharding import PartitionSpec as P

HEAD_DIM = 64
POOL_HEADS = 2
TRUNK = 8
BLOCK = 128
PAIR = 2 * BLOCK

NORM_EPSILON = 1e-05
MASK_VALUE = -1e30

f32 = jnp.float32
bf16 = jnp.bfloat16


def swap(value, axis):
    return lax.ppermute(value, axis, [(0, 1), (1, 0)])


def diagonal(value):
    return lax.ppermute(value, ("side", "core"), [(0, 3), (3, 0), (1, 2), (2, 1)])


def ring(value):
    count = lax.axis_size("shard")
    return lax.ppermute(value, "shard", [(i, (i + 1) % count) for i in range(count)])


def dot_nn(left, right):
    return lax.dot_general(left, right, (((1,), (0,)), ((), ())), preferred_element_type=f32)


def dot_tn(left, right):
    return lax.dot_general(left, right, (((0,), (0,)), ((), ())), preferred_element_type=f32)


def dot_nt(left, right):
    return lax.dot_general(left, right, (((1,), (1,)), ((), ())), preferred_element_type=f32)


def exact(left, right, dims):
    return lax.dot_general(
        left, right, (dims, ((), ())), precision=lax.Precision.HIGHEST, preferred_element_type=f32
    )


def norm_forward(resid, gain, shift):
    center = resid - jnp.mean(resid, axis=-1, keepdims=True)
    inverse = lax.rsqrt(jnp.mean(center * center, axis=-1, keepdims=True) + NORM_EPSILON)
    normed = center * inverse
    return (normed * gain + shift, normed, inverse)


def norm_backward(grad_out, normed, inverse, gain):
    scaled = grad_out * gain
    grad_in = inverse * (
        scaled
        - jnp.mean(scaled, axis=-1, keepdims=True)
        - normed * jnp.mean(scaled * normed, axis=-1, keepdims=True)
    )
    return (grad_in, jnp.sum(grad_out * normed, axis=0), jnp.sum(grad_out, axis=0))


def block_rows(index):
    return pl.ds(pl.multiple_of(index * BLOCK, BLOCK), BLOCK)


def split_heads(qkv, qs, ks, vs, heads):
    width = heads * HEAD_DIM
    for head in range(heads):
        first = head * HEAD_DIM
        qs[head] = qkv[:, first : first + HEAD_DIM] * bf16(HEAD_DIM**-0.5)
        ks[head] = qkv[:, width + first : width + first + HEAD_DIM]
        vs[head] = qkv[:, 2 * width + first : 2 * width + first + HEAD_DIM]


def tile_scores(keys, trunk_keys, queries, rows, kind):
    parts = [dot_nt(trunk_keys, queries)]
    if kind:
        parts.append(dot_nt(keys[rows[0], :], queries[:BLOCK]))
        parts.append(dot_nt(keys[rows[1], :], queries[BLOCK:]))
        parts.append(dot_nt(keys[rows[2], :], queries))
    return parts


def tile_softmax(parts, masked):
    top = jnp.max(parts[0], axis=0, keepdims=True)
    if len(parts) > 1:
        own = jnp.concatenate(
            [jnp.max(parts[1], axis=0, keepdims=True), jnp.max(parts[2], axis=0, keepdims=True)],
            axis=1,
        )
        branch = parts[3] + masked
        parts = [parts[0], parts[1], parts[2], branch]
        top = jnp.maximum(top, jnp.maximum(own, jnp.max(branch, axis=0, keepdims=True)))
        tops = [top, top[:, :BLOCK], top[:, BLOCK:], top]
    else:
        tops = [top]
    exps = [jnp.exp(part - t) for part, t in zip(parts, tops)]
    total = jnp.sum(exps[0], axis=0, keepdims=True)
    if len(parts) > 1:
        own = jnp.concatenate(
            [jnp.sum(exps[1], axis=0, keepdims=True), jnp.sum(exps[2], axis=0, keepdims=True)],
            axis=1,
        )
        total = total + own + jnp.sum(exps[3], axis=0, keepdims=True)
    return exps, total


def attn_fwd_kernel(heads, blocks, tab, qkv, out, qs, ks, vs, kt, vtt):
    tiles = blocks // 2
    split_heads(qkv, qs, ks, vs, heads)
    for j in range(TRUNK):
        rows = block_rows(tab[2 * blocks + j])
        for head in range(heads):
            kt[head, j * BLOCK : (j + 1) * BLOCK, :] = ks[head, rows, :]
            vtt[head, :, j * BLOCK : (j + 1) * BLOCK] = vs[head, rows, :].T

    def run(tile, kind):
        rows = [
            block_rows(tab[2 * tile]),
            block_rows(tab[2 * tile + 1]),
            block_rows(tab[blocks + tile]),
        ]
        masked = jnp.where(tab[blocks + tiles + tile] == 2, 0.0, MASK_VALUE).astype(f32)
        for head in range(heads):
            queries = jnp.concatenate([qs[head, rows[0], :], qs[head, rows[1], :]], axis=0)
            parts = tile_scores(ks.at[head], kt[head], queries, rows, kind)
            exps, total = tile_softmax(parts, masked)
            exps = [part.astype(bf16) for part in exps]
            result = dot_nn(vtt[head], exps[0])
            if kind:
                result = result + jnp.concatenate(
                    [
                        dot_tn(vs[head, rows[0], :], exps[1]),
                        dot_tn(vs[head, rows[1], :], exps[2]),
                    ],
                    axis=1,
                )
                result = result + dot_tn(vs[head, rows[2], :], exps[3])
            result = (result / total).astype(bf16)
            lanes = slice(head * HEAD_DIM, (head + 1) * HEAD_DIM)
            out[lanes, rows[0]] = result[:, :BLOCK]
            out[lanes, rows[1]] = result[:, BLOCK:]

    def step(tile, carry):
        trunk_only = tab[blocks + tiles + tile] == 0

        @pl.when(trunk_only)
        def _():
            run(tile, 0)

        @pl.when(jnp.logical_not(trunk_only))
        def _():
            run(tile, 1)

        return carry

    lax.fori_loop(0, tiles, step, 0)


def attn_bwd_kernel(
    heads, blocks, tab, qkv, dot, out, qs, ks, vs, kt, vt, ktt, dkt, dvt, dka, dva, dqa
):
    tiles = blocks // 2
    split_heads(qkv, qs, ks, vs, heads)
    for j in range(TRUNK):
        rows = block_rows(tab[2 * blocks + j])
        for head in range(heads):
            span = slice(j * BLOCK, (j + 1) * BLOCK)
            kt[head, span, :] = ks[head, rows, :]
            vt[head, span, :] = vs[head, rows, :]
            ktt[head, :, span] = ks[head, rows, :].T
    dkt[...] = jnp.zeros_like(dkt)
    dvt[...] = jnp.zeros_like(dvt)
    dka[...] = jnp.zeros_like(dka)
    dva[...] = jnp.zeros_like(dva)

    def run(tile, kind):
        rows = [
            block_rows(tab[2 * tile]),
            block_rows(tab[2 * tile + 1]),
            block_rows(tab[blocks + tile]),
        ]
        masked = jnp.where(tab[blocks + tiles + tile] == 2, 0.0, MASK_VALUE).astype(f32)
        for head in range(heads):
            lanes = slice(head * HEAD_DIM, (head + 1) * HEAD_DIM)
            queries = jnp.concatenate([qs[head, rows[0], :], qs[head, rows[1], :]], axis=0)
            grads = jnp.concatenate([dot[lanes, rows[0]], dot[lanes, rows[1]]], axis=1)
            parts = tile_scores(ks.at[head], kt[head], queries, rows, kind)
            exps, total = tile_softmax(parts, masked)
            inverse = 1.0 / total
            inverses = [inverse, inverse[:, :BLOCK], inverse[:, BLOCK:], inverse]
            probs = [part * inv for part, inv in zip(exps, inverses)]
            grad_parts = [dot_nn(vt[head], grads)]
            if kind:
                grad_parts.append(dot_nn(vs[head, rows[0], :], grads[:, :BLOCK]))
                grad_parts.append(dot_nn(vs[head, rows[1], :], grads[:, BLOCK:]))
                grad_parts.append(dot_nn(vs[head, rows[2], :], grads))
            inner = [jnp.sum(p * g, axis=0, keepdims=True) for p, g in zip(probs, grad_parts)]
            delta = inner[0]
            if kind:
                delta = delta + jnp.concatenate([inner[1], inner[2]], axis=1) + inner[3]
            deltas = [delta, delta[:, :BLOCK], delta[:, BLOCK:], delta]
            score_grads = [
                (p * (g - d)).astype(bf16) for p, g, d in zip(probs, grad_parts, deltas)
            ]
            probs = [p.astype(bf16) for p in probs]
            dvt[head] += dot_nt(probs[0], grads)
            dkt[head] += dot_nn(score_grads[0], queries)
            query_grad = dot_nn(ktt[head], score_grads[0])
            if kind:
                dva[head, rows[0], :] += dot_nt(probs[1], grads[:, :BLOCK])
                dva[head, rows[1], :] += dot_nt(probs[2], grads[:, BLOCK:])
                dva[head, rows[2], :] += dot_nt(probs[3], grads)
                dka[head, rows[0], :] += dot_nn(score_grads[1], queries[:BLOCK])
                dka[head, rows[1], :] += dot_nn(score_grads[2], queries[BLOCK:])
                dka[head, rows[2], :] += dot_nn(score_grads[3], queries)
                query_grad = query_grad + jnp.concatenate(
                    [
                        dot_tn(ks[head, rows[0], :], score_grads[1]),
                        dot_tn(ks[head, rows[1], :], score_grads[2]),
                    ],
                    axis=1,
                )
                query_grad = query_grad + dot_tn(ks[head, rows[2], :], score_grads[3])
            query_grad = (query_grad * HEAD_DIM**-0.5).T
            dqa[head, rows[0], :] = query_grad[:BLOCK]
            dqa[head, rows[1], :] = query_grad[BLOCK:]

    def step(tile, carry):
        trunk_only = tab[blocks + tiles + tile] == 0

        @pl.when(trunk_only)
        def _():
            run(tile, 0)

        @pl.when(jnp.logical_not(trunk_only))
        def _():
            run(tile, 1)

        return carry

    lax.fori_loop(0, tiles, step, 0)
    for j in range(TRUNK):
        rows = block_rows(tab[2 * blocks + j])
        for head in range(heads):
            span = slice(j * BLOCK, (j + 1) * BLOCK)
            dka[head, rows, :] = dkt[head, span, :]
            dva[head, rows, :] = dvt[head, span, :]
    width = heads * HEAD_DIM
    for head in range(heads):
        first = head * HEAD_DIM
        out[:, first : first + HEAD_DIM] = dqa[head].astype(bf16)
        out[:, width + first : width + first + HEAD_DIM] = dka[head].astype(bf16)
        out[:, 2 * width + first : 2 * width + first + HEAD_DIM] = dva[head].astype(bf16)


def attn_forward(table, qkv, heads, blocks):
    rows = qkv.shape[0]
    trunk = TRUNK * BLOCK
    return pl.pallas_call(
        functools.partial(attn_fwd_kernel, heads, blocks),
        out_shape=jax.ShapeDtypeStruct((heads * HEAD_DIM, rows), bf16),
        in_specs=[
            pl.BlockSpec(memory_space=pltpu.SMEM),
            pl.BlockSpec(memory_space=pltpu.VMEM),
        ],
        out_specs=pl.BlockSpec(memory_space=pltpu.VMEM),
        scratch_shapes=[pltpu.VMEM((heads, rows, HEAD_DIM), bf16)] * 3
        + [pltpu.VMEM((heads, trunk, HEAD_DIM), bf16), pltpu.VMEM((heads, HEAD_DIM, trunk), bf16)],
        compiler_params=pltpu.CompilerParams(vmem_limit_bytes=48 << 20),
        cost_estimate=pl.CostEstimate(
            flops=16 * rows * (trunk + PAIR) * HEAD_DIM * heads,
            bytes_accessed=8 * rows * heads * HEAD_DIM,
            transcendentals=rows * (trunk + PAIR) * heads,
        ),
        name="tree_attention",
    )(table, qkv)


def attn_backward(table, qkv, out_grad, heads, blocks):
    rows = qkv.shape[0]
    trunk = TRUNK * BLOCK
    return pl.pallas_call(
        functools.partial(attn_bwd_kernel, heads, blocks),
        out_shape=jax.ShapeDtypeStruct(qkv.shape, bf16),
        in_specs=[
            pl.BlockSpec(memory_space=pltpu.SMEM),
            pl.BlockSpec(memory_space=pltpu.VMEM),
            pl.BlockSpec(memory_space=pltpu.VMEM),
        ],
        out_specs=pl.BlockSpec(memory_space=pltpu.VMEM),
        scratch_shapes=[pltpu.VMEM((heads, rows, HEAD_DIM), bf16)] * 3
        + [pltpu.VMEM((heads, trunk, HEAD_DIM), bf16)] * 2
        + [pltpu.VMEM((heads, HEAD_DIM, trunk), bf16)]
        + [pltpu.VMEM((heads, trunk, HEAD_DIM), f32)] * 2
        + [pltpu.VMEM((heads, rows, HEAD_DIM), f32)] * 3,
        compiler_params=pltpu.CompilerParams(vmem_limit_bytes=56 << 20),
        cost_estimate=pl.CostEstimate(
            flops=40 * rows * (trunk + PAIR) * HEAD_DIM * heads,
            bytes_accessed=14 * rows * heads * HEAD_DIM,
            transcendentals=rows * (trunk + PAIR) * heads,
        ),
        name="tree_attention_grad",
    )(table, qkv, out_grad)


def attention_table(path, half_blocks):
    blocks = path.shape[1]
    place = jnp.arange(blocks, dtype=jnp.int32)
    kind = (path[1] != path[0]).astype(jnp.int32) + (path[2] != path[1]).astype(jnp.int32)
    key = kind * 65536 + jnp.where(kind == 2, path[1] * 32, 0) + place
    group = place // half_blocks
    before = (group[:, None] == group[None, :]) & (key[None, :] < key[:, None])
    rank = jnp.sum(before.astype(jnp.int32), axis=1) + group * half_blocks
    branch = jnp.sum(
        jnp.where((kind[None, :] == 1) & (path[2][None, :] == path[1][:, None]), place[None, :], 0),
        axis=1,
    )
    slot = (rank[None, :] == place[:, None]).astype(jnp.int32)
    order = jnp.sum(slot * place[None, :], axis=1)
    first = slot[::2]
    tile_branch = jnp.sum(first * jnp.where(kind == 2, branch, 0)[None, :], axis=1)
    tile_kind = jnp.sum(first * kind[None, :], axis=1)
    return order, tile_branch, tile_kind


def pool_kernel(
    stats,
    member,
    leaf,
    onehot,
    dense,
    head,
    dense_shift,
    cls_shift,
    spread_out,
    offset_out,
    grad_dense,
    grad_head,
    vectors,
):
    width = dense.shape[0]
    pool_dim = width // POOL_HEADS
    moment = stats[:, :width]
    seen = member[...] > 0.0
    is_leaf = leaf[...] > 0.0
    coeffs = []
    pooled = []
    for e in range(POOL_HEADS):
        peak = stats[:, width + e : width + e + 1]
        mass = stats[:, width + POOL_HEADS + e : width + POOL_HEADS + e + 1]
        top = jnp.max(jnp.where(seen, peak, MASK_VALUE), axis=0, keepdims=True)
        factor = jnp.where(seen, jnp.exp(jnp.where(seen, peak - top, MASK_VALUE)), 0.0)
        total = jnp.sum(factor * mass, axis=0, keepdims=True)
        total = jnp.where(total > 0.0, total, 1.0)
        coeff = factor / total
        coeffs.append(coeff)
        lanes = slice(e * pool_dim, (e + 1) * pool_dim)
        pooled.append(exact(coeff, moment[:, lanes], ((0,), (0,))))
    pooled = jnp.concatenate(pooled, axis=1)
    dense_out = jnp.tanh(exact(pooled, dense[...], ((1,), (0,))) + dense_shift[...])
    logits = exact(dense_out, head[...], ((1,), (0,))) + cls_shift[...]
    logits = logits - jnp.max(logits, axis=1, keepdims=True)
    chances = jnp.exp(logits)
    chances = chances / jnp.sum(chances, axis=1, keepdims=True)
    grad_logits = jnp.where(is_leaf, chances - onehot[...], 0.0)
    grad_head[...] = exact(dense_out, grad_logits, ((0,), (0,)))
    grad_pre = exact(grad_logits, head[...], ((1,), (1,))) * (1.0 - dense_out * dense_out)
    grad_dense[...] = exact(pooled, grad_pre, ((0,), (0,)))
    vectors[0:1, :] = jnp.sum(grad_pre, axis=0, keepdims=True)
    vectors[1:2, :] = jnp.sum(grad_logits, axis=0, keepdims=True)
    vectors[2:8, :] = jnp.zeros((6, width), f32)
    grad_pooled = exact(grad_pre, dense[...], ((1,), (1,)))
    product = grad_pooled * pooled
    for e in range(POOL_HEADS):
        lanes = slice(e * pool_dim, (e + 1) * pool_dim)
        spread_out[:, lanes] = exact(coeffs[e], grad_pooled[:, lanes], ((1,), (0,)))
        inner = jnp.sum(product[:, lanes], axis=1, keepdims=True)
        inner = jnp.broadcast_to(inner, (inner.shape[0], pool_dim))
        offset_out[:, lanes] = exact(coeffs[e], inner, ((1,), (0,)))


def pool_classifier(stats, member, leaf, onehot, dense, head, dense_shift, cls_shift):
    rows = stats.shape[0]
    width = dense.shape[0]
    return pl.pallas_call(
        pool_kernel,
        out_shape=(
            jax.ShapeDtypeStruct((rows, width), f32),
            jax.ShapeDtypeStruct((rows, width), f32),
            jax.ShapeDtypeStruct((width, width), f32),
            jax.ShapeDtypeStruct((width, width), f32),
            jax.ShapeDtypeStruct((8, width), f32),
        ),
        cost_estimate=pl.CostEstimate(
            flops=40 * rows * width * width, bytes_accessed=16 * width * width, transcendentals=0
        ),
        name="pool_classifier",
    )(stats, member, leaf, onehot, dense, head, dense_shift, cls_shift)


def body(
    tokens,
    cotangent,
    block_path,
    labels,
    w_attn_in,
    attn_bias,
    w_attn_out,
    w_up,
    up_bias,
    w_down,
    norm_gain,
    layer_bias,
    stu_proj,
    stu_bias,
    pool_query,
    stu_dense,
    stu_head,
    class_bias,
):
    row_count, model = tokens.shape[1:]
    own_blocks = labels.shape[1]
    tree_blocks = 2 * own_blocks
    group_width = w_attn_in.shape[2]
    heads = group_width // HEAD_DIM
    slab = w_up.shape[0]
    hidden = w_up.shape[1]
    shards = lax.axis_size("shard")
    trees = lax.axis_size("tree")
    stu_width = stu_proj.shape[1]
    pool_dim = stu_width // POOL_HEADS
    pool_scale = pool_dim ** (-0.5)
    class_count = class_bias.shape[0]
    part_rows = row_count // 2
    part_blocks = own_blocks // 2

    shard = lax.axis_index("shard")
    tree = lax.axis_index("tree")
    side = lax.axis_index("side")
    half = lax.axis_index("half")
    core = lax.axis_index("core")

    shift_rows = layer_bias.astype(f32)
    gain_rows = norm_gain.astype(f32)
    stu_shifts = stu_bias.astype(f32)
    pool_vec = pool_query.astype(f32)

    inputs = lax.dynamic_index_in_dim(tokens, half, 0, keepdims=False)
    own_part = lax.dynamic_slice_in_dim(inputs, core * part_rows, part_rows, 0)
    other_part = swap(own_part, "side")
    other_twin = swap(other_part, "core")
    other_low = jnp.where(core == 0, other_part, other_twin)
    other_high = jnp.where(core == 0, other_twin, other_part)
    tree_rows = jnp.concatenate([inputs, other_low, other_high], axis=0)

    qkv_shard = w_attn_in.transpose(1, 0, 2).reshape(slab, 3 * group_width)
    bias_row = jnp.concatenate(
        [attn_bias[0], jnp.zeros((group_width,), bf16), attn_bias[1]]
    ).reshape(1, 3 * group_width)
    qkv_message = jnp.concatenate(
        [qkv_shard, jnp.broadcast_to(bias_row, (16, 3 * group_width))], axis=0
    )
    qkv_message = jnp.where(side == half, qkv_message, swap(qkv_message, "half"))
    qkv_bias = qkv_message[slab].astype(f32)
    piece = qkv_message[:slab]
    qkv_weight = jnp.zeros((shards, slab, 3 * group_width), bf16)
    for k in range(shards):
        if k:
            piece = ring(piece)
        qkv_weight = lax.dynamic_update_index_in_dim(qkv_weight, piece, (shard - k) % shards, 0)
    qkv_weight = qkv_weight.reshape(model, 3 * group_width)

    out_rows = slab * group_width // model
    stu_rows = slab * stu_width // model
    message = jnp.concatenate(
        [
            w_up,
            w_down.T,
            w_attn_out.reshape(out_rows, model),
            stu_proj.reshape(stu_rows, model),
            jnp.broadcast_to(up_bias[None, :], (16, model)),
        ],
        axis=0,
    )
    first_out = 2 * slab
    first_stu = first_out + out_rows
    first_bias = first_stu + stu_rows
    up_weight = jnp.zeros((shards, slab, 2 * hidden), bf16)
    down_weight = jnp.zeros((shards, slab, 2 * hidden), bf16)
    out_pieces = jnp.zeros((2, shards, out_rows, model), bf16)
    stu_pieces = jnp.zeros((shards, stu_rows, model), bf16)
    piece = message
    biases = []
    for k in range(shards):
        if k:
            piece = ring(piece)
        place = (shard - k) % shards
        for j in range(2):
            got = swap(piece, "half") if j else piece
            if k == 0:
                biases.append(got[first_bias].astype(f32))
            up_weight = lax.dynamic_update_slice(
                up_weight, got[None, :slab], (place, 0, j * hidden)
            )
            down_weight = lax.dynamic_update_slice(
                down_weight, got[None, slab : 2 * slab], (place, 0, j * hidden)
            )
            out_pieces = lax.dynamic_update_slice(
                out_pieces,
                got[None, None, first_out:first_stu],
                (jnp.where(j == 0, half, 1 - half), place, 0, 0),
            )
            if j == 0:
                stu_pieces = lax.dynamic_update_slice(
                    stu_pieces, got[None, first_stu:first_bias], (place, 0, 0)
                )
    hidden_shift = jnp.concatenate(biases)
    up_weight = up_weight.reshape(model, 2 * hidden)
    down_weight = down_weight.reshape(model, 2 * hidden)
    stu_weight = stu_pieces.reshape(model, stu_width)
    out_twin = swap(out_pieces, "core")
    out_low = jnp.where(core == 0, out_pieces, out_twin)
    out_high = jnp.where(core == 0, out_twin, out_pieces)
    out_weight = (
        jnp.stack([out_low, out_high], axis=1)
        .reshape(2, 2, shards, group_width, slab)
        .transpose(0, 1, 3, 2, 4)
        .reshape(4 * group_width, model)
    )

    paths = lax.dynamic_index_in_dim(block_path, half, 0, keepdims=False)
    paths = lax.dynamic_slice_in_dim(paths, tree * tree_blocks, tree_blocks, 1)
    own_first = jnp.where(
        side == 0,
        paths,
        jnp.concatenate([paths[:, own_blocks:], paths[:, :own_blocks]], axis=1),
    )
    order, tile_branch, tile_kind = attention_table(own_first, own_blocks)
    trunk_list = jnp.where(
        side == 0, order[:TRUNK], order[own_blocks : own_blocks + TRUNK]
    )
    table = jnp.concatenate([order, tile_branch, tile_kind, trunk_list])

    qkv = (dot_nn(tree_rows, qkv_weight) + qkv_bias).astype(bf16)
    attended = attn_forward(table, qkv, heads, tree_blocks)

    def spread_heads(array):
        own_side = array[:, :row_count].reshape(group_width, 2, part_rows)
        far_side = array[:, row_count:].reshape(group_width, 2, part_rows)
        kept = lax.dynamic_index_in_dim(own_side, core, 1, keepdims=False)
        near = swap(lax.dynamic_index_in_dim(own_side, 1 - core, 1, keepdims=False), "core")
        across = swap(lax.dynamic_index_in_dim(far_side, core, 1, keepdims=False), "side")
        corner = diagonal(lax.dynamic_index_in_dim(far_side, 1 - core, 1, keepdims=False))
        result = jnp.zeros((4, group_width, part_rows), array.dtype)
        for piece, place in (
            (kept, 2 * side + core),
            (near, 2 * side + 1 - core),
            (across, 2 * (1 - side) + core),
            (corner, 2 * (1 - side) + 1 - core),
        ):
            result = lax.dynamic_update_index_in_dim(result, piece, place, 0)
        return result.reshape(4 * group_width, part_rows)

    def collect_heads(array):
        groups = array.reshape(4, group_width, part_rows)

        def group(place):
            return lax.dynamic_index_in_dim(groups, place, 0, keepdims=False)

        kept = group(2 * side + core)
        near = swap(group(2 * side + 1 - core), "core")
        across = swap(group(2 * (1 - side) + core), "side")
        corner = diagonal(group(2 * (1 - side) + 1 - core))
        result = jnp.zeros((group_width, 4, part_rows), array.dtype)
        for piece, place in (
            (kept, core),
            (near, 1 - core),
            (across, 2 + core),
            (corner, 3 - core),
        ):
            result = lax.dynamic_update_index_in_dim(result, piece, place, 1)
        return result.reshape(group_width, 4 * part_rows)

    heads_own = spread_heads(attended)
    attn = dot_tn(heads_own, out_weight)
    resid_one = own_part.astype(f32) + (attn + shift_rows[0])
    hidden_one, normed_one, inverse_one = norm_forward(resid_one, gain_rows[0], shift_rows[2])
    hidden_low = hidden_one.astype(bf16)

    hidden_both = jnp.concatenate([hidden_low, swap(hidden_low, "core")], axis=0)
    pre_act = dot_nn(hidden_both, up_weight) + hidden_shift
    normal_cdf = 0.5 * (1.0 + lax.erf(pre_act * 0.7071067811865476))
    active = (pre_act * normal_cdf).astype(bf16)
    slope = normal_cdf + pre_act * jnp.exp(-0.5 * pre_act * pre_act) * 0.3989422804014327
    ffn_far = swap(dot_nt(active[part_rows:], down_weight).astype(bf16), "core")
    ffn = dot_nt(active[:part_rows], down_weight) + ffn_far.astype(f32)
    hidden_two, normed_two, inverse_two = norm_forward(
        hidden_one + ffn + shift_rows[1], gain_rows[1], shift_rows[3]
    )
    block_low = hidden_two.astype(bf16)

    student = dot_nn(block_low, stu_weight) + stu_shifts[0]
    head_of = (jnp.arange(stu_width) // pool_dim)[:, None] == jnp.arange(POOL_HEADS)[None, :]
    scaled_query = jnp.where(head_of, pool_vec[:, None] * pool_scale, 0.0)
    pool_score = exact(student, scaled_query, ((1,), (0,)))
    score_blocks = pool_score.reshape(part_blocks, BLOCK, POOL_HEADS)
    block_peak = jnp.max(score_blocks, axis=1)
    weight_exp = jnp.exp(score_blocks - block_peak[:, None, :])
    block_mass = jnp.sum(weight_exp, axis=1)
    weight_lanes = jnp.repeat(weight_exp, pool_dim, axis=2)
    student_blocks = student.reshape(part_blocks, BLOCK, stu_width)
    moment = jnp.sum(weight_lanes * student_blocks, axis=1)
    own_labels = lax.dynamic_index_in_dim(labels, half, 0, keepdims=False)
    own_labels = lax.dynamic_slice_in_dim(own_labels, core * part_blocks, part_blocks, 0)
    stats = jnp.concatenate(
        [
            moment,
            block_peak,
            block_mass,
            own_labels.astype(f32)[:, None],
            jnp.zeros((part_blocks, stu_width - 2 * POOL_HEADS - 1), f32),
        ],
        axis=1,
    )
    stats = jnp.pad(stats, ((0, 8 - part_blocks), (0, 0)))
    twin_stats = swap(stats, "core")
    pair_stats = jnp.stack(
        [jnp.where(core == 0, stats, twin_stats), jnp.where(core == 0, twin_stats, stats)]
    )
    far_stats = swap(pair_stats, "side")
    tree_stats = jnp.stack(
        [jnp.where(side == 0, pair_stats, far_stats), jnp.where(side == 0, far_stats, pair_stats)]
    ).reshape(32, 2 * stu_width)

    def spaced(array):
        array = array.reshape((4, part_blocks) + array.shape[1:])
        pads = ((0, 0), (0, 8 - part_blocks)) + ((0, 0),) * (array.ndim - 2)
        return jnp.pad(array, pads).reshape((32,) + array.shape[2:])

    is_leaf = (paths[1] != paths[2]).astype(f32)
    member = jnp.any(paths[2][:, None, None] == paths.T[None, :, :], axis=2).astype(f32)
    member = member * is_leaf[None, :]
    member = spaced(spaced(member).T).T
    leaf_column = spaced(is_leaf)[:, None]
    onehot = (
        tree_stats[:, stu_width + 2 * POOL_HEADS : stu_width + 2 * POOL_HEADS + 1]
        == jnp.arange(stu_width, dtype=f32)[None, :]
    ).astype(f32)
    lane_pad = stu_width - class_count
    head_padded = jnp.pad(stu_head.astype(f32), ((0, 0), (0, lane_pad)))
    cls_padded = jnp.pad(class_bias.astype(f32), (0, lane_pad), constant_values=MASK_VALUE)
    spread, offset, grad_dense, grad_head, pool_vectors = pool_classifier(
        tree_stats,
        member,
        leaf_column,
        onehot,
        stu_dense.astype(f32),
        head_padded,
        stu_shifts[1][None, :],
        cls_padded[None, :],
    )
    first_block = (2 * side + core) * 8
    own_spread = lax.dynamic_slice_in_dim(spread, first_block, part_blocks, 0)
    own_offset = lax.dynamic_slice_in_dim(offset, first_block, part_blocks, 0)
    head_join = (
        (jnp.arange(stu_width) // pool_dim)[:, None] == (jnp.arange(stu_width) // pool_dim)[None, :]
    ).astype(f32)
    inner = exact(
        (student_blocks * own_spread[:, None, :]).reshape(part_rows, stu_width),
        head_join,
        ((1,), (0,)),
    ).reshape(part_blocks, BLOCK, stu_width)
    grad_score = weight_lanes * (inner - own_offset[:, None, :])
    grad_student = weight_lanes * own_spread[:, None, :] + grad_score * (pool_vec * pool_scale)
    grad_pool = jnp.sum(grad_score * student_blocks, axis=(0, 1)) * pool_scale
    student_low = grad_student.reshape(part_rows, stu_width).astype(bf16)
    grad_proj = dot_tn(block_low, student_low)
    grad_proj_shift = jnp.sum(student_low.astype(f32), axis=0)

    upstream = lax.dynamic_slice(
        cotangent, (half, core * part_rows, 0), (1, part_rows, model)
    )[0].astype(f32)
    grad_two = upstream + dot_nt(student_low, stu_weight)
    resid_grad_two, gain_grad_two, shift_grad_two = norm_backward(
        grad_two, normed_two, inverse_two, gain_rows[1]
    )
    down_shift_grad = jnp.sum(resid_grad_two, axis=0)
    ffn_low = resid_grad_two.astype(bf16)
    ffn_both = jnp.concatenate([ffn_low, swap(ffn_low, "core")], axis=0)
    pre_low = (dot_nn(ffn_both, down_weight) * slope).astype(bf16)
    grad_hidden_shift = jnp.sum(pre_low.astype(f32), axis=0)
    far_one = swap(dot_nt(pre_low[part_rows:], up_weight).astype(bf16), "core")
    grad_one = resid_grad_two + dot_nt(pre_low[:part_rows], up_weight) + far_one.astype(f32)
    grad_down = dot_tn(ffn_both, active).astype(bf16)
    grad_up = dot_tn(hidden_both, pre_low).astype(bf16)

    resid_grad_one, gain_grad_one, shift_grad_one = norm_backward(
        grad_one, normed_one, inverse_one, gain_rows[0]
    )
    out_shift_grad = jnp.sum(resid_grad_one, axis=0)
    attn_low = resid_grad_one.astype(bf16)
    heads_grad = dot_nt(out_weight, attn_low).astype(bf16)
    grad_out = dot_nn(heads_own, attn_low).astype(bf16)
    attended_grad = collect_heads(heads_grad)
    qkv_grad = attn_backward(table, qkv, attended_grad, heads, tree_blocks)

    input_grad = dot_nt(qkv_grad, qkv_weight).astype(bf16).reshape(2, 2, part_rows, model)
    kept_grad = lax.dynamic_index_in_dim(input_grad, core, 1, keepdims=False)
    sent_grad = lax.dynamic_index_in_dim(input_grad, 1 - core, 1, keepdims=False)
    pair_grad = kept_grad.astype(f32) + swap(sent_grad, "core").astype(f32)
    far_grad = swap(pair_grad[1].astype(bf16), "side")
    rows_grad = (resid_grad_one + pair_grad[0] + far_grad.astype(f32)).astype(bf16)

    def everywhere(rows, dtype):
        other = swap(rows, "half")
        twins = swap(jnp.stack([rows, other]), "core")
        result = jnp.zeros((2, 2, part_rows, model), dtype)
        for piece, row, column in (
            (rows, half, core),
            (other, 1 - half, core),
            (twins[0], half, 1 - core),
            (twins[1], 1 - half, 1 - core),
        ):
            result = lax.dynamic_update_slice(
                result, piece.astype(dtype)[None, None], (row, column, 0, 0)
            )
        return result.reshape(2, row_count, model)

    block_out = everywhere(block_low, bf16)
    tokens_grad = everywhere(rows_grad, f32)

    out_groups = grad_out.reshape(2, 2, group_width, model)
    kept_out = lax.dynamic_index_in_dim(out_groups, core, 1, keepdims=False)
    sent_out = lax.dynamic_index_in_dim(out_groups, 1 - core, 1, keepdims=False)
    proj_low = grad_proj.astype(bf16)
    out_sum = (kept_out.astype(f32) + swap(sent_out, "core").astype(f32)).astype(bf16)
    proj_sum = (proj_low.astype(f32) + swap(proj_low, "core").astype(f32)).astype(bf16)
    out_parts = (
        out_sum.reshape(2, group_width, shards, slab)
        .transpose(0, 2, 1, 3)
        .reshape(2, shards, out_rows, model)
    )
    proj_parts = proj_sum.reshape(shards, stu_rows, model)

    def grad_piece(j, place):
        row = place * slab
        return jnp.concatenate(
            [
                lax.dynamic_slice(grad_up, (row, j * hidden), (slab, hidden)),
                lax.dynamic_slice(grad_down, (row, j * hidden), (slab, hidden)),
                lax.dynamic_slice(
                    out_parts,
                    (jnp.where(j == 0, half, 1 - half), place, 0, 0),
                    (1, 1, out_rows, model),
                )[0, 0],
                lax.dynamic_index_in_dim(proj_parts, place, 0, keepdims=False),
            ],
            axis=0,
        )

    passed = None
    for k in range(1, shards + 1):
        place = (shard - k) % shards
        total = grad_piece(0, place).astype(f32) + swap(grad_piece(1, place), "half").astype(f32)
        if passed is not None:
            total = total + passed.astype(f32)
        if k < shards:
            passed = ring(total.astype(bf16))
    total = total.astype(bf16)
    total = total.astype(f32) + swap(total, "side").astype(f32)
    if trees > 1:
        total = lax.psum(total, "tree")

    grad_in = dot_tn(tree_rows, qkv_grad).astype(bf16).reshape(shards, 2, slab // 2, 3 * group_width)
    kept_in = lax.dynamic_index_in_dim(grad_in, half, 1, keepdims=False)
    sent_in = lax.dynamic_index_in_dim(grad_in, 1 - half, 1, keepdims=False)
    chip_in = kept_in.astype(f32) + swap(sent_in, "half").astype(f32)
    passed = None
    for k in range(1, shards + 1):
        place = (shard - k) % shards
        part = lax.dynamic_index_in_dim(chip_in, place, 0, keepdims=False)
        if passed is not None:
            part = part + passed.astype(f32)
        if k < shards:
            passed = ring(part.astype(bf16))
    if trees > 1:
        part = lax.psum(part, "tree")
    part = part.astype(bf16)
    part_twin = swap(part, "half")
    group_in = jnp.concatenate(
        [jnp.where(half == 0, part, part_twin), jnp.where(half == 0, part_twin, part)], axis=0
    )
    group_in = jnp.where(side == half, group_in, swap(group_in, "side"))
    grad_in_own = group_in.astype(f32).reshape(slab, 3, group_width).transpose(1, 0, 2)

    bias_sums = jnp.sum(qkv_grad.astype(f32), axis=0)
    bias_grad = jnp.stack([bias_sums[:group_width], bias_sums[2 * group_width :]])
    bias_grad = lax.dynamic_update_slice(
        jnp.zeros((2, model), f32), bias_grad, (0, (2 * side + core) * group_width)
    )
    up_grad = jnp.zeros((4, hidden), f32)
    for j in range(2):
        up_grad = lax.dynamic_update_slice(
            up_grad,
            grad_hidden_shift[None, j * hidden : (j + 1) * hidden],
            (2 * jnp.where(j == 0, half, 1 - half) + core, 0),
        )
    first = jnp.where((side == 0) & (core == 0), 1.0, 0.0)
    pieces = [
        gain_grad_one,
        gain_grad_two,
        out_shift_grad,
        down_shift_grad,
        shift_grad_one,
        shift_grad_two,
        up_grad.reshape(-1),
        bias_grad.reshape(-1),
        grad_proj_shift,
        pool_vectors[0] * first,
        grad_pool,
        pool_vectors[1] * first,
        (grad_dense * first).reshape(-1),
        (grad_head * first).reshape(-1),
    ]
    sizes = [piece.size for piece in pieces]
    small = jnp.concatenate(pieces)
    small = jnp.pad(small, (0, -small.size % (8 * model))).reshape(-1, model)
    for axis in ("core", "half", "side"):
        small = small + swap(small, axis)
    step = 1
    while step < shards:
        small = small + lax.ppermute(small, "shard", [(i, i ^ step) for i in range(shards)])
        step *= 2
    if trees > 1:
        small = lax.psum(small, "tree")
    small = small.reshape(-1)
    starts = [sum(sizes[:i]) for i in range(len(sizes) + 1)]

    def taken(low, high):
        return small[starts[low] : starts[high]]

    position = 2 * half + core
    return (
        block_out,
        tokens_grad,
        grad_in_own,
        lax.dynamic_slice_in_dim(taken(7, 8).reshape(2, model), position * group_width, group_width, 1),
        total[first_out:first_stu].reshape(group_width, slab),
        total[:slab],
        lax.dynamic_slice_in_dim(taken(6, 7), position * hidden, hidden, 0),
        total[slab : 2 * slab].T,
        taken(0, 2).reshape(2, model),
        taken(2, 6).reshape(4, model),
        total[first_stu:first_bias].reshape(slab, stu_width),
        taken(8, 10).reshape(2, stu_width),
        taken(10, 11),
        taken(12, 13).reshape(stu_width, stu_width),
        taken(13, 14).reshape(stu_width, stu_width)[:, :class_count],
        taken(11, 12)[:class_count],
    )


def solution(mesh):
    shape = dict(mesh.shape)
    split = Mesh(
        mesh.devices.reshape(shape["shard"], shape["ctx"] // 2, 2, 2, shape["tp"] // 2),
        ("shard", "tree", "side", "half", "core"),
    )
    ctx = ("tree", "side")
    tp = ("half", "core")
    rows = ("shard",) + ctx
    in_specs = (
        P(None, rows, None),
        P(None, rows, None),
        P(None, None, "shard"),
        P(None, rows),
        P(None, "shard", tp),
        P(None, tp),
        P(tp, "shard"),
        P("shard", tp),
        P(tp),
        P(tp, "shard"),
        P(),
        P(),
        P("shard", None),
        P(),
        P(),
        P(),
        P(),
        P(),
    )
    out_specs = (
        P(None, rows, None),
        P(None, rows, None),
        P(None, "shard", tp),
        P(None, tp),
        P(tp, "shard"),
        P("shard", tp),
        P(tp),
        P(tp, "shard"),
        P(),
        P(),
        P("shard", None),
        P(),
        P(),
        P(),
        P(),
        P(),
    )
    return jax.shard_map(body, mesh=split, in_specs=in_specs, out_specs=out_specs, check_vma=False)
```

```python
import functools

import jax
import jax.numpy as jnp
from jax import lax
from jax.experimental import pallas as pl
from jax.experimental.pallas import tpu as pltpu
from jax.sharding import Mesh
from jax.sharding import PartitionSpec as P

HEAD_DIM = 64
POOL_HEADS = 2
TRUNK = 8
BLOCK = 128
PAIR = 2 * BLOCK

NORM_EPSILON = 1e-05
MASK_VALUE = -1e30

f32 = jnp.float32
bf16 = jnp.bfloat16


def swap(value, axis):
    return lax.ppermute(value, axis, [(0, 1), (1, 0)])


def diagonal(value):
    return lax.ppermute(value, ("side", "core"), [(0, 3), (3, 0), (1, 2), (2, 1)])


def ring(value):
    count = lax.axis_size("shard")
    return lax.ppermute(value, "shard", [(i, (i + 1) % count) for i in range(count)])


def over_shards(value, step):
    pairs = [(i, i ^ step) for i in range(lax.axis_size("shard"))]
    return lax.ppermute(value, "shard", pairs)


def after(value, *others):
    return lax.optimization_barrier((value,) + others)[0]


def blank(shape, dtype):
    return pl.pallas_call(
        lambda out: None,
        out_shape=jax.ShapeDtypeStruct(shape, dtype),
        out_specs=pl.BlockSpec(memory_space=pl.ANY),
        name="blank",
    )()


def dot_nn(left, right):
    return lax.dot_general(left, right, (((1,), (0,)), ((), ())), preferred_element_type=f32)


def dot_tn(left, right):
    return lax.dot_general(left, right, (((0,), (0,)), ((), ())), preferred_element_type=f32)


def dot_nt(left, right):
    return lax.dot_general(left, right, (((1,), (1,)), ((), ())), preferred_element_type=f32)


def exact(left, right, dims):
    return lax.dot_general(
        left, right, (dims, ((), ())), precision=lax.Precision.HIGHEST, preferred_element_type=f32
    )


def norm_forward(resid, gain, shift):
    center = resid - jnp.mean(resid, axis=-1, keepdims=True)
    inverse = lax.rsqrt(jnp.mean(center * center, axis=-1, keepdims=True) + NORM_EPSILON)
    normed = center * inverse
    return (normed * gain + shift, normed, inverse)


def norm_backward(grad_out, normed, inverse, gain):
    scaled = grad_out * gain
    grad_in = inverse * (
        scaled
        - jnp.mean(scaled, axis=-1, keepdims=True)
        - normed * jnp.mean(scaled * normed, axis=-1, keepdims=True)
    )
    return (grad_in, jnp.sum(grad_out * normed, axis=0), jnp.sum(grad_out, axis=0))


def block_rows(index):
    return pl.ds(pl.multiple_of(index * BLOCK, BLOCK), BLOCK)


def split_head(head, width, qkv, qs, ks, vs):
    first = head * HEAD_DIM
    qs[...] = qkv[:, first : first + HEAD_DIM] * bf16(HEAD_DIM**-0.5)
    ks[...] = qkv[:, width + first : width + first + HEAD_DIM]
    vs[...] = qkv[:, 2 * width + first : 2 * width + first + HEAD_DIM]


def tile_scores(keys, trunk_keys, queries, rows, masked):
    parts = [dot_nt(trunk_keys, queries)]
    if masked is not None:
        parts.append(dot_nt(keys[rows[0], :], queries[:BLOCK]))
        parts.append(dot_nt(keys[rows[1], :], queries[BLOCK:]))
        parts.append(dot_nt(keys[rows[2], :], queries) + masked)
    return parts


def over_keys(reduce, join, parts):
    result = reduce(parts[0], axis=0, keepdims=True)
    if len(parts) > 1:
        own = [reduce(parts[1], axis=0, keepdims=True), reduce(parts[2], axis=0, keepdims=True)]
        result = join(result, jnp.concatenate(own, axis=1))
        result = join(result, reduce(parts[3], axis=0, keepdims=True))
    return result


def for_parts(row, count):
    return [row, row[:, :BLOCK], row[:, BLOCK:], row][:count]


def tile_softmax(parts):
    tops = for_parts(over_keys(jnp.max, jnp.maximum, parts), len(parts))
    exps = [jnp.exp(part - top) for part, top in zip(parts, tops)]
    return exps, over_keys(jnp.sum, jnp.add, exps)


def tile_places(tab, tile, blocks):
    first, second = tab[2 * tile], tab[2 * tile + 1]
    rows = [block_rows(first), block_rows(second), block_rows(tab[blocks + tile])]
    masked = jnp.where(tab[blocks + blocks // 2 + tile] == 2, 0.0, MASK_VALUE).astype(f32)
    return (first, second), rows, masked


def tile_loops(blocks, run):
    def trunk_step(tile, carry):
        run(tile, False)
        return carry

    def step(tile, carry):
        run(tile, True)
        return carry

    lax.fori_loop(0, TRUNK // 2, trunk_step, 0)
    lax.fori_loop(TRUNK // 2, blocks // 2, step, 0)


def place_of(index, part_blocks):
    quarter = index // part_blocks
    return quarter, block_rows(index - quarter * part_blocks)


def attn_fwd_kernel(head, heads, blocks, tab, qkv, before, out, qs, ks, vs, kt, vtt, result, sem):
    del before
    part_blocks = blocks // 4
    split_head(head, heads * HEAD_DIM, qkv, qs, ks, vs)
    for j in range(TRUNK):
        rows = block_rows(tab[j])
        kt[j * BLOCK : (j + 1) * BLOCK, :] = ks[rows, :]
        vtt[:, j * BLOCK : (j + 1) * BLOCK] = vs[rows, :].T

    def run(tile, beside):
        pair, rows, masked = tile_places(tab, tile, blocks)
        queries = jnp.concatenate([qs[rows[0], :], qs[rows[1], :]], axis=0)
        parts = tile_scores(ks, kt[...], queries, rows, masked if beside else None)
        exps, total = tile_softmax(parts)
        exps = [part.astype(bf16) for part in exps]
        acc = dot_nn(vtt[...], exps[0])
        if beside:
            own = [dot_tn(vs[rows[0], :], exps[1]), dot_tn(vs[rows[1], :], exps[2])]
            acc = acc + jnp.concatenate(own, axis=1) + dot_tn(vs[rows[2], :], exps[3])
        acc = (acc / total).astype(bf16)
        for i in range(2):
            quarter, columns = place_of(pair[i], part_blocks)
            result[quarter, :, columns] = acc[:, i * BLOCK : (i + 1) * BLOCK]

    tile_loops(blocks, run)
    span = pl.ds(head * HEAD_DIM, HEAD_DIM)
    copy = pltpu.make_async_copy(result, out.at[:, span, :], sem)
    copy.start()
    copy.wait()


def attn_bwd_kernel(
    head, heads, blocks, tab, qkv, dot, before, out, *scratch
):
    del before
    qs, ks, vs, kt, vt, ktt, dkt, dvt, dka, dva, result, sem = scratch
    part_blocks = blocks // 4
    split_head(head, heads * HEAD_DIM, qkv, qs, ks, vs)
    for j in range(TRUNK):
        rows = block_rows(tab[j])
        span = slice(j * BLOCK, (j + 1) * BLOCK)
        kt[span, :] = ks[rows, :]
        vt[span, :] = vs[rows, :]
        ktt[:, span] = ks[rows, :].T
    dkt[...] = jnp.zeros_like(dkt)
    dvt[...] = jnp.zeros_like(dvt)
    dka[...] = jnp.zeros_like(dka)
    dva[...] = jnp.zeros_like(dva)
    lanes = slice(head * HEAD_DIM, (head + 1) * HEAD_DIM)

    def run(tile, beside):
        pair, rows, masked = tile_places(tab, tile, blocks)
        queries = jnp.concatenate([qs[rows[0], :], qs[rows[1], :]], axis=0)
        places = [place_of(index, part_blocks) for index in pair]
        grads = jnp.concatenate([dot[q, lanes, columns] for q, columns in places], axis=1)
        parts = tile_scores(ks, kt[...], queries, rows, masked if beside else None)
        exps, total = tile_softmax(parts)
        count = len(parts)
        inverses = for_parts(1.0 / total, count)
        probs = [part * inv for part, inv in zip(exps, inverses)]
        grad_parts = [dot_nn(vt[...], grads)]
        if beside:
            grad_parts.append(dot_nn(vs[rows[0], :], grads[:, :BLOCK]))
            grad_parts.append(dot_nn(vs[rows[1], :], grads[:, BLOCK:]))
            grad_parts.append(dot_nn(vs[rows[2], :], grads))
        products = [p * g for p, g in zip(probs, grad_parts)]
        deltas = for_parts(over_keys(jnp.sum, jnp.add, products), count)
        score_grads = [(p * (g - d)).astype(bf16) for p, g, d in zip(probs, grad_parts, deltas)]
        probs = [p.astype(bf16) for p in probs]
        dvt[...] += dot_nt(probs[0], grads)
        dkt[...] += dot_nn(score_grads[0], queries)
        query_grad = dot_nn(ktt[...], score_grads[0])
        if beside:
            dva[rows[0], :] += dot_nt(probs[1], grads[:, :BLOCK])
            dva[rows[1], :] += dot_nt(probs[2], grads[:, BLOCK:])
            dva[rows[2], :] += dot_nt(probs[3], grads)
            dka[rows[0], :] += dot_nn(score_grads[1], queries[:BLOCK])
            dka[rows[1], :] += dot_nn(score_grads[2], queries[BLOCK:])
            dka[rows[2], :] += dot_nn(score_grads[3], queries)
            own = [
                dot_tn(ks[rows[0], :], score_grads[1]),
                dot_tn(ks[rows[1], :], score_grads[2]),
            ]
            query_grad = query_grad + jnp.concatenate(own, axis=1)
            query_grad = query_grad + dot_tn(ks[rows[2], :], score_grads[3])
        query_grad = (query_grad * HEAD_DIM**-0.5).astype(bf16)
        result[0, :, rows[0]] = query_grad[:, :BLOCK]
        result[0, :, rows[1]] = query_grad[:, BLOCK:]

    tile_loops(blocks, run)
    for j in range(TRUNK):
        rows = block_rows(tab[j])
        span = slice(j * BLOCK, (j + 1) * BLOCK)
        dka[rows, :] = dkt[span, :]
        dva[rows, :] = dvt[span, :]
    result[1] = dka[...].T.astype(bf16)
    result[2] = dva[...].T.astype(bf16)
    copies = [
        pltpu.make_async_copy(
            result.at[i], out.at[pl.ds((i * heads + head) * HEAD_DIM, HEAD_DIM), :], sem.at[i]
        )
        for i in range(3)
    ]
    for copy in copies:
        copy.start()
    for copy in copies:
        copy.wait()


def attn_forward(table, qkv, before, head, heads, blocks):
    rows = qkv.shape[0]
    trunk = TRUNK * BLOCK
    return pl.pallas_call(
        functools.partial(attn_fwd_kernel, head, heads, blocks),
        out_shape=jax.ShapeDtypeStruct(before.shape, bf16),
        in_specs=[
            pl.BlockSpec(memory_space=pltpu.SMEM),
            pl.BlockSpec(memory_space=pltpu.VMEM),
            pl.BlockSpec(memory_space=pl.ANY),
        ],
        out_specs=pl.BlockSpec(memory_space=pl.ANY),
        input_output_aliases={2: 0},
        scratch_shapes=[pltpu.VMEM((rows, HEAD_DIM), bf16)] * 3
        + [pltpu.VMEM((trunk, HEAD_DIM), bf16), pltpu.VMEM((HEAD_DIM, trunk), bf16)]
        + [pltpu.VMEM((4, HEAD_DIM, rows // 4), bf16), pltpu.SemaphoreType.DMA],
        compiler_params=pltpu.CompilerParams(vmem_limit_bytes=32 << 20),
        cost_estimate=pl.CostEstimate(
            flops=6 * rows * trunk * BLOCK,
            bytes_accessed=8 * rows * HEAD_DIM,
            transcendentals=0,
        ),
        name="tree_attention",
    )(table, qkv, before)


def attn_backward(table, qkv, out_grad, before, head, heads, blocks):
    rows = qkv.shape[0]
    trunk = TRUNK * BLOCK
    return pl.pallas_call(
        functools.partial(attn_bwd_kernel, head, heads, blocks),
        out_shape=jax.ShapeDtypeStruct(before.shape, bf16),
        in_specs=[
            pl.BlockSpec(memory_space=pltpu.SMEM),
            pl.BlockSpec(memory_space=pltpu.VMEM),
            pl.BlockSpec(memory_space=pltpu.VMEM),
            pl.BlockSpec(memory_space=pl.ANY),
        ],
        out_specs=pl.BlockSpec(memory_space=pl.ANY),
        input_output_aliases={3: 0},
        scratch_shapes=[pltpu.VMEM((rows, HEAD_DIM), bf16)] * 3
        + [pltpu.VMEM((trunk, HEAD_DIM), bf16)] * 2
        + [pltpu.VMEM((HEAD_DIM, trunk), bf16)]
        + [pltpu.VMEM((trunk, HEAD_DIM), f32)] * 2
        + [pltpu.VMEM((rows, HEAD_DIM), f32)] * 2
        + [pltpu.VMEM((3, HEAD_DIM, rows), bf16), pltpu.SemaphoreType.DMA((3,))],
        compiler_params=pltpu.CompilerParams(vmem_limit_bytes=40 << 20),
        cost_estimate=pl.CostEstimate(
            flops=16 * rows * trunk * BLOCK,
            bytes_accessed=14 * rows * HEAD_DIM,
            transcendentals=0,
        ),
        name="tree_attention_grad",
    )(table, qkv, out_grad, before)


def attention_table(path):
    blocks = path.shape[1]
    place = jnp.arange(blocks, dtype=jnp.int32)
    kind = (path[1] != path[0]).astype(jnp.int32) + (path[2] != path[1]).astype(jnp.int32)
    key = kind * 65536 + jnp.where(kind == 2, path[1] * 32, 0) + place
    rank = jnp.sum((key[None, :] < key[:, None]).astype(jnp.int32), axis=1)
    branch = jnp.sum(
        jnp.where((kind[None, :] == 1) & (path[2][None, :] == path[1][:, None]), place[None, :], 0),
        axis=1,
    )
    slot = (rank[None, :] == place[:, None]).astype(jnp.int32)
    columns = jnp.stack([place, jnp.where(kind == 2, branch, 0), kind])
    sorted_columns = jnp.sum(slot[None] * columns[:, None, :], axis=2)
    return jnp.concatenate([sorted_columns[0], sorted_columns[1, ::2], sorted_columns[2, ::2]])


def assemble_kernel(count, spans, flags, *refs):
    pieces, outs = refs[: 2 * count], refs[2 * count :]
    slab = pieces[0].shape[0]
    for j in range(2):
        for k in range(count):
            place = lax.rem(flags[0] + (count - k), count)
            rows = pl.ds(pl.multiple_of(place * slab, 16), slab)
            piece = pieces[j * count + k]
            for out, (lanes, kind) in zip(outs, spans):
                width = lanes.stop - lanes.start
                if kind == 1 or j == 0 and kind == 0:
                    out[rows, j * width : (j + 1) * width] = piece[:, lanes]
                for crossed in range(2 if kind == 2 else 0):

                    @pl.when(flags[1] == crossed)
                    def _():
                        first = (j ^ crossed) * width
                        out[rows, first : first + width] = piece[:, lanes]


def assembled(shard, crossed, own, twin, spans):
    count = len(own)
    rows = count * own[0].shape[0]
    vmem = pl.BlockSpec(memory_space=pltpu.VMEM)
    shapes = [
        jax.ShapeDtypeStruct((rows, (lanes.stop - lanes.start) * (2 if kind else 1)), bf16)
        for lanes, kind in spans
    ]
    return pl.pallas_call(
        functools.partial(assemble_kernel, count, spans),
        out_shape=shapes,
        in_specs=[pl.BlockSpec(memory_space=pltpu.SMEM)] + [vmem] * (2 * count),
        out_specs=[vmem] * len(spans),
        compiler_params=pltpu.CompilerParams(vmem_limit_bytes=24 << 20),
        cost_estimate=pl.CostEstimate(
            flops=0, bytes_accessed=4 * sum(piece.size for piece in own + twin), transcendentals=0
        ),
        name="assembled_weights",
    )(jnp.stack([shard, crossed]).astype(jnp.int32), *own, *twin)


def pack_kernel(count, j, flags, up, down, proj, out, small, *pieces):
    slab = up.shape[0] // count
    group = pieces[0].shape[1] - up.shape[1] - down.shape[1] - proj.shape[1]
    for k in range(count):
        place = lax.rem(flags[0] + (count - k - 1), count)
        rows = pl.ds(pl.multiple_of(place * slab, 16), slab)
        first = 0
        for source in (up, down, proj):
            pieces[k][:slab, first : first + source.shape[1]] = source[rows, :]
            first += source.shape[1]
        for crossed in range(2):

            @pl.when(flags[1] == crossed)
            def _():
                lane = (j ^ crossed) * group
                pieces[k][:slab, first:] = out[rows, lane : lane + group]

        pieces[k][slab:, :] = small[place]


def packed_pieces(shard, crossed, count, up, down, proj, out, small, j):
    rows = up.shape[0] // count + small.shape[1]
    width = small.shape[2]
    vmem = pl.BlockSpec(memory_space=pltpu.VMEM)
    return pl.pallas_call(
        functools.partial(pack_kernel, count, j),
        out_shape=[jax.ShapeDtypeStruct((rows, width), bf16)] * count,
        in_specs=[pl.BlockSpec(memory_space=pltpu.SMEM)] + [vmem] * 5,
        out_specs=[vmem] * count,
        compiler_params=pltpu.CompilerParams(vmem_limit_bytes=24 << 20),
        cost_estimate=pl.CostEstimate(
            flops=0, bytes_accessed=4 * count * rows * width, transcendentals=0
        ),
        name="packed_gradients",
    )(jnp.stack([shard, crossed]).astype(jnp.int32), up, down, proj, out, small)


def place_kernel(start, places, first, second, third, fourth, before, out, wide, sem):
    del before
    rows = first.shape[0]
    half, core = places[0], places[1]
    spots = [(half, core), (1 - half, core), (half, 1 - core), (1 - half, 1 - core)]
    copies = []
    for i, piece in enumerate((first, second, third, fourth)):
        wide[i] = piece[...].astype(wide.dtype)
        row, column = spots[i]
        target = out.at[row, column, pl.ds(start, rows), :]
        copy = pltpu.make_async_copy(wide.at[i], target, sem.at[i])
        copy.start()
        copies.append(copy)
    for copy in copies:
        copy.wait()


def place_rows(places, pieces, before, start):
    rows, width = pieces[0].shape
    vmem = pl.BlockSpec(memory_space=pltpu.VMEM)
    return pl.pallas_call(
        functools.partial(place_kernel, start),
        out_shape=jax.ShapeDtypeStruct(before.shape, before.dtype),
        in_specs=[pl.BlockSpec(memory_space=pltpu.SMEM)]
        + [vmem] * 4
        + [pl.BlockSpec(memory_space=pl.ANY)],
        out_specs=pl.BlockSpec(memory_space=pl.ANY),
        input_output_aliases={5: 0},
        scratch_shapes=[
            pltpu.VMEM((4, rows, width), before.dtype),
            pltpu.SemaphoreType.DMA((4,)),
        ],
        compiler_params=pltpu.CompilerParams(vmem_limit_bytes=24 << 20),
        cost_estimate=pl.CostEstimate(
            flops=0, bytes_accessed=24 * rows * width, transcendentals=0
        ),
        name="placed_rows",
    )(places, *pieces, before)


def student_kernel(part_blocks, labels, rows, weight, shift, query, student, weights, stats):
    width = weight.shape[1]
    pool_dim = width // POOL_HEADS
    value = dot_nn(rows[...], weight[...]) + shift[...]
    student[...] = value
    lane = lax.broadcasted_iota(jnp.int32, (1, width), 1)
    first_head = lane < pool_dim
    product = value * query[...]
    scores = [
        jnp.sum(product[:, e * pool_dim : (e + 1) * pool_dim], axis=1, keepdims=True)
        for e in range(POOL_HEADS)
    ]
    stats[...] = jnp.zeros_like(stats)
    for block in range(part_blocks):
        span = slice(block * BLOCK, (block + 1) * BLOCK)
        peaks = [jnp.max(score[span], axis=0, keepdims=True) for score in scores]
        exps = [jnp.exp(score[span] - peak) for score, peak in zip(scores, peaks)]
        masses = [jnp.sum(part, axis=0, keepdims=True) for part in exps]
        lanes = jnp.where(first_head, exps[0], exps[1])
        weights[span, :] = lanes
        stats[block : block + 1, :width] = jnp.sum(lanes * value[span], axis=0, keepdims=True)
        label = jnp.full((1, width), labels[block], jnp.int32).astype(f32)
        tail = jnp.where(lane == 4, label, 0.0)
        for place, part in enumerate(peaks + masses):
            tail = jnp.where(lane == place, part, tail)
        stats[block : block + 1, width:] = tail


def student_stats(labels, rows, weight, shift, query, part_blocks):
    count = rows.shape[0]
    width = weight.shape[1]
    vmem = pl.BlockSpec(memory_space=pltpu.VMEM)
    return pl.pallas_call(
        functools.partial(student_kernel, part_blocks),
        out_shape=(
            jax.ShapeDtypeStruct((count, width), f32),
            jax.ShapeDtypeStruct((count, width), f32),
            jax.ShapeDtypeStruct((8, 2 * width), f32),
        ),
        in_specs=[pl.BlockSpec(memory_space=pltpu.SMEM)] + [vmem] * 4,
        out_specs=(vmem,) * 3,
        cost_estimate=pl.CostEstimate(
            flops=2 * rows.size * width, bytes_accessed=2 * rows.size, transcendentals=count
        ),
        name="student_stats",
    )(labels, rows, weight, shift, query)


def pool_kernel(
    part_blocks,
    own,
    near,
    across,
    corner,
    member,
    leaf,
    dense,
    head,
    dense_shift,
    cls_shift,
    student,
    weights,
    query,
    student_low,
    grad_dense,
    grad_head,
    vectors,
):
    width = dense.shape[0]
    pool_dim = width // POOL_HEADS
    pool_scale = pool_dim ** (-0.5)
    stats = jnp.concatenate([own[...], near[...], across[...], corner[...]], axis=0)
    moment = stats[:, :width]
    seen = member[...] > 0.0
    is_leaf = leaf[...] > 0.0
    coeffs = []
    pooled = []
    for e in range(POOL_HEADS):
        peak = stats[:, width + e : width + e + 1]
        mass = stats[:, width + POOL_HEADS + e : width + POOL_HEADS + e + 1]
        top = jnp.max(jnp.where(seen, peak, MASK_VALUE), axis=0, keepdims=True)
        factor = jnp.where(seen, jnp.exp(jnp.where(seen, peak - top, MASK_VALUE)), 0.0)
        total = jnp.sum(factor * mass, axis=0, keepdims=True)
        total = jnp.where(total > 0.0, total, 1.0)
        coeff = factor / total
        coeffs.append(coeff)
        lanes = slice(e * pool_dim, (e + 1) * pool_dim)
        pooled.append(exact(coeff, moment[:, lanes], ((0,), (0,))))
    pooled = jnp.concatenate(pooled, axis=1)
    dense_out = jnp.tanh(exact(pooled, dense[...], ((1,), (0,))) + dense_shift[...])
    logits = exact(dense_out, head[...], ((1,), (0,))) + cls_shift[...]
    logits = logits - jnp.max(logits, axis=1, keepdims=True)
    chances = jnp.exp(logits)
    chances = chances / jnp.sum(chances, axis=1, keepdims=True)
    label = stats[:, width + 2 * POOL_HEADS : width + 2 * POOL_HEADS + 1]
    classes = lax.broadcasted_iota(jnp.int32, (1, width), 1).astype(f32)
    onehot = jnp.where(label == classes, 1.0, 0.0)
    grad_logits = jnp.where(is_leaf, chances - onehot, 0.0)
    grad_head[...] = exact(dense_out, grad_logits, ((0,), (0,)))
    grad_pre = exact(grad_logits, head[...], ((1,), (1,))) * (1.0 - dense_out * dense_out)
    grad_dense[...] = exact(pooled, grad_pre, ((0,), (0,)))
    grad_pooled = exact(grad_pre, dense[...], ((1,), (1,)))
    product = grad_pooled * pooled
    spread = []
    offset = []
    for e in range(POOL_HEADS):
        lanes = slice(e * pool_dim, (e + 1) * pool_dim)
        spread.append(exact(coeffs[e], grad_pooled[:, lanes], ((1,), (0,))))
        inner = jnp.sum(product[:, lanes], axis=1, keepdims=True)
        inner = jnp.broadcast_to(inner, (inner.shape[0], pool_dim))
        offset.append(exact(coeffs[e], inner, ((1,), (0,))))
    spread = jnp.concatenate(spread, axis=1)
    offset = jnp.concatenate(offset, axis=1)
    grad_query = jnp.zeros((1, width), f32)
    grad_shift = jnp.zeros((1, width), f32)
    first_head = lax.broadcasted_iota(jnp.int32, (1, width), 1) < pool_dim
    for block in range(part_blocks):
        span = slice(block * BLOCK, (block + 1) * BLOCK)
        value = student[span, :]
        weight = weights[span, :]
        row = spread[block : block + 1]
        product = value * row
        inner = jnp.where(
            first_head,
            jnp.sum(product[:, :pool_dim], axis=1, keepdims=True),
            jnp.sum(product[:, pool_dim:], axis=1, keepdims=True),
        )
        grad_score = weight * (inner - offset[block : block + 1])
        grad_query = grad_query + jnp.sum(grad_score * value, axis=0, keepdims=True)
        low = (weight * row + grad_score * query[...]).astype(bf16)
        student_low[span, :] = low
        grad_shift = grad_shift + jnp.sum(low.astype(f32), axis=0, keepdims=True)
    vectors[0:1, :] = jnp.sum(grad_pre, axis=0, keepdims=True)
    vectors[1:2, :] = jnp.sum(grad_logits, axis=0, keepdims=True)
    vectors[2:3, :] = grad_query * pool_scale
    vectors[3:4, :] = grad_shift
    vectors[4:8, :] = jnp.zeros((4, width), f32)


def pool_classifier(part_blocks, *operands):
    student = operands[-3]
    width = student.shape[1]
    return pl.pallas_call(
        functools.partial(pool_kernel, part_blocks),
        out_shape=(
            jax.ShapeDtypeStruct(student.shape, bf16),
            jax.ShapeDtypeStruct((width, width), f32),
            jax.ShapeDtypeStruct((width, width), f32),
            jax.ShapeDtypeStruct((8, width), f32),
        ),
        cost_estimate=pl.CostEstimate(
            flops=2000 * width * width, bytes_accessed=16 * student.size, transcendentals=0
        ),
        name="pool_classifier",
    )(*operands)


def body(
    tokens,
    cotangent,
    block_path,
    labels,
    w_attn_in,
    attn_bias,
    w_attn_out,
    w_up,
    up_bias,
    w_down,
    norm_gain,
    layer_bias,
    stu_proj,
    stu_bias,
    pool_query,
    stu_dense,
    stu_head,
    class_bias,
):
    row_count, model = tokens.shape[1:]
    own_blocks = labels.shape[1]
    tree_blocks = 2 * own_blocks
    group_width = w_attn_in.shape[2]
    heads = group_width // HEAD_DIM
    slab = w_up.shape[0]
    hidden = w_up.shape[1]
    shards = lax.axis_size("shard")
    trees = lax.axis_size("tree")
    stu_width = stu_proj.shape[1]
    pool_dim = stu_width // POOL_HEADS
    pool_scale = pool_dim ** (-0.5)
    class_count = class_bias.shape[0]
    part_rows = row_count // 2
    part_blocks = own_blocks // 2

    shard = lax.axis_index("shard")
    tree = lax.axis_index("tree")
    side = lax.axis_index("side")
    half = lax.axis_index("half")
    core = lax.axis_index("core")

    shift_rows = layer_bias.astype(f32)
    gain_rows = norm_gain.astype(f32)
    stu_shifts = stu_bias.astype(f32)
    pool_vec = pool_query.astype(f32)

    def by_shard(pieces):
        result = blank((shards,) + pieces[0].shape, pieces[0].dtype)
        for k, piece in enumerate(pieces):
            result = lax.dynamic_update_index_in_dim(result, piece, (shard - k) % shards, 0)
        return result

    def rows_of(array, part):
        place = (half, part * part_rows, 0)
        return lax.dynamic_slice(array, place, (1, part_rows, model))[0]

    own_part = rows_of(tokens, core)
    other_part = swap(own_part, "side")
    other_twin = swap(other_part, "core")
    own_rest = rows_of(after(tokens, own_part), 1 - core)
    tree_rows = jnp.concatenate([own_part, other_part, own_rest, other_twin], axis=0)

    qkv_width = 3 * group_width
    bias_row = jnp.concatenate([attn_bias[0], jnp.zeros((group_width,), bf16), attn_bias[1]])
    up_rows = jnp.pad(up_bias.reshape(2, hidden // 2), ((0, 0), (0, qkv_width - hidden // 2)))
    qkv_message = jnp.concatenate(
        [
            w_attn_in.transpose(1, 0, 2).reshape(slab, qkv_width),
            bias_row[None],
            up_rows,
            jnp.zeros((13, qkv_width), bf16),
        ],
        axis=0,
    )
    qkv_twin = swap(after(qkv_message, own_part), "half")
    twin_bias = qkv_twin[slab + 1 : slab + 3, : hidden // 2].reshape(hidden)
    qkv_message = jnp.where(side == half, qkv_message, qkv_twin)
    qkv_bias = qkv_message[slab].astype(f32)
    qkv_pieces = [qkv_message]
    for k in range(1, shards):
        qkv_pieces.append(ring(after(qkv_pieces[-1], other_part) if k == 2 else qkv_pieces[-1]))
    qkv_weight = by_shard([piece[:slab] for piece in qkv_pieces]).reshape(model, qkv_width)

    stu_lanes = slice(hidden, hidden + stu_width)
    out_lanes = slice(hidden + stu_width, hidden + stu_width + group_width)
    message_one = jnp.concatenate([w_up, stu_proj, w_attn_out.T], axis=1)
    message_two = w_down.T
    own_one = [after(message_one, qkv_pieces[-1], other_twin)]
    own_one.append(ring(own_one[0]))
    twin_one = [swap(after(message_one, qkv_message), "half")]

    paths = lax.dynamic_index_in_dim(block_path, half, 0, keepdims=False)
    paths = lax.dynamic_slice_in_dim(paths, tree * tree_blocks, tree_blocks, 1)
    paths = after(paths, qkv_pieces[1])
    quarters = paths.reshape(3, 2, 2, part_blocks)
    quarters = jnp.where(side == 0, quarters, quarters[:, ::-1])
    quarters = jnp.where(core == 0, quarters, quarters[:, :, ::-1])
    table = attention_table(quarters.swapaxes(1, 2).reshape(3, tree_blocks))

    quarters = jnp.pad(quarters, ((0, 0),) * 3 + ((0, 8 - part_blocks),), constant_values=-1)
    quarters = quarters.reshape(3, 32)
    is_leaf = (quarters[1] != quarters[2]).astype(f32)
    member = jnp.any(quarters[2][:, None, None] == quarters.T[None, :, :], axis=2).astype(f32)
    member = member * is_leaf[None, :]
    leaf_column = is_leaf[:, None]
    lane_pad = stu_width - class_count
    dense_full = stu_dense.astype(f32)
    head_padded = jnp.pad(stu_head.astype(f32), ((0, 0), (0, lane_pad)))
    cls_padded = jnp.pad(
        class_bias.astype(f32)[None, :], ((0, 0), (0, lane_pad)), constant_values=MASK_VALUE
    )
    own_labels = lax.dynamic_slice(labels, (half, core * part_blocks), (1, part_blocks))[0]
    dense_shift = stu_bias[1:2].astype(f32)
    proj_shift = stu_bias[0:1].astype(f32)
    scaled_query = (pool_vec * pool_scale)[None, :]
    prepared = lax.optimization_barrier(
        (
            tree_rows,
            member,
            leaf_column,
            dense_full,
            head_padded,
            cls_padded,
            own_labels,
            dense_shift,
            proj_shift,
            scaled_query,
        )
    )
    tree_rows, member, leaf_column, dense_full, head_padded, cls_padded = prepared[:6]
    own_labels, dense_shift, proj_shift, scaled_query = prepared[6:]

    qkv = (dot_nn(tree_rows, qkv_weight) + qkv_bias).astype(bf16)
    attended = blank((4, group_width, part_rows), bf16)
    attended = attn_forward(table, qkv, attended, 0, heads, tree_blocks)
    twin_two = [swap(after(message_two, twin_one[0]), "half")]
    one = after(own_one[1], attended)
    own_one.append(ring(one))
    twin_one.append(swap(one, "half"))
    attended = after(attended, twin_one[0], twin_two[0])
    attended = attn_forward(table, qkv, attended, 1, heads, tree_blocks)
    one = after(own_one[2], attended)
    own_one.append(ring(one))
    twin_one.append(swap(one, "half"))
    own_two = [after(message_two, attended)]
    own_two.append(ring(own_two[0]))
    attended = after(attended, twin_one[1])
    attended = attn_forward(table, qkv, attended, 2, heads, tree_blocks)
    twin_one.append(swap(after(own_one[3], attended), "half"))
    own_two.append(ring(after(own_two[1], attended)))
    attended = after(attended, twin_one[2])

    def exchange(pieces):
        return [
            pieces[0],
            swap(pieces[1], "core"),
            swap(pieces[2], "side"),
            diagonal(pieces[3]),
        ]

    def at(array, place):
        return lax.dynamic_index_in_dim(array, place, 0, keepdims=False)

    def placed(pieces, places):
        result = blank((len(pieces),) + pieces[0].shape, pieces[0].dtype)
        for piece, place in zip(pieces, places):
            result = lax.dynamic_update_index_in_dim(result, piece, place, 0)
        return result

    quarter_places = [0, 2, 1, 3]
    crossed = jnp.where(side == half, 0, 1)

    def in_quarters(pieces):
        kept, near, across, corner = pieces
        return jnp.stack([kept, across, near, corner])

    crossing = exchange([attended[place] for place in quarter_places])
    own_one[0] = after(own_one[0], *crossing[1:])
    heads_own = in_quarters(crossing)
    heads_own = heads_own.reshape(4 * group_width, part_rows)
    heads_own = after(heads_own, twin_one[3], own_two[2])
    twin_two.append(swap(after(own_two[1], heads_own), "half"))
    twin_two.append(swap(after(own_two[2], heads_own), "half"))
    own_two.append(ring(after(own_two[2], heads_own)))
    up_weight, stu_weight, out_half = assembled(
        shard,
        crossed,
        own_one,
        twin_one,
        [(slice(0, hidden), 1), (stu_lanes, 0), (out_lanes, 2)],
    )
    out_weight = jnp.concatenate([out_half, swap(out_half, "core")], axis=1)
    hidden_shift = jnp.concatenate([up_bias, twin_bias]).astype(f32)

    attn = lax.dot_general(
        heads_own, out_weight, (((0,), (1,)), ((), ())), preferred_element_type=f32
    )
    resid_one = own_part.astype(f32) + (attn + shift_rows[0])
    hidden_one, normed_one, inverse_one = norm_forward(resid_one, gain_rows[0], shift_rows[2])
    hidden_low = hidden_one.astype(bf16)
    hidden_low = after(hidden_low, own_two[3])
    twin_two.append(swap(after(own_two[3], hidden_low), "half"))

    hidden_both = jnp.concatenate([hidden_low, swap(hidden_low, "core")], axis=0)
    pre_act = dot_nn(hidden_both, up_weight) + hidden_shift
    normal_cdf = 0.5 * (1.0 + lax.erf(pre_act * 0.7071067811865476))
    active = (pre_act * normal_cdf).astype(bf16)
    slope = normal_cdf + pre_act * jnp.exp(-0.5 * pre_act * pre_act) * 0.3989422804014327
    own_two[0] = after(own_two[0], active)
    (down_weight,) = assembled(shard, crossed, own_two, twin_two, [(slice(0, hidden), 1)])
    ffn_far = swap(dot_nt(active[part_rows:], down_weight).astype(bf16), "core")
    ffn = dot_nt(active[:part_rows], down_weight) + ffn_far.astype(f32)
    hidden_two, normed_two, inverse_two = norm_forward(
        hidden_one + ffn + shift_rows[1], gain_rows[1], shift_rows[3]
    )
    block_low = hidden_two.astype(bf16)

    def everywhere(rows, other):
        return rows, other, [swap(rows, "core"), swap(other, "core")]

    def placed(result, start, rows, other, twins):
        places = jnp.stack([half, core]).astype(jnp.int32)
        return place_rows(places, [rows, other] + twins, result, start)

    block_other = swap(block_low, "half")

    student, weights, stats = student_stats(
        own_labels, block_low, stu_weight, proj_shift, scaled_query, part_blocks
    )
    student_low, grad_dense, grad_head, pool_vectors = pool_classifier(
        part_blocks,
        *exchange([stats] * 4),
        member,
        leaf_column,
        dense_full,
        head_padded,
        dense_shift,
        cls_padded,
        student,
        weights,
        scaled_query,
    )
    grad_proj = dot_tn(block_low, student_low)

    upstream = lax.dynamic_slice(
        cotangent, (half, core * part_rows, 0), (1, part_rows, model)
    )[0].astype(f32)
    grad_two = upstream + dot_nt(student_low, stu_weight)
    resid_grad_two, gain_grad_two, shift_grad_two = norm_backward(
        grad_two, normed_two, inverse_two, gain_rows[1]
    )
    down_shift_grad = jnp.sum(resid_grad_two, axis=0)
    ffn_low = resid_grad_two.astype(bf16)
    ffn_both = jnp.concatenate([ffn_low, swap(ffn_low, "core")], axis=0)
    pre_low = (dot_nn(ffn_both, down_weight) * slope).astype(bf16)
    grad_hidden_shift = jnp.sum(pre_low.astype(f32), axis=0)
    far_one = swap(dot_nt(pre_low[part_rows:], up_weight).astype(bf16), "core")
    grad_one = resid_grad_two + dot_nt(pre_low[:part_rows], up_weight) + far_one.astype(f32)

    resid_grad_one, gain_grad_one, shift_grad_one = norm_backward(
        grad_one, normed_one, inverse_one, gain_rows[0]
    )
    out_shift_grad = jnp.sum(resid_grad_one, axis=0)
    attn_low = resid_grad_one.astype(bf16)
    block_spread = everywhere(block_low, after(block_other, attn_low))
    heads_grad = lax.dot_general(
        out_weight, attn_low, (((0,), (1,)), ((), ())), preferred_element_type=f32
    ).astype(bf16)
    grad_out = lax.dot_general(
        attn_low, heads_own, (((0,), (1,)), ((), ())), preferred_element_type=f32
    ).astype(bf16)
    heads_grad = heads_grad.reshape(4, group_width, part_rows)
    pieces = [heads_grad[place] for place in quarter_places]
    pieces = lax.optimization_barrier((*pieces, grad_out, ffn_both, pre_low))
    ffn_both, pre_low = pieces[5:7]
    attended_grad = in_quarters(exchange(pieces[:4]))

    def halves(array):
        return [array[:, :hidden], array[:, hidden:]]

    grad_down = [dot_tn(ffn_both, part).astype(bf16) for part in halves(active)]
    grad_up = [dot_tn(hidden_both, part).astype(bf16) for part in halves(pre_low)]

    up_grad = jnp.zeros((4, hidden), f32)
    for j in range(2):
        up_grad = lax.dynamic_update_slice(
            up_grad,
            grad_hidden_shift[None, j * hidden : (j + 1) * hidden],
            (2 * jnp.where(j == 0, half, 1 - half) + core, 0),
        )
    first = jnp.where((side == 0) & (core == 0), 1.0, 0.0)
    pieces = [
        gain_grad_one,
        gain_grad_two,
        out_shift_grad,
        down_shift_grad,
        shift_grad_one,
        shift_grad_two,
        up_grad.reshape(-1),
        pool_vectors[3],
        pool_vectors[0] * first,
        pool_vectors[2],
        pool_vectors[1] * first,
        (grad_dense * first).reshape(-1),
        (grad_head[:, :16] * first).reshape(-1),
    ]
    sizes = [piece.size for piece in pieces]
    starts = [sum(sizes[:i]) for i in range(len(sizes) + 1)]
    packed = 2 * hidden + stu_width + group_width
    small = jnp.concatenate(pieces)
    small = jnp.pad(small, (0, -small.size % (shards * packed)))
    small_rows = small.size // (shards * packed)
    small = small.reshape(shards, small_rows, packed)
    small = jnp.pad(small, ((0, 0), (0, 16 - small_rows), (0, 0)))
    small = (small + swap(small, "core")).astype(bf16)

    half_out = 2 * group_width
    proj_low = grad_proj.astype(bf16)
    out_sum = grad_out[:, :half_out].astype(f32) + swap(grad_out[:, half_out:], "core").astype(f32)
    out_sum = out_sum.astype(bf16)
    proj_sum = (proj_low.astype(f32) + swap(proj_low, "core").astype(f32)).astype(bf16)
    out_sum = after(out_sum, attended_grad, *block_spread[2])
    kept, sent = [
        packed_pieces(
            shard, crossed, shards, grad_up[j], grad_down[j], proj_sum, out_sum, small, j
        )
        for j in range(2)
    ]

    def reduced(k, got, last):
        total = kept[k].astype(f32) + got.astype(f32)
        if last is not None:
            total = total + last.astype(f32)
        return total.astype(bf16)

    qkv_grad = blank((qkv_width, 4 * part_rows), bf16)
    qkv_grad = after(qkv_grad, *sent)
    got = [swap(sent[0], "half"), swap(sent[1], "half")]
    qkv_grad = attn_backward(table, qkv, attended_grad, qkv_grad, 0, heads, tree_blocks)
    kept = lax.optimization_barrier((qkv_grad, *kept))[1:]
    totals = [reduced(0, got[0], None)]
    passed = ring(totals[0])
    got.append(swap(after(sent[2], totals[0]), "half"))
    qkv_grad = after(qkv_grad, totals[0])
    qkv_grad = attn_backward(table, qkv, attended_grad, qkv_grad, 1, heads, tree_blocks)
    totals.append(reduced(1, after(got[1], qkv_grad), passed))
    passed = ring(totals[1])
    got.append(swap(after(sent[3], totals[1]), "half"))
    qkv_grad = after(qkv_grad, totals[1])
    qkv_grad = attn_backward(table, qkv, attended_grad, qkv_grad, 2, heads, tree_blocks)
    totals.append(reduced(2, after(got[2], qkv_grad), passed))
    passed = ring(totals[2])
    qkv_grad = after(qkv_grad, totals[2])

    def to_rows(columns):
        return lax.dot_general(
            columns, qkv_weight, (((0,), (1,)), ((), ())), preferred_element_type=f32
        ).astype(bf16)

    sent_grad = to_rows(qkv_grad[:, row_count:])
    near_grad = swap(sent_grad, "core")
    kept_grad = to_rows(after(qkv_grad, sent_grad)[:, :row_count])
    far_rows = kept_grad[part_rows:].astype(f32) + near_grad[part_rows:].astype(f32)
    far_rows = far_rows.astype(bf16)
    chunk = part_rows // 2
    spans = [slice(0, chunk), slice(chunk, part_rows)]
    far_rows = after(far_rows, got[3])
    far_chunks = [swap(far_rows[span], "side") for span in spans]

    grad_in = lax.dot_general(
        after(tree_rows, kept_grad), qkv_grad, (((0,), (1,)), ((), ())), preferred_element_type=f32
    )
    grad_in = grad_in.astype(bf16).reshape(shards, 2, slab // 2, qkv_width)
    kept_in = lax.dynamic_index_in_dim(grad_in, half, 1, keepdims=False)
    sent_in = lax.dynamic_index_in_dim(grad_in, 1 - half, 1, keepdims=False)
    bias_sums = jnp.sum(qkv_grad.astype(f32), axis=1).astype(bf16)
    bias_rows = bias_sums.reshape(shards, 1, qkv_width // shards)
    bias_rows = jnp.pad(bias_rows, ((0, 0), (0, 15), (0, qkv_width - qkv_width // shards)))
    got_in = swap(after(jnp.concatenate([sent_in, bias_rows], axis=1), far_rows), "half")
    kept_in = jnp.concatenate([kept_in, bias_rows], axis=1)

    def at_in(k):
        place = (shard - k) % shards
        return at(kept_in, place).astype(f32) + at(got_in, place).astype(f32)

    def tokens_part(i, far):
        near = kept_grad[:part_rows][spans[i]].astype(f32)
        near = near + near_grad[:part_rows][spans[i]].astype(f32)
        return (resid_grad_one[spans[i]] + near + far.astype(f32)).astype(bf16)

    tokens_grad = blank((2, 2, part_rows, model), f32)
    total = reduced(3, got[3], passed)
    far_low = after(far_chunks[0], total)
    rows_low = tokens_part(0, far_low)
    other_low = swap(rows_low, "half")
    twin_low = swap(rows_low, "core")
    total_far = swap(after(total, rows_low), "side")
    passed_in = ring(at_in(1).astype(bf16))
    far_high = after(far_chunks[1], twin_low, passed_in)
    rows_high = tokens_part(1, far_high)
    other_high = swap(rows_high, "half")
    twin_high = swap(rows_high, "core")
    passed_in = ring((at_in(2) + passed_in.astype(f32)).astype(bf16))
    other_low = after(other_low, rows_high, passed_in)
    twins_low = [twin_low, swap(other_low, "core")]
    block_out = placed(
        blank((2, 2, part_rows, model), bf16), 0, after(block_low, rows_high), *block_spread[1:]
    )
    block_out = block_out.reshape(2, row_count, model)
    passed_in = ring((at_in(3) + passed_in.astype(f32)).astype(bf16))
    tokens_grad = placed(tokens_grad, 0, rows_low, other_low, twins_low)
    other_high = after(other_high, passed_in)
    twins_high = [twin_high, swap(other_high, "core")]
    total = total.astype(f32) + total_far.astype(f32)
    part = at_in(4) + passed_in.astype(f32)
    if trees > 1:
        total = lax.psum(total, "tree")
        part = lax.psum(part, "tree")
    part = part.astype(bf16)
    half_slab = slab // 2
    part_twin = swap(part[:half_slab], "half")
    tokens_grad = placed(tokens_grad, chunk, rows_high, other_high, twins_high)
    tokens_grad = tokens_grad.reshape(2, row_count, model)

    small = total[slab : slab + small_rows]
    bias_part = jnp.pad(part[half_slab : half_slab + 1], ((0, 0), (0, packed - qkv_width)))
    small = jnp.concatenate([small, bias_part.astype(f32)], axis=0)
    small = jnp.pad(small, ((0, 16 - small.shape[0]), (0, 0))).astype(bf16)
    small_pieces = [small]
    for k in range(1, shards):
        pairs = [(i, (i + k) % shards) for i in range(shards)]
        small_pieces.append(lax.ppermute(small, "shard", pairs))
    small = by_shard(small_pieces).astype(f32)
    bias_own = small[:, small_rows, : qkv_width // shards].reshape(1, qkv_width)
    small = small[:, :small_rows].reshape(-1)

    group_in = jnp.concatenate(
        [
            jnp.where(half == 0, part[:half_slab], part_twin),
            jnp.where(half == 0, part_twin, part[:half_slab]),
            jnp.pad(bias_own.astype(bf16), ((0, 15), (0, 0))),
        ],
        axis=0,
    )
    group_in = jnp.where(side == half, group_in, swap(group_in, "side")).astype(f32)
    grad_in_own = group_in[:slab].reshape(slab, 3, group_width).transpose(1, 0, 2)
    bias_own = group_in[slab]

    def taken(low, high):
        return small[starts[low] : starts[high]]

    position = 2 * half + core
    return (
        block_out,
        tokens_grad,
        grad_in_own,
        jnp.stack([bias_own[:group_width], bias_own[2 * group_width : qkv_width]]),
        total[:slab, 2 * hidden + stu_width :].T,
        total[:slab, :hidden],
        lax.dynamic_slice_in_dim(taken(6, 7), position * hidden, hidden, 0),
        total[:slab, hidden : 2 * hidden].T,
        taken(0, 2).reshape(2, model),
        taken(2, 6).reshape(4, model),
        total[:slab, 2 * hidden : 2 * hidden + stu_width],
        taken(7, 9).reshape(2, stu_width),
        taken(9, 10),
        taken(11, 12).reshape(stu_width, stu_width),
        taken(12, 13).reshape(stu_width, 16)[:, :class_count],
        taken(10, 11)[:class_count],
    )


def solution(mesh):
    shape = dict(mesh.shape)
    split = Mesh(
        mesh.devices.reshape(shape["shard"], shape["ctx"] // 2, 2, 2, shape["tp"] // 2),
        ("shard", "tree", "side", "half", "core"),
    )
    ctx = ("tree", "side")
    tp = ("half", "core")
    rows = ("shard",) + ctx
    in_specs = (
        P(None, rows, None),
        P(None, rows, None),
        P(None, None, "shard"),
        P(None, rows),
        P(None, "shard", tp),
        P(None, tp),
        P(tp, "shard"),
        P("shard", tp),
        P(tp),
        P(tp, "shard"),
        P(),
        P(),
        P("shard", None),
        P(),
        P(),
        P(),
        P(),
        P(),
    )
    out_specs = (
        P(None, rows, None),
        P(None, rows, None),
        P(None, "shard", tp),
        P(None, tp),
        P(tp, "shard"),
        P("shard", tp),
        P(tp),
        P(tp, "shard"),
        P(),
        P(),
        P("shard", None),
        P(),
        P(),
        P(),
        P(),
        P(),
    )
    return jax.shard_map(body, mesh=split, in_specs=in_specs, out_specs=out_specs, check_vma=False)
```

```python
import functools

import jax
import jax.numpy as jnp
from jax import lax
from jax.experimental import pallas as pl
from jax.experimental.pallas import tpu as pltpu
from jax.sharding import Mesh
from jax.sharding import PartitionSpec as P

HEAD_DIM = 64
POOL_HEADS = 2
TRUNK = 8
BLOCK = 128
PAIR = 2 * BLOCK

NORM_EPSILON = 1e-05
MASK_VALUE = -1e30

f32 = jnp.float32
bf16 = jnp.bfloat16


def swap(value, axis):
    return lax.ppermute(value, axis, [(0, 1), (1, 0)])


def diagonal(value):
    return lax.ppermute(value, ("side", "core"), [(0, 3), (3, 0), (1, 2), (2, 1)])


def ring(value):
    count = lax.axis_size("shard")
    return lax.ppermute(value, "shard", [(i, (i + 1) % count) for i in range(count)])


def over_shards(value, step):
    pairs = [(i, i ^ step) for i in range(lax.axis_size("shard"))]
    return lax.ppermute(value, "shard", pairs)


def after(value, *others):
    return lax.optimization_barrier((value,) + others)[0]


def blank(shape, dtype):
    return pl.pallas_call(
        lambda out: None,
        out_shape=jax.ShapeDtypeStruct(shape, dtype),
        out_specs=pl.BlockSpec(memory_space=pl.ANY),
        name="blank",
    )()


def dot_nn(left, right):
    return lax.dot_general(left, right, (((1,), (0,)), ((), ())), preferred_element_type=f32)


def dot_tn(left, right):
    return lax.dot_general(left, right, (((0,), (0,)), ((), ())), preferred_element_type=f32)


def dot_nt(left, right):
    return lax.dot_general(left, right, (((1,), (1,)), ((), ())), preferred_element_type=f32)


def exact(left, right, dims):
    return lax.dot_general(
        left, right, (dims, ((), ())), precision=lax.Precision.HIGHEST, preferred_element_type=f32
    )


def norm_forward(resid, gain, shift):
    center = resid - jnp.mean(resid, axis=-1, keepdims=True)
    inverse = lax.rsqrt(jnp.mean(center * center, axis=-1, keepdims=True) + NORM_EPSILON)
    normed = center * inverse
    return (normed * gain + shift, normed, inverse)


def norm_backward(grad_out, normed, inverse, gain):
    scaled = grad_out * gain
    grad_in = inverse * (
        scaled
        - jnp.mean(scaled, axis=-1, keepdims=True)
        - normed * jnp.mean(scaled * normed, axis=-1, keepdims=True)
    )
    return (grad_in, jnp.sum(grad_out * normed, axis=0), jnp.sum(grad_out, axis=0))


def block_rows(index):
    return pl.ds(pl.multiple_of(index * BLOCK, BLOCK), BLOCK)


def split_head(head, width, qkv, qs, ks, vs):
    first = head * HEAD_DIM
    qs[...] = qkv[:, first : first + HEAD_DIM] * bf16(HEAD_DIM**-0.5)
    ks[...] = qkv[:, width + first : width + first + HEAD_DIM]
    vs[...] = qkv[:, 2 * width + first : 2 * width + first + HEAD_DIM]


def tile_scores(keys, trunk_keys, queries, rows, masked):
    parts = [dot_nt(trunk_keys, queries)]
    if masked is not None:
        parts.append(dot_nt(keys[rows[0], :], queries[:BLOCK]))
        parts.append(dot_nt(keys[rows[1], :], queries[BLOCK:]))
        parts.append(dot_nt(keys[rows[2], :], queries) + masked)
    return parts


def over_keys(reduce, join, parts):
    result = reduce(parts[0], axis=0, keepdims=True)
    if len(parts) > 1:
        own = [reduce(parts[1], axis=0, keepdims=True), reduce(parts[2], axis=0, keepdims=True)]
        result = join(result, jnp.concatenate(own, axis=1))
        result = join(result, reduce(parts[3], axis=0, keepdims=True))
    return result


def for_parts(row, count):
    return [row, row[:, :BLOCK], row[:, BLOCK:], row][:count]


def tile_softmax(parts):
    tops = for_parts(over_keys(jnp.max, jnp.maximum, parts), len(parts))
    exps = [jnp.exp(part - top) for part, top in zip(parts, tops)]
    return exps, tops[0], over_keys(jnp.sum, jnp.add, exps)


def tile_places(tab, tile, blocks):
    first, second = tab[2 * tile], tab[2 * tile + 1]
    rows = [block_rows(first), block_rows(second), block_rows(tab[blocks + tile])]
    masked = jnp.where(tab[blocks + blocks // 2 + tile] == 2, 0.0, MASK_VALUE).astype(f32)
    return (first, second), rows, masked


def tile_loops(blocks, run):
    def trunk_step(pair, carry):
        run(2 * pair, False)
        run(2 * pair + 1, False)
        return carry

    def step(pair, carry):
        run(2 * pair, True)
        run(2 * pair + 1, True)
        return carry

    lax.fori_loop(0, TRUNK // 4, trunk_step, 0)
    lax.fori_loop(TRUNK // 4, blocks // 4, step, 0)


def place_of(index, part_blocks):
    quarter = index // part_blocks
    return quarter, block_rows(index - quarter * part_blocks)


def attn_fwd_kernel(head, heads, blocks, tab, qkv, before, out, log_sums, *scratch):
    del before
    qs, ks, vs, kt, vtt, result, sem = scratch
    part_blocks = blocks // 4
    split_head(head, heads * HEAD_DIM, qkv, qs, ks, vs)
    for j in range(TRUNK):
        rows = block_rows(tab[j])
        kt[j * BLOCK : (j + 1) * BLOCK, :] = ks[rows, :]
        vtt[:, j * BLOCK : (j + 1) * BLOCK] = vs[rows, :].T

    def run(tile, beside):
        pair, rows, masked = tile_places(tab, tile, blocks)
        queries = jnp.concatenate([qs[rows[0], :], qs[rows[1], :]], axis=0)
        parts = tile_scores(ks, kt[...], queries, rows, masked if beside else None)
        exps, top, total = tile_softmax(parts)
        log_sums[pl.ds(tile, 1), :] = top + jnp.log(total)
        exps = [part.astype(bf16) for part in exps]
        acc = dot_nn(vtt[...], exps[0])
        if beside:
            own = [dot_tn(vs[rows[0], :], exps[1]), dot_tn(vs[rows[1], :], exps[2])]
            acc = acc + jnp.concatenate(own, axis=1) + dot_tn(vs[rows[2], :], exps[3])
        acc = (acc / total).astype(bf16)
        for i in range(2):
            quarter, columns = place_of(pair[i], part_blocks)
            result[quarter, :, columns] = acc[:, i * BLOCK : (i + 1) * BLOCK]

    tile_loops(blocks, run)
    span = pl.ds(head * HEAD_DIM, HEAD_DIM)
    copy = pltpu.make_async_copy(result, out.at[:, span, :], sem)
    copy.start()
    copy.wait()


def attn_bwd_kernel(
    head, heads, blocks, tab, qkv, dot, log_sums, before, out, *scratch
):
    del before
    qs, ks, vs, kt, vt, ktt, dkt, dvt, dka, dva, result, sem = scratch
    part_blocks = blocks // 4
    split_head(head, heads * HEAD_DIM, qkv, qs, ks, vs)
    for j in range(TRUNK):
        rows = block_rows(tab[j])
        span = slice(j * BLOCK, (j + 1) * BLOCK)
        kt[span, :] = ks[rows, :]
        vt[span, :] = vs[rows, :]
        ktt[:, span] = ks[rows, :].T
    dkt[...] = jnp.zeros_like(dkt)
    dvt[...] = jnp.zeros_like(dvt)
    dka[...] = jnp.zeros_like(dka)
    dva[...] = jnp.zeros_like(dva)
    lanes = slice(head * HEAD_DIM, (head + 1) * HEAD_DIM)

    def run(tile, beside):
        pair, rows, masked = tile_places(tab, tile, blocks)
        queries = jnp.concatenate([qs[rows[0], :], qs[rows[1], :]], axis=0)
        places = [place_of(index, part_blocks) for index in pair]
        grads = jnp.concatenate([dot[q, lanes, columns] for q, columns in places], axis=1)
        parts = tile_scores(ks, kt[...], queries, rows, masked if beside else None)
        count = len(parts)
        row_sums = for_parts(log_sums[pl.ds(tile, 1), :], count)
        probs = [jnp.exp(part - row_sum) for part, row_sum in zip(parts, row_sums)]
        grad_parts = [dot_nn(vt[...], grads)]
        if beside:
            grad_parts.append(dot_nn(vs[rows[0], :], grads[:, :BLOCK]))
            grad_parts.append(dot_nn(vs[rows[1], :], grads[:, BLOCK:]))
            grad_parts.append(dot_nn(vs[rows[2], :], grads))
        products = [p * g for p, g in zip(probs, grad_parts)]
        deltas = for_parts(over_keys(jnp.sum, jnp.add, products), count)
        score_grads = [(p * (g - d)).astype(bf16) for p, g, d in zip(probs, grad_parts, deltas)]
        probs = [p.astype(bf16) for p in probs]
        dvt[...] += dot_nt(probs[0], grads)
        dkt[...] += dot_nn(score_grads[0], queries)
        query_grad = dot_nn(ktt[...], score_grads[0])
        if beside:
            dva[rows[0], :] += dot_nt(probs[1], grads[:, :BLOCK])
            dva[rows[1], :] += dot_nt(probs[2], grads[:, BLOCK:])
            dva[rows[2], :] += dot_nt(probs[3], grads)
            dka[rows[0], :] += dot_nn(score_grads[1], queries[:BLOCK])
            dka[rows[1], :] += dot_nn(score_grads[2], queries[BLOCK:])
            dka[rows[2], :] += dot_nn(score_grads[3], queries)
            own = [
                dot_tn(ks[rows[0], :], score_grads[1]),
                dot_tn(ks[rows[1], :], score_grads[2]),
            ]
            query_grad = query_grad + jnp.concatenate(own, axis=1)
            query_grad = query_grad + dot_tn(ks[rows[2], :], score_grads[3])
        query_grad = (query_grad * HEAD_DIM**-0.5).astype(bf16)
        result[0, :, rows[0]] = query_grad[:, :BLOCK]
        result[0, :, rows[1]] = query_grad[:, BLOCK:]

    tile_loops(blocks, run)
    for j in range(TRUNK):
        rows = block_rows(tab[j])
        span = slice(j * BLOCK, (j + 1) * BLOCK)
        dka[rows, :] = dkt[span, :]
        dva[rows, :] = dvt[span, :]
    result[1] = dka[...].T.astype(bf16)
    result[2] = dva[...].T.astype(bf16)
    copies = [
        pltpu.make_async_copy(
            result.at[i], out.at[pl.ds((i * heads + head) * HEAD_DIM, HEAD_DIM), :], sem.at[i]
        )
        for i in range(3)
    ]
    for copy in copies:
        copy.start()
    for copy in copies:
        copy.wait()


def attn_forward(table, qkv, before, head, heads, blocks):
    rows = qkv.shape[0]
    trunk = TRUNK * BLOCK
    return pl.pallas_call(
        functools.partial(attn_fwd_kernel, head, heads, blocks),
        out_shape=(
            jax.ShapeDtypeStruct(before.shape, bf16),
            jax.ShapeDtypeStruct((16, PAIR), f32),
        ),
        in_specs=[
            pl.BlockSpec(memory_space=pltpu.SMEM),
            pl.BlockSpec(memory_space=pltpu.VMEM),
            pl.BlockSpec(memory_space=pl.ANY),
        ],
        out_specs=(
            pl.BlockSpec(memory_space=pl.ANY),
            pl.BlockSpec(memory_space=pltpu.VMEM),
        ),
        input_output_aliases={2: 0},
        scratch_shapes=[pltpu.VMEM((rows, HEAD_DIM), bf16)] * 3
        + [pltpu.VMEM((trunk, HEAD_DIM), bf16), pltpu.VMEM((HEAD_DIM, trunk), bf16)]
        + [pltpu.VMEM((4, HEAD_DIM, rows // 4), bf16), pltpu.SemaphoreType.DMA],
        compiler_params=pltpu.CompilerParams(vmem_limit_bytes=32 << 20),
        cost_estimate=pl.CostEstimate(
            flops=6 * rows * trunk * BLOCK,
            bytes_accessed=8 * rows * HEAD_DIM,
            transcendentals=0,
        ),
        name="tree_attention",
    )(table, qkv, before)


def attn_backward(table, qkv, out_grad, log_sums, before, head, heads, blocks):
    rows = qkv.shape[0]
    trunk = TRUNK * BLOCK
    return pl.pallas_call(
        functools.partial(attn_bwd_kernel, head, heads, blocks),
        out_shape=jax.ShapeDtypeStruct(before.shape, bf16),
        in_specs=[
            pl.BlockSpec(memory_space=pltpu.SMEM),
            pl.BlockSpec(memory_space=pltpu.VMEM),
            pl.BlockSpec(memory_space=pltpu.VMEM),
            pl.BlockSpec(memory_space=pltpu.VMEM),
            pl.BlockSpec(memory_space=pl.ANY),
        ],
        out_specs=pl.BlockSpec(memory_space=pl.ANY),
        input_output_aliases={4: 0},
        scratch_shapes=[pltpu.VMEM((rows, HEAD_DIM), bf16)] * 3
        + [pltpu.VMEM((trunk, HEAD_DIM), bf16)] * 2
        + [pltpu.VMEM((HEAD_DIM, trunk), bf16)]
        + [pltpu.VMEM((trunk, HEAD_DIM), f32)] * 2
        + [pltpu.VMEM((rows, HEAD_DIM), f32)] * 2
        + [pltpu.VMEM((3, HEAD_DIM, rows), bf16), pltpu.SemaphoreType.DMA((3,))],
        compiler_params=pltpu.CompilerParams(vmem_limit_bytes=40 << 20),
        cost_estimate=pl.CostEstimate(
            flops=16 * rows * trunk * BLOCK,
            bytes_accessed=14 * rows * HEAD_DIM,
            transcendentals=0,
        ),
        name="tree_attention_grad",
    )(table, qkv, out_grad, log_sums, before)


def attention_table(path):
    blocks = path.shape[1]
    place = jnp.arange(blocks, dtype=jnp.int32)
    kind = (path[1] != path[0]).astype(jnp.int32) + (path[2] != path[1]).astype(jnp.int32)
    key = kind * 65536 + jnp.where(kind == 2, path[1] * 32, 0) + place
    rank = jnp.sum((key[None, :] < key[:, None]).astype(jnp.int32), axis=1)
    branch = jnp.sum(
        jnp.where((kind[None, :] == 1) & (path[2][None, :] == path[1][:, None]), place[None, :], 0),
        axis=1,
    )
    slot = (rank[None, :] == place[:, None]).astype(jnp.int32)
    columns = jnp.stack([place, jnp.where(kind == 2, branch, 0), kind])
    sorted_columns = jnp.sum(slot[None] * columns[:, None, :], axis=2)
    return jnp.concatenate([sorted_columns[0], sorted_columns[1, ::2], sorted_columns[2, ::2]])


def assemble_kernel(count, spans, flags, *refs):
    pieces, outs = refs[: 2 * count], refs[2 * count :]
    slab = pieces[0].shape[0]
    for j in range(2):
        for k in range(count):
            place = lax.rem(flags[0] + (count - k), count)
            rows = pl.ds(pl.multiple_of(place * slab, 16), slab)
            piece = pieces[j * count + k]
            for out, (lanes, kind) in zip(outs, spans):
                width = lanes.stop - lanes.start
                if kind == 1 or j == 0 and kind == 0:
                    out[rows, j * width : (j + 1) * width] = piece[:, lanes]
                for crossed in range(2 if kind == 2 else 0):

                    @pl.when(flags[1] == crossed)
                    def _():
                        first = (j ^ crossed) * width
                        out[rows, first : first + width] = piece[:, lanes]


def assembled(shard, crossed, own, twin, spans):
    count = len(own)
    rows = count * own[0].shape[0]
    vmem = pl.BlockSpec(memory_space=pltpu.VMEM)
    shapes = [
        jax.ShapeDtypeStruct((rows, (lanes.stop - lanes.start) * (2 if kind else 1)), bf16)
        for lanes, kind in spans
    ]
    return pl.pallas_call(
        functools.partial(assemble_kernel, count, spans),
        out_shape=shapes,
        in_specs=[pl.BlockSpec(memory_space=pltpu.SMEM)] + [vmem] * (2 * count),
        out_specs=[vmem] * len(spans),
        compiler_params=pltpu.CompilerParams(vmem_limit_bytes=24 << 20),
        cost_estimate=pl.CostEstimate(
            flops=0, bytes_accessed=4 * sum(piece.size for piece in own + twin), transcendentals=0
        ),
        name="assembled_weights",
    )(jnp.stack([shard, crossed]).astype(jnp.int32), *own, *twin)


def pack_kernel(count, j, flags, up, down, proj, out, small, *pieces):
    slab = up.shape[0] // count
    group = pieces[0].shape[1] - up.shape[1] - down.shape[1] - proj.shape[1]
    for k in range(count):
        place = lax.rem(flags[0] + (count - k - 1), count)
        rows = pl.ds(pl.multiple_of(place * slab, 16), slab)
        first = 0
        for source in (up, down, proj):
            pieces[k][:slab, first : first + source.shape[1]] = source[rows, :]
            first += source.shape[1]
        for crossed in range(2):

            @pl.when(flags[1] == crossed)
            def _():
                lane = (j ^ crossed) * group
                pieces[k][:slab, first:] = out[rows, lane : lane + group]

        pieces[k][slab:, :] = small[place]


def packed_pieces(shard, crossed, count, up, down, proj, out, small, j):
    rows = up.shape[0] // count + small.shape[1]
    width = small.shape[2]
    vmem = pl.BlockSpec(memory_space=pltpu.VMEM)
    return pl.pallas_call(
        functools.partial(pack_kernel, count, j),
        out_shape=[jax.ShapeDtypeStruct((rows, width), bf16)] * count,
        in_specs=[pl.BlockSpec(memory_space=pltpu.SMEM)] + [vmem] * 5,
        out_specs=[vmem] * count,
        compiler_params=pltpu.CompilerParams(vmem_limit_bytes=24 << 20),
        cost_estimate=pl.CostEstimate(
            flops=0, bytes_accessed=4 * count * rows * width, transcendentals=0
        ),
        name="packed_gradients",
    )(jnp.stack([shard, crossed]).astype(jnp.int32), up, down, proj, out, small)


def place_kernel(start, places, first, second, third, fourth, before, out, wide, sem):
    del before
    rows = first.shape[0]
    half, core = places[0], places[1]
    spots = [(half, core), (1 - half, core), (half, 1 - core), (1 - half, 1 - core)]
    copies = []
    for i, piece in enumerate((first, second, third, fourth)):
        wide[i] = piece[...].astype(wide.dtype)
        row, column = spots[i]
        target = out.at[row, column, pl.ds(start, rows), :]
        copy = pltpu.make_async_copy(wide.at[i], target, sem.at[i])
        copy.start()
        copies.append(copy)
    for copy in copies:
        copy.wait()


def place_rows(places, pieces, before, start):
    rows, width = pieces[0].shape
    vmem = pl.BlockSpec(memory_space=pltpu.VMEM)
    return pl.pallas_call(
        functools.partial(place_kernel, start),
        out_shape=jax.ShapeDtypeStruct(before.shape, before.dtype),
        in_specs=[pl.BlockSpec(memory_space=pltpu.SMEM)]
        + [vmem] * 4
        + [pl.BlockSpec(memory_space=pl.ANY)],
        out_specs=pl.BlockSpec(memory_space=pl.ANY),
        input_output_aliases={5: 0},
        scratch_shapes=[
            pltpu.VMEM((4, rows, width), before.dtype),
            pltpu.SemaphoreType.DMA((4,)),
        ],
        compiler_params=pltpu.CompilerParams(vmem_limit_bytes=24 << 20),
        cost_estimate=pl.CostEstimate(
            flops=0, bytes_accessed=24 * rows * width, transcendentals=0
        ),
        name="placed_rows",
    )(places, *pieces, before)


def student_kernel(part_blocks, labels, rows, weight, shift, query, student, weights, stats):
    width = weight.shape[1]
    pool_dim = width // POOL_HEADS
    value = dot_nn(rows[...], weight[...]) + shift[...]
    student[...] = value
    lane = lax.broadcasted_iota(jnp.int32, (1, width), 1)
    first_head = lane < pool_dim
    product = value * query[...]
    scores = [
        jnp.sum(product[:, e * pool_dim : (e + 1) * pool_dim], axis=1, keepdims=True)
        for e in range(POOL_HEADS)
    ]
    stats[...] = jnp.zeros_like(stats)
    for block in range(part_blocks):
        span = slice(block * BLOCK, (block + 1) * BLOCK)
        peaks = [jnp.max(score[span], axis=0, keepdims=True) for score in scores]
        exps = [jnp.exp(score[span] - peak) for score, peak in zip(scores, peaks)]
        masses = [jnp.sum(part, axis=0, keepdims=True) for part in exps]
        lanes = jnp.where(first_head, exps[0], exps[1])
        weights[span, :] = lanes
        stats[block : block + 1, :width] = jnp.sum(lanes * value[span], axis=0, keepdims=True)
        label = jnp.full((1, width), labels[block], jnp.int32).astype(f32)
        tail = jnp.where(lane == 4, label, 0.0)
        for place, part in enumerate(peaks + masses):
            tail = jnp.where(lane == place, part, tail)
        stats[block : block + 1, width:] = tail


def student_stats(labels, rows, weight, shift, query, part_blocks):
    count = rows.shape[0]
    width = weight.shape[1]
    vmem = pl.BlockSpec(memory_space=pltpu.VMEM)
    return pl.pallas_call(
        functools.partial(student_kernel, part_blocks),
        out_shape=(
            jax.ShapeDtypeStruct((count, width), f32),
            jax.ShapeDtypeStruct((count, width), f32),
            jax.ShapeDtypeStruct((8, 2 * width), f32),
        ),
        in_specs=[pl.BlockSpec(memory_space=pltpu.SMEM)] + [vmem] * 4,
        out_specs=(vmem,) * 3,
        cost_estimate=pl.CostEstimate(
            flops=2 * rows.size * width, bytes_accessed=2 * rows.size, transcendentals=count
        ),
        name="student_stats",
    )(labels, rows, weight, shift, query)


def pool_kernel(
    part_blocks,
    own,
    near,
    across,
    corner,
    member,
    leaf,
    dense,
    head,
    dense_shift,
    cls_shift,
    student,
    weights,
    query,
    student_low,
    grad_dense,
    grad_head,
    vectors,
):
    width = dense.shape[0]
    pool_dim = width // POOL_HEADS
    pool_scale = pool_dim ** (-0.5)
    stats = jnp.concatenate([own[...], near[...], across[...], corner[...]], axis=0)
    moment = stats[:, :width]
    seen = member[...] > 0.0
    is_leaf = leaf[...] > 0.0
    coeffs = []
    pooled = []
    for e in range(POOL_HEADS):
        peak = stats[:, width + e : width + e + 1]
        mass = stats[:, width + POOL_HEADS + e : width + POOL_HEADS + e + 1]
        top = jnp.max(jnp.where(seen, peak, MASK_VALUE), axis=0, keepdims=True)
        factor = jnp.where(seen, jnp.exp(jnp.where(seen, peak - top, MASK_VALUE)), 0.0)
        total = jnp.sum(factor * mass, axis=0, keepdims=True)
        total = jnp.where(total > 0.0, total, 1.0)
        coeff = factor / total
        coeffs.append(coeff)
        lanes = slice(e * pool_dim, (e + 1) * pool_dim)
        pooled.append(exact(coeff, moment[:, lanes], ((0,), (0,))))
    pooled = jnp.concatenate(pooled, axis=1)
    dense_out = jnp.tanh(exact(pooled, dense[...], ((1,), (0,))) + dense_shift[...])
    logits = exact(dense_out, head[...], ((1,), (0,))) + cls_shift[...]
    logits = logits - jnp.max(logits, axis=1, keepdims=True)
    chances = jnp.exp(logits)
    chances = chances / jnp.sum(chances, axis=1, keepdims=True)
    label = stats[:, width + 2 * POOL_HEADS : width + 2 * POOL_HEADS + 1]
    classes = lax.broadcasted_iota(jnp.int32, (1, width), 1).astype(f32)
    onehot = jnp.where(label == classes, 1.0, 0.0)
    grad_logits = jnp.where(is_leaf, chances - onehot, 0.0)
    grad_head[...] = exact(dense_out, grad_logits, ((0,), (0,)))
    grad_pre = exact(grad_logits, head[...], ((1,), (1,))) * (1.0 - dense_out * dense_out)
    grad_dense[...] = exact(pooled, grad_pre, ((0,), (0,)))
    grad_pooled = exact(grad_pre, dense[...], ((1,), (1,)))
    product = grad_pooled * pooled
    spread = []
    offset = []
    for e in range(POOL_HEADS):
        lanes = slice(e * pool_dim, (e + 1) * pool_dim)
        spread.append(exact(coeffs[e], grad_pooled[:, lanes], ((1,), (0,))))
        inner = jnp.sum(product[:, lanes], axis=1, keepdims=True)
        inner = jnp.broadcast_to(inner, (inner.shape[0], pool_dim))
        offset.append(exact(coeffs[e], inner, ((1,), (0,))))
    spread = jnp.concatenate(spread, axis=1)
    offset = jnp.concatenate(offset, axis=1)
    grad_query = jnp.zeros((1, width), f32)
    grad_shift = jnp.zeros((1, width), f32)
    first_head = lax.broadcasted_iota(jnp.int32, (1, width), 1) < pool_dim
    for block in range(part_blocks):
        span = slice(block * BLOCK, (block + 1) * BLOCK)
        value = student[span, :]
        weight = weights[span, :]
        row = spread[block : block + 1]
        product = value * row
        inner = jnp.where(
            first_head,
            jnp.sum(product[:, :pool_dim], axis=1, keepdims=True),
            jnp.sum(product[:, pool_dim:], axis=1, keepdims=True),
        )
        grad_score = weight * (inner - offset[block : block + 1])
        grad_query = grad_query + jnp.sum(grad_score * value, axis=0, keepdims=True)
        low = (weight * row + grad_score * query[...]).astype(bf16)
        student_low[span, :] = low
        grad_shift = grad_shift + jnp.sum(low.astype(f32), axis=0, keepdims=True)
    vectors[0:1, :] = jnp.sum(grad_pre, axis=0, keepdims=True)
    vectors[1:2, :] = jnp.sum(grad_logits, axis=0, keepdims=True)
    vectors[2:3, :] = grad_query * pool_scale
    vectors[3:4, :] = grad_shift
    vectors[4:8, :] = jnp.zeros((4, width), f32)


def pool_classifier(part_blocks, *operands):
    student = operands[-3]
    width = student.shape[1]
    return pl.pallas_call(
        functools.partial(pool_kernel, part_blocks),
        out_shape=(
            jax.ShapeDtypeStruct(student.shape, bf16),
            jax.ShapeDtypeStruct((width, width), f32),
            jax.ShapeDtypeStruct((width, width), f32),
            jax.ShapeDtypeStruct((8, width), f32),
        ),
        cost_estimate=pl.CostEstimate(
            flops=2000 * width * width, bytes_accessed=16 * student.size, transcendentals=0
        ),
        name="pool_classifier",
    )(*operands)


def body(
    tokens,
    cotangent,
    block_path,
    labels,
    w_attn_in,
    attn_bias,
    w_attn_out,
    w_up,
    up_bias,
    w_down,
    norm_gain,
    layer_bias,
    stu_proj,
    stu_bias,
    pool_query,
    stu_dense,
    stu_head,
    class_bias,
):
    row_count, model = tokens.shape[1:]
    own_blocks = labels.shape[1]
    tree_blocks = 2 * own_blocks
    group_width = w_attn_in.shape[2]
    heads = group_width // HEAD_DIM
    slab = w_up.shape[0]
    hidden = w_up.shape[1]
    shards = lax.axis_size("shard")
    trees = lax.axis_size("tree")
    stu_width = stu_proj.shape[1]
    pool_dim = stu_width // POOL_HEADS
    pool_scale = pool_dim ** (-0.5)
    class_count = class_bias.shape[0]
    part_rows = row_count // 2
    part_blocks = own_blocks // 2

    shard = lax.axis_index("shard")
    tree = lax.axis_index("tree")
    side = lax.axis_index("side")
    half = lax.axis_index("half")
    core = lax.axis_index("core")

    shift_rows = layer_bias.astype(f32)
    gain_rows = norm_gain.astype(f32)
    stu_shifts = stu_bias.astype(f32)
    pool_vec = pool_query.astype(f32)

    def by_shard(pieces):
        result = blank((shards,) + pieces[0].shape, pieces[0].dtype)
        for k, piece in enumerate(pieces):
            result = lax.dynamic_update_index_in_dim(result, piece, (shard - k) % shards, 0)
        return result

    def rows_of(array, part):
        place = (half, part * part_rows, 0)
        return lax.dynamic_slice(array, place, (1, part_rows, model))[0]

    own_part = rows_of(tokens, core)
    other_part = swap(own_part, "side")
    other_twin = swap(other_part, "core")
    own_rest = rows_of(after(tokens, own_part), 1 - core)
    tree_rows = jnp.concatenate([own_part, other_part, own_rest, other_twin], axis=0)

    qkv_width = 3 * group_width
    bias_row = jnp.concatenate([attn_bias[0], jnp.zeros((group_width,), bf16), attn_bias[1]])
    up_rows = jnp.pad(up_bias.reshape(2, hidden // 2), ((0, 0), (0, qkv_width - hidden // 2)))
    qkv_message = jnp.concatenate(
        [
            w_attn_in.transpose(1, 0, 2).reshape(slab, qkv_width),
            bias_row[None],
            up_rows,
            jnp.zeros((13, qkv_width), bf16),
        ],
        axis=0,
    )
    qkv_twin = swap(after(qkv_message, own_part), "half")
    twin_bias = qkv_twin[slab + 1 : slab + 3, : hidden // 2].reshape(hidden)
    qkv_message = jnp.where(side == half, qkv_message, qkv_twin)
    qkv_bias = qkv_message[slab].astype(f32)
    qkv_pieces = [qkv_message]
    for k in range(1, shards):
        qkv_pieces.append(ring(after(qkv_pieces[-1], other_part) if k == 3 else qkv_pieces[-1]))
    qkv_weight = by_shard([piece[:slab] for piece in qkv_pieces]).reshape(model, qkv_width)

    stu_lanes = slice(hidden, hidden + stu_width)
    out_lanes = slice(hidden + stu_width, hidden + stu_width + group_width)
    message_one = jnp.concatenate([w_up, stu_proj, w_attn_out.T], axis=1)
    message_two = w_down.T
    own_one = [after(message_one, qkv_pieces[-1], other_twin)]
    own_one.append(ring(own_one[0]))
    twin_one = [swap(after(message_one, qkv_message), "half")]

    paths = lax.dynamic_index_in_dim(block_path, half, 0, keepdims=False)
    paths = lax.dynamic_slice_in_dim(paths, tree * tree_blocks, tree_blocks, 1)
    paths = after(paths, qkv_pieces[1])
    quarters = paths.reshape(3, 2, 2, part_blocks)
    quarters = jnp.where(side == 0, quarters, quarters[:, ::-1])
    quarters = jnp.where(core == 0, quarters, quarters[:, :, ::-1])
    table = attention_table(quarters.swapaxes(1, 2).reshape(3, tree_blocks))

    quarters = jnp.pad(quarters, ((0, 0),) * 3 + ((0, 8 - part_blocks),), constant_values=-1)
    quarters = quarters.reshape(3, 32)
    is_leaf = (quarters[1] != quarters[2]).astype(f32)
    member = jnp.any(quarters[2][:, None, None] == quarters.T[None, :, :], axis=2).astype(f32)
    member = member * is_leaf[None, :]
    leaf_column = is_leaf[:, None]
    lane_pad = stu_width - class_count
    dense_full = stu_dense.astype(f32)
    head_padded = jnp.pad(stu_head.astype(f32), ((0, 0), (0, lane_pad)))
    cls_padded = jnp.pad(
        class_bias.astype(f32)[None, :], ((0, 0), (0, lane_pad)), constant_values=MASK_VALUE
    )
    own_labels = lax.dynamic_slice(labels, (half, core * part_blocks), (1, part_blocks))[0]
    dense_shift = stu_bias[1:2].astype(f32)
    proj_shift = stu_bias[0:1].astype(f32)
    scaled_query = (pool_vec * pool_scale)[None, :]
    prepared = lax.optimization_barrier(
        (
            tree_rows,
            member,
            leaf_column,
            dense_full,
            head_padded,
            cls_padded,
            own_labels,
            dense_shift,
            proj_shift,
            scaled_query,
        )
    )
    tree_rows, member, leaf_column, dense_full, head_padded, cls_padded = prepared[:6]
    own_labels, dense_shift, proj_shift, scaled_query = prepared[6:]

    qkv = (dot_nn(tree_rows, qkv_weight) + qkv_bias).astype(bf16)
    attended = blank((4, group_width, part_rows), bf16)
    attended, sums_0 = attn_forward(table, qkv, attended, 0, heads, tree_blocks)
    twin_two = [swap(after(message_two, twin_one[0]), "half")]
    one = after(own_one[1], attended)
    own_one.append(ring(one))
    twin_one.append(swap(one, "half"))
    attended = after(attended, twin_one[0], twin_two[0])
    attended, sums_1 = attn_forward(table, qkv, attended, 1, heads, tree_blocks)
    one = after(own_one[2], attended)
    own_one.append(ring(one))
    twin_one.append(swap(one, "half"))
    own_two = [after(message_two, attended)]
    own_two.append(ring(own_two[0]))
    attended = after(attended, twin_one[1])
    attended, sums_2 = attn_forward(table, qkv, attended, 2, heads, tree_blocks)
    twin_one.append(swap(after(own_one[3], attended), "half"))
    own_two.append(ring(after(own_two[1], attended)))
    attended = after(attended, twin_one[2], own_two[1])

    def exchange(pieces):
        return [
            pieces[0],
            swap(pieces[1], "core"),
            swap(pieces[2], "side"),
            diagonal(pieces[3]),
        ]

    def at(array, place):
        return lax.dynamic_index_in_dim(array, place, 0, keepdims=False)

    def placed(pieces, places):
        result = blank((len(pieces),) + pieces[0].shape, pieces[0].dtype)
        for piece, place in zip(pieces, places):
            result = lax.dynamic_update_index_in_dim(result, piece, place, 0)
        return result

    quarter_places = [0, 2, 1, 3]
    crossed = jnp.where(side == half, 0, 1)

    def in_quarters(pieces):
        kept, near, across, corner = pieces
        return jnp.stack([kept, across, near, corner])

    crossing = exchange([attended[place] for place in quarter_places])
    own_one[0] = after(own_one[0], *crossing[1:], own_two[2])
    heads_own = in_quarters(crossing)
    heads_own = heads_own.reshape(4 * group_width, part_rows)
    heads_own = after(heads_own, twin_one[3])
    up_weight, stu_weight, out_half = assembled(
        shard,
        crossed,
        own_one,
        twin_one,
        [(slice(0, hidden), 1), (stu_lanes, 0), (out_lanes, 2)],
    )
    twin_two.append(swap(after(own_two[1], up_weight), "half"))
    own_two.append(ring(after(own_two[2], up_weight)))
    out_weight = jnp.concatenate([out_half, swap(out_half, "core")], axis=1)
    out_weight = after(out_weight, twin_two[1], own_two[3])
    twin_two.append(swap(after(own_two[2], out_weight), "half"))
    twin_two.append(swap(after(own_two[3], out_weight), "half"))
    hidden_shift = jnp.concatenate([up_bias, twin_bias]).astype(f32)

    attn = lax.dot_general(
        heads_own, out_weight, (((0,), (1,)), ((), ())), preferred_element_type=f32
    )
    resid_one = own_part.astype(f32) + (attn + shift_rows[0])
    hidden_one, normed_one, inverse_one = norm_forward(resid_one, gain_rows[0], shift_rows[2])
    hidden_low = hidden_one.astype(bf16)
    hidden_low = after(hidden_low, twin_two[2])

    hidden_both = jnp.concatenate([hidden_low, swap(hidden_low, "core")], axis=0)
    pre_act = dot_nn(hidden_both, up_weight) + hidden_shift
    normal_cdf = 0.5 * (1.0 + lax.erf(pre_act * 0.7071067811865476))
    active = (pre_act * normal_cdf).astype(bf16)
    slope = normal_cdf + pre_act * jnp.exp(-0.5 * pre_act * pre_act) * 0.3989422804014327
    own_two[0] = after(own_two[0], active)
    (down_weight,) = assembled(shard, crossed, own_two, twin_two, [(slice(0, hidden), 1)])
    ffn_far = swap(dot_nt(active[part_rows:], down_weight).astype(bf16), "core")
    ffn = dot_nt(active[:part_rows], down_weight) + ffn_far.astype(f32)
    hidden_two, normed_two, inverse_two = norm_forward(
        hidden_one + ffn + shift_rows[1], gain_rows[1], shift_rows[3]
    )
    block_low = hidden_two.astype(bf16)

    def everywhere(rows, other):
        return rows, other, [swap(rows, "core"), swap(other, "core")]

    def placed(result, start, rows, other, twins):
        places = jnp.stack([half, core]).astype(jnp.int32)
        return place_rows(places, [rows, other] + twins, result, start)

    block_other = swap(block_low, "half")

    student, weights, stats = student_stats(
        own_labels, block_low, stu_weight, proj_shift, scaled_query, part_blocks
    )
    student_low, grad_dense, grad_head, pool_vectors = pool_classifier(
        part_blocks,
        *exchange([stats] * 4),
        member,
        leaf_column,
        dense_full,
        head_padded,
        dense_shift,
        cls_padded,
        student,
        weights,
        scaled_query,
    )
    grad_proj = dot_tn(block_low, student_low)

    upstream = lax.dynamic_slice(
        cotangent, (half, core * part_rows, 0), (1, part_rows, model)
    )[0].astype(f32)
    grad_two = upstream + dot_nt(student_low, stu_weight)
    resid_grad_two, gain_grad_two, shift_grad_two = norm_backward(
        grad_two, normed_two, inverse_two, gain_rows[1]
    )
    down_shift_grad = jnp.sum(resid_grad_two, axis=0)
    ffn_low = resid_grad_two.astype(bf16)
    ffn_twin = swap(ffn_low, "core")
    ffn_both = jnp.concatenate([ffn_low, ffn_twin], axis=0)
    pre_low = (dot_nn(ffn_both, down_weight) * slope).astype(bf16)
    grad_hidden_shift = jnp.sum(pre_low.astype(f32), axis=0)
    far_one = swap(dot_nt(pre_low[part_rows:], up_weight).astype(bf16), "core")
    grad_one = resid_grad_two + dot_nt(pre_low[:part_rows], up_weight) + far_one.astype(f32)

    resid_grad_one, gain_grad_one, shift_grad_one = norm_backward(
        grad_one, normed_one, inverse_one, gain_rows[0]
    )
    out_shift_grad = jnp.sum(resid_grad_one, axis=0)
    attn_low = resid_grad_one.astype(bf16)
    block_spread = everywhere(block_low, after(block_other, attn_low))
    heads_grad = lax.dot_general(
        out_weight, attn_low, (((0,), (1,)), ((), ())), preferred_element_type=f32
    ).astype(bf16)
    grad_out = lax.dot_general(
        attn_low, heads_own, (((0,), (1,)), ((), ())), preferred_element_type=f32
    ).astype(bf16)
    heads_grad = heads_grad.reshape(4, group_width, part_rows)
    pieces = [heads_grad[place] for place in quarter_places]
    pieces = lax.optimization_barrier((*pieces, grad_out, ffn_low, ffn_twin, pre_low))
    ffn_low, ffn_twin, pre_low = pieces[5:8]
    ffn_both = jnp.concatenate([ffn_low, ffn_twin], axis=0)
    attended_grad = in_quarters(exchange(pieces[:4]))

    def halves(array):
        return [array[:, :hidden], array[:, hidden:]]

    grad_down = [dot_tn(ffn_both, part).astype(bf16) for part in halves(active)]
    grad_up = [dot_tn(hidden_both, part).astype(bf16) for part in halves(pre_low)]

    up_grad = jnp.zeros((4, hidden), f32)
    for j in range(2):
        up_grad = lax.dynamic_update_slice(
            up_grad,
            grad_hidden_shift[None, j * hidden : (j + 1) * hidden],
            (2 * jnp.where(j == 0, half, 1 - half) + core, 0),
        )
    first = jnp.where((side == 0) & (core == 0), 1.0, 0.0)
    pieces = [
        gain_grad_one,
        gain_grad_two,
        out_shift_grad,
        down_shift_grad,
        shift_grad_one,
        shift_grad_two,
        up_grad.reshape(-1),
        pool_vectors[3],
        pool_vectors[0] * first,
        pool_vectors[2],
        pool_vectors[1] * first,
        (grad_dense * first).reshape(-1),
        (grad_head[:, :16] * first).reshape(-1),
    ]
    sizes = [piece.size for piece in pieces]
    starts = [sum(sizes[:i]) for i in range(len(sizes) + 1)]
    packed = 2 * hidden + stu_width + group_width
    small = jnp.concatenate(pieces)
    small = jnp.pad(small, (0, -small.size % (shards * packed)))
    small_rows = small.size // (shards * packed)
    small = small.reshape(shards, small_rows, packed)
    small = jnp.pad(small, ((0, 0), (0, 16 - small_rows), (0, 0)))
    small = (small + swap(small, "core")).astype(bf16)

    half_out = 2 * group_width
    proj_low = grad_proj.astype(bf16)
    out_sum = grad_out[:, :half_out].astype(f32) + swap(grad_out[:, half_out:], "core").astype(f32)
    out_sum = out_sum.astype(bf16)
    proj_sum = (proj_low.astype(f32) + swap(proj_low, "core").astype(f32)).astype(bf16)
    out_sum = after(out_sum, attended_grad, *block_spread[2])
    kept, sent = [
        packed_pieces(
            shard, crossed, shards, grad_up[j], grad_down[j], proj_sum, out_sum, small, j
        )
        for j in range(2)
    ]

    def reduced(k, got, last):
        total = kept[k].astype(f32) + got.astype(f32)
        if last is not None:
            total = total + last.astype(f32)
        return total.astype(bf16)

    qkv_grad = blank((qkv_width, 4 * part_rows), bf16)
    qkv_grad = after(qkv_grad, *sent)
    got = [swap(sent[0], "half"), swap(sent[1], "half")]
    qkv_grad = attn_backward(
        table, qkv, attended_grad, sums_0, qkv_grad, 0, heads, tree_blocks
    )
    kept = lax.optimization_barrier((qkv_grad, *kept))[1:]
    totals = [reduced(0, got[0], None)]
    passed = ring(totals[0])
    got.append(swap(after(sent[2], totals[0]), "half"))
    qkv_grad = after(qkv_grad, totals[0])
    qkv_grad = attn_backward(
        table, qkv, attended_grad, sums_1, qkv_grad, 1, heads, tree_blocks
    )
    totals.append(reduced(1, after(got[1], qkv_grad), passed))
    passed = ring(totals[1])
    got.append(swap(after(sent[3], totals[1]), "half"))
    qkv_grad = after(qkv_grad, totals[1])
    qkv_grad = attn_backward(
        table, qkv, attended_grad, sums_2, qkv_grad, 2, heads, tree_blocks
    )
    totals.append(reduced(2, after(got[2], qkv_grad), passed))
    passed = ring(totals[2])
    qkv_grad = after(qkv_grad, totals[2])

    def to_rows(columns):
        return lax.dot_general(
            columns, qkv_weight, (((0,), (1,)), ((), ())), preferred_element_type=f32
        ).astype(bf16)

    sent_grad = to_rows(qkv_grad[:, row_count:])
    near_grad = swap(sent_grad, "core")
    kept_grad = to_rows(after(qkv_grad, sent_grad)[:, :row_count])
    far_rows = kept_grad[part_rows:].astype(f32) + near_grad[part_rows:].astype(f32)
    far_rows = far_rows.astype(bf16)
    chunk = part_rows // 2
    spans = [slice(0, chunk), slice(chunk, part_rows)]

    grad_in = lax.dot_general(
        tree_rows, after(qkv_grad, far_rows), (((0,), (1,)), ((), ())), preferred_element_type=f32
    )
    grad_in = grad_in.astype(bf16).reshape(shards, 2, slab // 2, qkv_width)
    kept_in = lax.dynamic_index_in_dim(grad_in, half, 1, keepdims=False)
    sent_in = lax.dynamic_index_in_dim(grad_in, 1 - half, 1, keepdims=False)
    bias_sums = jnp.sum(qkv_grad.astype(f32), axis=1).astype(bf16)
    bias_rows = bias_sums.reshape(shards, 1, qkv_width // shards)
    bias_rows = jnp.pad(bias_rows, ((0, 0), (0, 15), (0, qkv_width - qkv_width // shards)))
    far_first = swap(far_rows[spans[0]], "side")
    sent_in, far_rows, far_first = lax.optimization_barrier(
        (jnp.concatenate([sent_in, bias_rows], axis=1), far_rows, far_first)
    )
    far_second = swap(far_rows[spans[1]], "side")
    got_in = swap(sent_in, "half")
    kept_in = jnp.concatenate([kept_in, bias_rows], axis=1)

    def at_in(k):
        place = (shard - k) % shards
        return at(kept_in, place).astype(f32) + at(got_in, place).astype(f32)

    def tokens_part(i, far):
        near = kept_grad[:part_rows][spans[i]].astype(f32)
        near = near + near_grad[:part_rows][spans[i]].astype(f32)
        return (resid_grad_one[spans[i]] + near + far.astype(f32)).astype(bf16)

    tokens_grad = blank((2, 2, part_rows, model), f32)
    total = reduced(3, got[3], passed)
    got_in, far_second, total = lax.optimization_barrier((got_in, far_second, total))
    chip_in = (kept_in.astype(f32) + got_in.astype(f32)).astype(bf16)
    rows_low, rows_high = [tokens_part(i, far) for i, far in enumerate((far_first, far_second))]
    rows_all = jnp.concatenate([rows_low, rows_high], axis=0)
    chip_in, rows_all, total = lax.optimization_barrier((chip_in, rows_all, total))
    other_all = swap(rows_all, "half")
    total_far = swap(total, "side")
    parts_in = [at(chip_in, shard)]
    for k in range(1, shards):
        pairs = [(i, (i + k) % shards) for i in range(shards)]
        sent_part = at(chip_in, (shard + k) % shards)
        parts_in.append(lax.ppermute(sent_part, "shard", pairs))
    block_out = placed(
        blank((2, 2, part_rows, model), bf16), 0, after(block_low, rows_all), *block_spread[1:]
    )
    gathered = lax.optimization_barrier(
        (other_all, total_far, *parts_in, rows_all, total, block_out)
    )
    other_all, total_far, parts_in = gathered[0], gathered[1], gathered[2 : 2 + shards]
    rows_all, total, block_out = gathered[2 + shards :]
    block_out = block_out.reshape(2, row_count, model)
    part = sum(piece.astype(f32) for piece in parts_in)
    total = total.astype(f32) + total_far.astype(f32)
    if trees > 1:
        total = lax.psum(total, "tree")
        part = lax.psum(part, "tree")
    part = part.astype(bf16)
    half_slab = slab // 2
    part_twin = swap(part[:half_slab], "half")
    twins = [swap(rows_all, "core"), swap(other_all, "core")]
    bias_part = jnp.pad(part[half_slab : half_slab + 1], ((0, 0), (0, packed - qkv_width)))
    small = jnp.concatenate([total[slab : slab + small_rows], bias_part.astype(f32)], axis=0)
    small = jnp.pad(small, ((0, 16 - small.shape[0]), (0, 0))).astype(bf16)[None]

    def joined(own, other, bit):
        low = (shard // bit) % 2 == 0
        return jnp.concatenate([jnp.where(low, own, other), jnp.where(low, other, own)], axis=0)

    small_other = over_shards(small, 1)
    part_twin, twins[0], twins[1], part, small, small_other = lax.optimization_barrier(
        (part_twin, *twins, part, small, small_other)
    )
    small = joined(small, small_other, 1)
    step = 2
    while step < shards:
        small = joined(small, over_shards(small, step), step)
        step *= 2
    tokens_grad = placed(tokens_grad, 0, rows_all, other_all, twins)
    tokens_grad = tokens_grad.reshape(2, row_count, model)
    small = small.astype(f32)
    bias_own = small[:, small_rows, : qkv_width // shards].reshape(1, qkv_width)
    small = small[:, :small_rows].reshape(-1)

    group_in = jnp.concatenate(
        [
            jnp.where(half == 0, part[:half_slab], part_twin),
            jnp.where(half == 0, part_twin, part[:half_slab]),
            jnp.pad(bias_own.astype(bf16), ((0, 15), (0, 0))),
        ],
        axis=0,
    )
    group_in = jnp.where(side == half, group_in, swap(group_in, "side")).astype(f32)
    grad_in_own = group_in[:slab].reshape(slab, 3, group_width).transpose(1, 0, 2)
    bias_own = group_in[slab]

    def taken(low, high):
        return small[starts[low] : starts[high]]

    position = 2 * half + core
    return (
        block_out,
        tokens_grad,
        grad_in_own,
        jnp.stack([bias_own[:group_width], bias_own[2 * group_width : qkv_width]]),
        total[:slab, 2 * hidden + stu_width :].T,
        total[:slab, :hidden],
        lax.dynamic_slice_in_dim(taken(6, 7), position * hidden, hidden, 0),
        total[:slab, hidden : 2 * hidden].T,
        taken(0, 2).reshape(2, model),
        taken(2, 6).reshape(4, model),
        total[:slab, 2 * hidden : 2 * hidden + stu_width],
        taken(7, 9).reshape(2, stu_width),
        taken(9, 10),
        taken(11, 12).reshape(stu_width, stu_width),
        taken(12, 13).reshape(stu_width, 16)[:, :class_count],
        taken(10, 11)[:class_count],
    )


def solution(mesh):
    shape = dict(mesh.shape)
    split = Mesh(
        mesh.devices.reshape(shape["shard"], shape["ctx"] // 2, 2, 2, shape["tp"] // 2),
        ("shard", "tree", "side", "half", "core"),
    )
    ctx = ("tree", "side")
    tp = ("half", "core")
    rows = ("shard",) + ctx
    in_specs = (
        P(None, rows, None),
        P(None, rows, None),
        P(None, None, "shard"),
        P(None, rows),
        P(None, "shard", tp),
        P(None, tp),
        P(tp, "shard"),
        P("shard", tp),
        P(tp),
        P(tp, "shard"),
        P(),
        P(),
        P("shard", None),
        P(),
        P(),
        P(),
        P(),
        P(),
    )
    out_specs = (
        P(None, rows, None),
        P(None, rows, None),
        P(None, "shard", tp),
        P(None, tp),
        P(tp, "shard"),
        P("shard", tp),
        P(tp),
        P(tp, "shard"),
        P(),
        P(),
        P("shard", None),
        P(),
        P(),
        P(),
        P(),
        P(),
    )
    return jax.shard_map(body, mesh=split, in_specs=in_specs, out_specs=out_specs, check_vma=False)
```

```python
import functools

import jax
import jax.numpy as jnp
from jax import lax
from jax.experimental import pallas as pl
from jax.experimental.pallas import tpu as pltpu
from jax.sharding import Mesh
from jax.sharding import PartitionSpec as P

HEAD_DIM = 64
POOL_HEADS = 2
TRUNK = 8
BLOCK = 128
PAIR = 2 * BLOCK

NORM_EPSILON = 1e-05
MASK_VALUE = -1e30

f32 = jnp.float32
bf16 = jnp.bfloat16


def swap(value, axis):
    return lax.ppermute(value, axis, [(0, 1), (1, 0)])


def diagonal(value):
    return lax.ppermute(value, ("side", "core"), [(0, 3), (3, 0), (1, 2), (2, 1)])


def ring(value):
    count = lax.axis_size("shard")
    return lax.ppermute(value, "shard", [(i, (i + 1) % count) for i in range(count)])


def over_shards(value, step):
    pairs = [(i, i ^ step) for i in range(lax.axis_size("shard"))]
    return lax.ppermute(value, "shard", pairs)


def after(value, *others):
    return lax.optimization_barrier((value,) + others)[0]


def blank(shape, dtype):
    return pl.pallas_call(
        lambda out: None,
        out_shape=jax.ShapeDtypeStruct(shape, dtype),
        out_specs=pl.BlockSpec(memory_space=pl.ANY),
        name="blank",
    )()


def dot_nn(left, right):
    return lax.dot_general(left, right, (((1,), (0,)), ((), ())), preferred_element_type=f32)


def dot_tn(left, right):
    return lax.dot_general(left, right, (((0,), (0,)), ((), ())), preferred_element_type=f32)


def dot_nt(left, right):
    return lax.dot_general(left, right, (((1,), (1,)), ((), ())), preferred_element_type=f32)


def exact(left, right, dims):
    return lax.dot_general(
        left, right, (dims, ((), ())), precision=lax.Precision.HIGHEST, preferred_element_type=f32
    )


def norm_forward(resid, gain, shift):
    center = resid - jnp.mean(resid, axis=-1, keepdims=True)
    inverse = lax.rsqrt(jnp.mean(center * center, axis=-1, keepdims=True) + NORM_EPSILON)
    normed = center * inverse
    return (normed * gain + shift, normed, inverse)


def norm_backward(grad_out, normed, inverse, gain):
    scaled = grad_out * gain
    grad_in = inverse * (
        scaled
        - jnp.mean(scaled, axis=-1, keepdims=True)
        - normed * jnp.mean(scaled * normed, axis=-1, keepdims=True)
    )
    return (grad_in, jnp.sum(grad_out * normed, axis=0), jnp.sum(grad_out, axis=0))


def block_rows(index):
    return pl.ds(pl.multiple_of(index * BLOCK, BLOCK), BLOCK)


def split_head(head, width, qkv, qs, ks, vs):
    first = head * HEAD_DIM
    qs[...] = qkv[:, first : first + HEAD_DIM] * bf16(HEAD_DIM**-0.5)
    ks[...] = qkv[:, width + first : width + first + HEAD_DIM]
    vs[...] = qkv[:, 2 * width + first : 2 * width + first + HEAD_DIM]


def tile_scores(keys, trunk_keys, queries, rows, masked):
    parts = [dot_nt(trunk_keys, queries)]
    if masked is not None:
        parts.append(dot_nt(keys[rows[0], :], queries[:BLOCK]))
        parts.append(dot_nt(keys[rows[1], :], queries[BLOCK:]))
        parts.append(dot_nt(keys[rows[2], :], queries) + masked)
    return parts


def over_keys(reduce, join, parts):
    result = reduce(parts[0], axis=0, keepdims=True)
    if len(parts) > 1:
        own = [reduce(parts[1], axis=0, keepdims=True), reduce(parts[2], axis=0, keepdims=True)]
        result = join(result, jnp.concatenate(own, axis=1))
        result = join(result, reduce(parts[3], axis=0, keepdims=True))
    return result


def for_parts(row, count):
    return [row, row[:, :BLOCK], row[:, BLOCK:], row][:count]


def tile_softmax(parts):
    tops = for_parts(over_keys(jnp.max, jnp.maximum, parts), len(parts))
    exps = [jnp.exp(part - top) for part, top in zip(parts, tops)]
    return exps, tops[0], over_keys(jnp.sum, jnp.add, exps)


def tile_places(tab, tile, blocks):
    first, second = tab[2 * tile], tab[2 * tile + 1]
    rows = [block_rows(first), block_rows(second), block_rows(tab[blocks + tile])]
    masked = jnp.where(tab[blocks + blocks // 2 + tile] == 2, 0.0, MASK_VALUE).astype(f32)
    return (first, second), rows, masked


def tile_loops(blocks, run):
    def trunk_step(pair, carry):
        run(2 * pair, False)
        run(2 * pair + 1, False)
        return carry

    def step(pair, carry):
        run(2 * pair, True)
        run(2 * pair + 1, True)
        return carry

    lax.fori_loop(0, TRUNK // 4, trunk_step, 0)
    lax.fori_loop(TRUNK // 4, blocks // 4, step, 0)


def place_of(index, part_blocks):
    quarter = index // part_blocks
    return quarter, block_rows(index - quarter * part_blocks)


def attn_fwd_kernel(head, heads, blocks, tab, qkv, before, out, log_sums, *scratch):
    del before
    qs, ks, vs, kt, vtt, result, sem = scratch
    part_blocks = blocks // 4
    split_head(head, heads * HEAD_DIM, qkv, qs, ks, vs)
    for j in range(TRUNK):
        rows = block_rows(tab[j])
        kt[j * BLOCK : (j + 1) * BLOCK, :] = ks[rows, :]
        vtt[:, j * BLOCK : (j + 1) * BLOCK] = vs[rows, :].T

    def run(tile, beside):
        pair, rows, masked = tile_places(tab, tile, blocks)
        queries = jnp.concatenate([qs[rows[0], :], qs[rows[1], :]], axis=0)
        parts = tile_scores(ks, kt[...], queries, rows, masked if beside else None)
        exps, top, total = tile_softmax(parts)
        log_sums[pl.ds(tile, 1), :] = top + jnp.log(total)
        exps = [part.astype(bf16) for part in exps]
        acc = dot_nn(vtt[...], exps[0])
        if beside:
            own = [dot_tn(vs[rows[0], :], exps[1]), dot_tn(vs[rows[1], :], exps[2])]
            acc = acc + jnp.concatenate(own, axis=1) + dot_tn(vs[rows[2], :], exps[3])
        acc = (acc / total).astype(bf16)
        for i in range(2):
            quarter, columns = place_of(pair[i], part_blocks)
            result[quarter, :, columns] = acc[:, i * BLOCK : (i + 1) * BLOCK]

    tile_loops(blocks, run)
    span = pl.ds(head * HEAD_DIM, HEAD_DIM)
    copy = pltpu.make_async_copy(result, out.at[:, span, :], sem)
    copy.start()
    copy.wait()


def attn_bwd_kernel(
    head, heads, blocks, tab, qkv, dot, log_sums, before, out, *scratch
):
    del before
    qs, ks, vs, kt, vt, ktt, dkt, dvt, dka, dva, result, sem = scratch
    part_blocks = blocks // 4
    split_head(head, heads * HEAD_DIM, qkv, qs, ks, vs)
    for j in range(TRUNK):
        rows = block_rows(tab[j])
        span = slice(j * BLOCK, (j + 1) * BLOCK)
        kt[span, :] = ks[rows, :]
        vt[span, :] = vs[rows, :]
        ktt[:, span] = ks[rows, :].T
    dkt[...] = jnp.zeros_like(dkt)
    dvt[...] = jnp.zeros_like(dvt)
    dka[...] = jnp.zeros_like(dka)
    dva[...] = jnp.zeros_like(dva)
    lanes = slice(head * HEAD_DIM, (head + 1) * HEAD_DIM)

    def run(tile, beside):
        pair, rows, masked = tile_places(tab, tile, blocks)
        queries = jnp.concatenate([qs[rows[0], :], qs[rows[1], :]], axis=0)
        places = [place_of(index, part_blocks) for index in pair]
        grads = jnp.concatenate([dot[q, lanes, columns] for q, columns in places], axis=1)
        parts = tile_scores(ks, kt[...], queries, rows, masked if beside else None)
        count = len(parts)
        row_sums = for_parts(log_sums[pl.ds(tile, 1), :], count)
        probs = [jnp.exp(part - row_sum) for part, row_sum in zip(parts, row_sums)]
        grad_parts = [dot_nn(vt[...], grads)]
        if beside:
            grad_parts.append(dot_nn(vs[rows[0], :], grads[:, :BLOCK]))
            grad_parts.append(dot_nn(vs[rows[1], :], grads[:, BLOCK:]))
            grad_parts.append(dot_nn(vs[rows[2], :], grads))
        products = [p * g for p, g in zip(probs, grad_parts)]
        deltas = for_parts(over_keys(jnp.sum, jnp.add, products), count)
        score_grads = [(p * (g - d)).astype(bf16) for p, g, d in zip(probs, grad_parts, deltas)]
        probs = [p.astype(bf16) for p in probs]
        dvt[...] += dot_nt(probs[0], grads)
        dkt[...] += dot_nn(score_grads[0], queries)
        query_grad = dot_nn(ktt[...], score_grads[0])
        if beside:
            dva[rows[0], :] += dot_nt(probs[1], grads[:, :BLOCK])
            dva[rows[1], :] += dot_nt(probs[2], grads[:, BLOCK:])
            dva[rows[2], :] += dot_nt(probs[3], grads)
            dka[rows[0], :] += dot_nn(score_grads[1], queries[:BLOCK])
            dka[rows[1], :] += dot_nn(score_grads[2], queries[BLOCK:])
            dka[rows[2], :] += dot_nn(score_grads[3], queries)
            own = [
                dot_tn(ks[rows[0], :], score_grads[1]),
                dot_tn(ks[rows[1], :], score_grads[2]),
            ]
            query_grad = query_grad + jnp.concatenate(own, axis=1)
            query_grad = query_grad + dot_tn(ks[rows[2], :], score_grads[3])
        query_grad = (query_grad * HEAD_DIM**-0.5).astype(bf16)
        result[0, :, rows[0]] = query_grad[:, :BLOCK]
        result[0, :, rows[1]] = query_grad[:, BLOCK:]

    tile_loops(blocks, run)
    for j in range(TRUNK):
        rows = block_rows(tab[j])
        span = slice(j * BLOCK, (j + 1) * BLOCK)
        dka[rows, :] = dkt[span, :]
        dva[rows, :] = dvt[span, :]
    result[1] = dka[...].T.astype(bf16)
    result[2] = dva[...].T.astype(bf16)
    copies = [
        pltpu.make_async_copy(
            result.at[i], out.at[pl.ds((i * heads + head) * HEAD_DIM, HEAD_DIM), :], sem.at[i]
        )
        for i in range(3)
    ]
    for copy in copies:
        copy.start()
    for copy in copies:
        copy.wait()


def attn_forward(table, qkv, before, head, heads, blocks):
    rows = qkv.shape[0]
    trunk = TRUNK * BLOCK
    return pl.pallas_call(
        functools.partial(attn_fwd_kernel, head, heads, blocks),
        out_shape=(
            jax.ShapeDtypeStruct(before.shape, bf16),
            jax.ShapeDtypeStruct((16, PAIR), f32),
        ),
        in_specs=[
            pl.BlockSpec(memory_space=pltpu.SMEM),
            pl.BlockSpec(memory_space=pltpu.VMEM),
            pl.BlockSpec(memory_space=pl.ANY),
        ],
        out_specs=(
            pl.BlockSpec(memory_space=pl.ANY),
            pl.BlockSpec(memory_space=pltpu.VMEM),
        ),
        input_output_aliases={2: 0},
        scratch_shapes=[pltpu.VMEM((rows, HEAD_DIM), bf16)] * 3
        + [pltpu.VMEM((trunk, HEAD_DIM), bf16), pltpu.VMEM((HEAD_DIM, trunk), bf16)]
        + [pltpu.VMEM((4, HEAD_DIM, rows // 4), bf16), pltpu.SemaphoreType.DMA],
        compiler_params=pltpu.CompilerParams(vmem_limit_bytes=32 << 20),
        cost_estimate=pl.CostEstimate(
            flops=6 * rows * trunk * BLOCK,
            bytes_accessed=8 * rows * HEAD_DIM,
            transcendentals=0,
        ),
        name="tree_attention",
    )(table, qkv, before)


def attn_backward(table, qkv, out_grad, log_sums, before, head, heads, blocks):
    rows = qkv.shape[0]
    trunk = TRUNK * BLOCK
    return pl.pallas_call(
        functools.partial(attn_bwd_kernel, head, heads, blocks),
        out_shape=jax.ShapeDtypeStruct(before.shape, bf16),
        in_specs=[
            pl.BlockSpec(memory_space=pltpu.SMEM),
            pl.BlockSpec(memory_space=pltpu.VMEM),
            pl.BlockSpec(memory_space=pltpu.VMEM),
            pl.BlockSpec(memory_space=pltpu.VMEM),
            pl.BlockSpec(memory_space=pl.ANY),
        ],
        out_specs=pl.BlockSpec(memory_space=pl.ANY),
        input_output_aliases={4: 0},
        scratch_shapes=[pltpu.VMEM((rows, HEAD_DIM), bf16)] * 3
        + [pltpu.VMEM((trunk, HEAD_DIM), bf16)] * 2
        + [pltpu.VMEM((HEAD_DIM, trunk), bf16)]
        + [pltpu.VMEM((trunk, HEAD_DIM), f32)] * 2
        + [pltpu.VMEM((rows, HEAD_DIM), f32)] * 2
        + [pltpu.VMEM((3, HEAD_DIM, rows), bf16), pltpu.SemaphoreType.DMA((3,))],
        compiler_params=pltpu.CompilerParams(vmem_limit_bytes=40 << 20),
        cost_estimate=pl.CostEstimate(
            flops=16 * rows * trunk * BLOCK,
            bytes_accessed=14 * rows * HEAD_DIM,
            transcendentals=0,
        ),
        name="tree_attention_grad",
    )(table, qkv, out_grad, log_sums, before)


def attention_table(path):
    blocks = path.shape[1]
    place = jnp.arange(blocks, dtype=jnp.int32)
    kind = (path[1] != path[0]).astype(jnp.int32) + (path[2] != path[1]).astype(jnp.int32)
    key = kind * 65536 + jnp.where(kind == 2, path[1] * 32, 0) + place
    rank = jnp.sum((key[None, :] < key[:, None]).astype(jnp.int32), axis=1)
    branch = jnp.sum(
        jnp.where((kind[None, :] == 1) & (path[2][None, :] == path[1][:, None]), place[None, :], 0),
        axis=1,
    )
    slot = (rank[None, :] == place[:, None]).astype(jnp.int32)
    columns = jnp.stack([place, jnp.where(kind == 2, branch, 0), kind])
    sorted_columns = jnp.sum(slot[None] * columns[:, None, :], axis=2)
    return jnp.concatenate([sorted_columns[0], sorted_columns[1, ::2], sorted_columns[2, ::2]])


def assemble_kernel(count, spans, flags, *refs):
    pieces, outs = refs[: 2 * count], refs[2 * count :]
    slab = pieces[0].shape[0]
    for j in range(2):
        for k in range(count):
            place = lax.rem(flags[0] + (count - k), count)
            rows = pl.ds(pl.multiple_of(place * slab, 16), slab)
            piece = pieces[j * count + k]
            for out, (lanes, kind) in zip(outs, spans):
                width = lanes.stop - lanes.start
                if kind == 1 or j == 0 and kind == 0:
                    out[rows, j * width : (j + 1) * width] = piece[:, lanes]
                for crossed in range(2 if kind == 2 else 0):

                    @pl.when(flags[1] == crossed)
                    def _():
                        first = (j ^ crossed) * width
                        out[rows, first : first + width] = piece[:, lanes]


def assembled(shard, crossed, own, twin, spans):
    count = len(own)
    rows = count * own[0].shape[0]
    vmem = pl.BlockSpec(memory_space=pltpu.VMEM)
    shapes = [
        jax.ShapeDtypeStruct((rows, (lanes.stop - lanes.start) * (2 if kind else 1)), bf16)
        for lanes, kind in spans
    ]
    return pl.pallas_call(
        functools.partial(assemble_kernel, count, spans),
        out_shape=shapes,
        in_specs=[pl.BlockSpec(memory_space=pltpu.SMEM)] + [vmem] * (2 * count),
        out_specs=[vmem] * len(spans),
        compiler_params=pltpu.CompilerParams(vmem_limit_bytes=24 << 20),
        cost_estimate=pl.CostEstimate(
            flops=0, bytes_accessed=4 * sum(piece.size for piece in own + twin), transcendentals=0
        ),
        name="assembled_weights",
    )(jnp.stack([shard, crossed]).astype(jnp.int32), *own, *twin)


def pack_kernel(count, j, flags, up, down, proj, out, small, *pieces):
    slab = up.shape[0] // count
    group = pieces[0].shape[1] - up.shape[1] - down.shape[1] - proj.shape[1]
    for k in range(count):
        place = lax.rem(flags[0] + (count - k - 1), count)
        rows = pl.ds(pl.multiple_of(place * slab, 16), slab)
        first = 0
        for source in (up, down, proj):
            pieces[k][:slab, first : first + source.shape[1]] = source[rows, :]
            first += source.shape[1]
        for crossed in range(2):

            @pl.when(flags[1] == crossed)
            def _():
                lane = (j ^ crossed) * group
                pieces[k][:slab, first:] = out[rows, lane : lane + group]

        pieces[k][slab:, :] = small[place]


def packed_pieces(shard, crossed, count, up, down, proj, out, small, j):
    rows = up.shape[0] // count + small.shape[1]
    width = small.shape[2]
    vmem = pl.BlockSpec(memory_space=pltpu.VMEM)
    return pl.pallas_call(
        functools.partial(pack_kernel, count, j),
        out_shape=[jax.ShapeDtypeStruct((rows, width), bf16)] * count,
        in_specs=[pl.BlockSpec(memory_space=pltpu.SMEM)] + [vmem] * 5,
        out_specs=[vmem] * count,
        compiler_params=pltpu.CompilerParams(vmem_limit_bytes=24 << 20),
        cost_estimate=pl.CostEstimate(
            flops=0, bytes_accessed=4 * count * rows * width, transcendentals=0
        ),
        name="packed_gradients",
    )(jnp.stack([shard, crossed]).astype(jnp.int32), up, down, proj, out, small)


def place_kernel(start, places, first, second, third, fourth, before, out, wide, sem):
    del before
    rows = first.shape[0]
    half, core = places[0], places[1]
    spots = [(half, core), (1 - half, core), (half, 1 - core), (1 - half, 1 - core)]
    copies = []
    for i, piece in enumerate((first, second, third, fourth)):
        wide[i] = piece[...].astype(wide.dtype)
        row, column = spots[i]
        target = out.at[row, column, pl.ds(start, rows), :]
        copy = pltpu.make_async_copy(wide.at[i], target, sem.at[i])
        copy.start()
        copies.append(copy)
    for copy in copies:
        copy.wait()


def place_rows(places, pieces, before, start):
    rows, width = pieces[0].shape
    vmem = pl.BlockSpec(memory_space=pltpu.VMEM)
    return pl.pallas_call(
        functools.partial(place_kernel, start),
        out_shape=jax.ShapeDtypeStruct(before.shape, before.dtype),
        in_specs=[pl.BlockSpec(memory_space=pltpu.SMEM)]
        + [vmem] * 4
        + [pl.BlockSpec(memory_space=pl.ANY)],
        out_specs=pl.BlockSpec(memory_space=pl.ANY),
        input_output_aliases={5: 0},
        scratch_shapes=[
            pltpu.VMEM((4, rows, width), before.dtype),
            pltpu.SemaphoreType.DMA((4,)),
        ],
        compiler_params=pltpu.CompilerParams(vmem_limit_bytes=24 << 20),
        cost_estimate=pl.CostEstimate(
            flops=0, bytes_accessed=24 * rows * width, transcendentals=0
        ),
        name="placed_rows",
    )(places, *pieces, before)


def student_kernel(part_blocks, labels, rows, weight, shift, query, student, weights, stats):
    width = weight.shape[1]
    pool_dim = width // POOL_HEADS
    value = dot_nn(rows[...], weight[...]) + shift[...]
    student[...] = value
    lane = lax.broadcasted_iota(jnp.int32, (1, width), 1)
    first_head = lane < pool_dim
    product = value * query[...]
    scores = [
        jnp.sum(product[:, e * pool_dim : (e + 1) * pool_dim], axis=1, keepdims=True)
        for e in range(POOL_HEADS)
    ]
    stats[...] = jnp.zeros_like(stats)
    for block in range(part_blocks):
        span = slice(block * BLOCK, (block + 1) * BLOCK)
        peaks = [jnp.max(score[span], axis=0, keepdims=True) for score in scores]
        exps = [jnp.exp(score[span] - peak) for score, peak in zip(scores, peaks)]
        masses = [jnp.sum(part, axis=0, keepdims=True) for part in exps]
        lanes = jnp.where(first_head, exps[0], exps[1])
        weights[span, :] = lanes
        stats[block : block + 1, :width] = jnp.sum(lanes * value[span], axis=0, keepdims=True)
        label = jnp.full((1, width), labels[block], jnp.int32).astype(f32)
        tail = jnp.where(lane == 4, label, 0.0)
        for place, part in enumerate(peaks + masses):
            tail = jnp.where(lane == place, part, tail)
        stats[block : block + 1, width:] = tail


def student_stats(labels, rows, weight, shift, query, part_blocks):
    count = rows.shape[0]
    width = weight.shape[1]
    vmem = pl.BlockSpec(memory_space=pltpu.VMEM)
    return pl.pallas_call(
        functools.partial(student_kernel, part_blocks),
        out_shape=(
            jax.ShapeDtypeStruct((count, width), f32),
            jax.ShapeDtypeStruct((count, width), f32),
            jax.ShapeDtypeStruct((8, 2 * width), f32),
        ),
        in_specs=[pl.BlockSpec(memory_space=pltpu.SMEM)] + [vmem] * 4,
        out_specs=(vmem,) * 3,
        cost_estimate=pl.CostEstimate(
            flops=2 * rows.size * width, bytes_accessed=2 * rows.size, transcendentals=count
        ),
        name="student_stats",
    )(labels, rows, weight, shift, query)


def pool_kernel(
    part_blocks,
    own,
    near,
    across,
    corner,
    member,
    leaf,
    dense,
    head,
    dense_shift,
    cls_shift,
    student,
    weights,
    query,
    student_low,
    grad_dense,
    grad_head,
    vectors,
):
    width = dense.shape[0]
    pool_dim = width // POOL_HEADS
    pool_scale = pool_dim ** (-0.5)
    stats = jnp.concatenate([own[...], near[...], across[...], corner[...]], axis=0)
    moment = stats[:, :width]
    seen = member[...] > 0.0
    is_leaf = leaf[...] > 0.0
    coeffs = []
    pooled = []
    for e in range(POOL_HEADS):
        peak = stats[:, width + e : width + e + 1]
        mass = stats[:, width + POOL_HEADS + e : width + POOL_HEADS + e + 1]
        top = jnp.max(jnp.where(seen, peak, MASK_VALUE), axis=0, keepdims=True)
        factor = jnp.where(seen, jnp.exp(jnp.where(seen, peak - top, MASK_VALUE)), 0.0)
        total = jnp.sum(factor * mass, axis=0, keepdims=True)
        total = jnp.where(total > 0.0, total, 1.0)
        coeff = factor / total
        coeffs.append(coeff)
        lanes = slice(e * pool_dim, (e + 1) * pool_dim)
        pooled.append(exact(coeff, moment[:, lanes], ((0,), (0,))))
    pooled = jnp.concatenate(pooled, axis=1)
    dense_out = jnp.tanh(exact(pooled, dense[...], ((1,), (0,))) + dense_shift[...])
    logits = exact(dense_out, head[...], ((1,), (0,))) + cls_shift[...]
    logits = logits - jnp.max(logits, axis=1, keepdims=True)
    chances = jnp.exp(logits)
    chances = chances / jnp.sum(chances, axis=1, keepdims=True)
    label = stats[:, width + 2 * POOL_HEADS : width + 2 * POOL_HEADS + 1]
    classes = lax.broadcasted_iota(jnp.int32, (1, width), 1).astype(f32)
    onehot = jnp.where(label == classes, 1.0, 0.0)
    grad_logits = jnp.where(is_leaf, chances - onehot, 0.0)
    grad_head[...] = exact(dense_out, grad_logits, ((0,), (0,)))
    grad_pre = exact(grad_logits, head[...], ((1,), (1,))) * (1.0 - dense_out * dense_out)
    grad_dense[...] = exact(pooled, grad_pre, ((0,), (0,)))
    grad_pooled = exact(grad_pre, dense[...], ((1,), (1,)))
    product = grad_pooled * pooled
    spread = []
    offset = []
    for e in range(POOL_HEADS):
        lanes = slice(e * pool_dim, (e + 1) * pool_dim)
        spread.append(exact(coeffs[e], grad_pooled[:, lanes], ((1,), (0,))))
        inner = jnp.sum(product[:, lanes], axis=1, keepdims=True)
        inner = jnp.broadcast_to(inner, (inner.shape[0], pool_dim))
        offset.append(exact(coeffs[e], inner, ((1,), (0,))))
    spread = jnp.concatenate(spread, axis=1)
    offset = jnp.concatenate(offset, axis=1)
    grad_query = jnp.zeros((1, width), f32)
    grad_shift = jnp.zeros((1, width), f32)
    first_head = lax.broadcasted_iota(jnp.int32, (1, width), 1) < pool_dim
    for block in range(part_blocks):
        span = slice(block * BLOCK, (block + 1) * BLOCK)
        value = student[span, :]
        weight = weights[span, :]
        row = spread[block : block + 1]
        product = value * row
        inner = jnp.where(
            first_head,
            jnp.sum(product[:, :pool_dim], axis=1, keepdims=True),
            jnp.sum(product[:, pool_dim:], axis=1, keepdims=True),
        )
        grad_score = weight * (inner - offset[block : block + 1])
        grad_query = grad_query + jnp.sum(grad_score * value, axis=0, keepdims=True)
        low = (weight * row + grad_score * query[...]).astype(bf16)
        student_low[span, :] = low
        grad_shift = grad_shift + jnp.sum(low.astype(f32), axis=0, keepdims=True)
    vectors[0:1, :] = jnp.sum(grad_pre, axis=0, keepdims=True)
    vectors[1:2, :] = jnp.sum(grad_logits, axis=0, keepdims=True)
    vectors[2:3, :] = grad_query * pool_scale
    vectors[3:4, :] = grad_shift
    vectors[4:8, :] = jnp.zeros((4, width), f32)


def pool_classifier(part_blocks, *operands):
    student = operands[-3]
    width = student.shape[1]
    return pl.pallas_call(
        functools.partial(pool_kernel, part_blocks),
        out_shape=(
            jax.ShapeDtypeStruct(student.shape, bf16),
            jax.ShapeDtypeStruct((width, width), f32),
            jax.ShapeDtypeStruct((width, width), f32),
            jax.ShapeDtypeStruct((8, width), f32),
        ),
        cost_estimate=pl.CostEstimate(
            flops=2000 * width * width, bytes_accessed=16 * student.size, transcendentals=0
        ),
        name="pool_classifier",
    )(*operands)


def body(
    tokens,
    cotangent,
    block_path,
    labels,
    w_attn_in,
    attn_bias,
    w_attn_out,
    w_up,
    up_bias,
    w_down,
    norm_gain,
    layer_bias,
    stu_proj,
    stu_bias,
    pool_query,
    stu_dense,
    stu_head,
    class_bias,
):
    row_count, model = tokens.shape[1:]
    own_blocks = labels.shape[1]
    tree_blocks = 2 * own_blocks
    group_width = w_attn_in.shape[2]
    heads = group_width // HEAD_DIM
    slab = w_up.shape[0]
    hidden = w_up.shape[1]
    shards = lax.axis_size("shard")
    trees = lax.axis_size("tree")
    stu_width = stu_proj.shape[1]
    pool_dim = stu_width // POOL_HEADS
    pool_scale = pool_dim ** (-0.5)
    class_count = class_bias.shape[0]
    part_rows = row_count // 2
    part_blocks = own_blocks // 2

    shard = lax.axis_index("shard")
    tree = lax.axis_index("tree")
    side = lax.axis_index("side")
    half = lax.axis_index("half")
    core = lax.axis_index("core")

    shift_rows = layer_bias.astype(f32)
    gain_rows = norm_gain.astype(f32)
    stu_shifts = stu_bias.astype(f32)
    pool_vec = pool_query.astype(f32)

    def by_shard(pieces):
        result = blank((shards,) + pieces[0].shape, pieces[0].dtype)
        for k, piece in enumerate(pieces):
            result = lax.dynamic_update_index_in_dim(result, piece, (shard - k) % shards, 0)
        return result

    def rows_of(array, part):
        place = (half, part * part_rows, 0)
        return lax.dynamic_slice(array, place, (1, part_rows, model))[0]

    own_part = rows_of(tokens, core)
    other_part = swap(own_part, "side")
    own_rest = rows_of(after(tokens, own_part), 1 - core)

    qkv_width = 3 * group_width
    bias_row = jnp.concatenate([attn_bias[0], jnp.zeros((group_width,), bf16), attn_bias[1]])
    up_rows = jnp.pad(up_bias.reshape(2, hidden // 2), ((0, 0), (0, qkv_width - hidden // 2)))
    qkv_message = jnp.concatenate(
        [
            w_attn_in.transpose(1, 0, 2).reshape(slab, qkv_width),
            bias_row[None],
            up_rows,
            jnp.zeros((13, qkv_width), bf16),
        ],
        axis=0,
    )
    qkv_twin = swap(after(qkv_message, own_part), "half")
    twin_bias = qkv_twin[slab + 1 : slab + 3, : hidden // 2].reshape(hidden)
    qkv_message = jnp.where(side == half, qkv_message, qkv_twin)
    qkv_bias = qkv_message[slab].astype(f32)
    qkv_pieces = [qkv_message]
    for k in range(1, shards):
        qkv_pieces.append(ring(qkv_pieces[-1]))
    other_twin = swap(after(other_part, qkv_pieces[2]), "core")
    tree_rows = jnp.concatenate([own_part, other_part, own_rest, other_twin], axis=0)
    qkv_weight = by_shard([piece[:slab] for piece in qkv_pieces]).reshape(model, qkv_width)

    stu_lanes = slice(hidden, hidden + stu_width)
    out_lanes = slice(hidden + stu_width, hidden + stu_width + group_width)
    message_one = jnp.concatenate([w_up, stu_proj, w_attn_out.T], axis=1)
    message_two = w_down.T
    own_one = [after(message_one, qkv_pieces[-1], other_twin)]
    own_one.append(ring(own_one[0]))
    twin_one = [swap(after(message_one, qkv_message), "half")]

    paths = lax.dynamic_index_in_dim(block_path, half, 0, keepdims=False)
    paths = lax.dynamic_slice_in_dim(paths, tree * tree_blocks, tree_blocks, 1)
    paths = after(paths, qkv_pieces[1])
    quarters = paths.reshape(3, 2, 2, part_blocks)
    quarters = jnp.where(side == 0, quarters, quarters[:, ::-1])
    quarters = jnp.where(core == 0, quarters, quarters[:, :, ::-1])
    table = attention_table(quarters.swapaxes(1, 2).reshape(3, tree_blocks))

    quarters = jnp.pad(quarters, ((0, 0),) * 3 + ((0, 8 - part_blocks),), constant_values=-1)
    quarters = quarters.reshape(3, 32)
    is_leaf = (quarters[1] != quarters[2]).astype(f32)
    member = jnp.any(quarters[2][:, None, None] == quarters.T[None, :, :], axis=2).astype(f32)
    member = member * is_leaf[None, :]
    leaf_column = is_leaf[:, None]
    lane_pad = stu_width - class_count
    dense_full = stu_dense.astype(f32)
    head_padded = jnp.pad(stu_head.astype(f32), ((0, 0), (0, lane_pad)))
    cls_padded = jnp.pad(
        class_bias.astype(f32)[None, :], ((0, 0), (0, lane_pad)), constant_values=MASK_VALUE
    )
    own_labels = lax.dynamic_slice(labels, (half, core * part_blocks), (1, part_blocks))[0]
    dense_shift = stu_bias[1:2].astype(f32)
    proj_shift = stu_bias[0:1].astype(f32)
    scaled_query = (pool_vec * pool_scale)[None, :]
    prepared = lax.optimization_barrier(
        (
            tree_rows,
            member,
            leaf_column,
            dense_full,
            head_padded,
            cls_padded,
            own_labels,
            dense_shift,
            proj_shift,
            scaled_query,
        )
    )
    tree_rows, member, leaf_column, dense_full, head_padded, cls_padded = prepared[:6]
    own_labels, dense_shift, proj_shift, scaled_query = prepared[6:]

    qkv = (dot_nn(tree_rows, qkv_weight) + qkv_bias).astype(bf16)
    attended = blank((4, group_width, part_rows), bf16)
    attended, sums_0 = attn_forward(table, qkv, attended, 0, heads, tree_blocks)
    twin_two = [swap(after(message_two, twin_one[0]), "half")]
    one = after(own_one[1], attended)
    own_one.append(ring(one))
    twin_one.append(swap(one, "half"))
    attended = after(attended, twin_one[0], twin_two[0])
    attended, sums_1 = attn_forward(table, qkv, attended, 1, heads, tree_blocks)
    one = after(own_one[2], attended)
    own_one.append(ring(one))
    twin_one.append(swap(one, "half"))
    attended = after(attended, twin_one[1])
    attended, sums_2 = attn_forward(table, qkv, attended, 2, heads, tree_blocks)
    twin_one.append(swap(after(own_one[3], attended), "half"))
    own_two = [after(message_two, attended)]
    own_two.append(ring(own_two[0]))
    attended = after(attended, twin_one[2])

    def exchange(pieces):
        return [
            pieces[0],
            swap(pieces[1], "core"),
            swap(pieces[2], "side"),
            diagonal(pieces[3]),
        ]

    def at(array, place):
        return lax.dynamic_index_in_dim(array, place, 0, keepdims=False)

    def placed(pieces, places):
        result = blank((len(pieces),) + pieces[0].shape, pieces[0].dtype)
        for piece, place in zip(pieces, places):
            result = lax.dynamic_update_index_in_dim(result, piece, place, 0)
        return result

    quarter_places = [0, 2, 1, 3]
    crossed = jnp.where(side == half, 0, 1)

    def in_quarters(pieces):
        kept, near, across, corner = pieces
        return jnp.stack([kept, across, near, corner])

    crossing = exchange([attended[place] for place in quarter_places])
    own_two.append(ring(after(own_two[1], crossing[1])))
    own_one[0] = after(own_one[0], *crossing[1:], own_two[2])
    heads_own = in_quarters(crossing)
    heads_own = heads_own.reshape(4 * group_width, part_rows)
    heads_own = after(heads_own, twin_one[3])
    up_weight, stu_weight, out_half = assembled(
        shard,
        crossed,
        own_one,
        twin_one,
        [(slice(0, hidden), 1), (stu_lanes, 0), (out_lanes, 2)],
    )
    twin_two.append(swap(after(own_two[1], up_weight), "half"))
    own_two.append(ring(after(own_two[2], up_weight)))
    out_weight = jnp.concatenate([out_half, swap(out_half, "core")], axis=1)
    twin_two.append(swap(after(own_two[2], up_weight), "half"))
    out_weight = after(out_weight, twin_two[1], twin_two[2], own_two[3])
    twin_two.append(swap(after(own_two[3], out_weight), "half"))
    hidden_shift = jnp.concatenate([up_bias, twin_bias]).astype(f32)

    attn = lax.dot_general(
        heads_own, out_weight, (((0,), (1,)), ((), ())), preferred_element_type=f32
    )
    resid_one = own_part.astype(f32) + (attn + shift_rows[0])
    hidden_one, normed_one, inverse_one = norm_forward(resid_one, gain_rows[0], shift_rows[2])
    hidden_low = hidden_one.astype(bf16)

    hidden_both = jnp.concatenate([hidden_low, swap(hidden_low, "core")], axis=0)
    pre_act = dot_nn(hidden_both, up_weight) + hidden_shift
    normal_cdf = 0.5 * (1.0 + lax.erf(pre_act * 0.7071067811865476))
    active = (pre_act * normal_cdf).astype(bf16)
    slope = normal_cdf + pre_act * jnp.exp(-0.5 * pre_act * pre_act) * 0.3989422804014327
    own_two[0] = after(own_two[0], active)
    (down_weight,) = assembled(shard, crossed, own_two, twin_two, [(slice(0, hidden), 1)])
    ffn_far = swap(dot_nt(active[part_rows:], down_weight).astype(bf16), "core")
    ffn = dot_nt(active[:part_rows], down_weight) + ffn_far.astype(f32)
    hidden_two, normed_two, inverse_two = norm_forward(
        hidden_one + ffn + shift_rows[1], gain_rows[1], shift_rows[3]
    )
    block_low = hidden_two.astype(bf16)

    def everywhere(rows, other):
        return rows, other, [swap(rows, "core"), swap(other, "core")]

    def placed(result, start, rows, other, twins):
        places = jnp.stack([half, core]).astype(jnp.int32)
        return place_rows(places, [rows, other] + twins, result, start)

    block_other = swap(block_low, "half")

    student, weights, stats = student_stats(
        own_labels, block_low, stu_weight, proj_shift, scaled_query, part_blocks
    )
    student_low, grad_dense, grad_head, pool_vectors = pool_classifier(
        part_blocks,
        *exchange([stats] * 4),
        member,
        leaf_column,
        dense_full,
        head_padded,
        dense_shift,
        cls_padded,
        student,
        weights,
        scaled_query,
    )
    grad_proj = dot_tn(block_low, student_low)

    upstream = lax.dynamic_slice(
        cotangent, (half, core * part_rows, 0), (1, part_rows, model)
    )[0].astype(f32)
    grad_two = upstream + dot_nt(student_low, stu_weight)
    resid_grad_two, gain_grad_two, shift_grad_two = norm_backward(
        grad_two, normed_two, inverse_two, gain_rows[1]
    )
    down_shift_grad = jnp.sum(resid_grad_two, axis=0)
    ffn_low = resid_grad_two.astype(bf16)
    ffn_twin = swap(ffn_low, "core")
    ffn_both = jnp.concatenate([ffn_low, ffn_twin], axis=0)
    pre_low = (dot_nn(ffn_both, down_weight) * slope).astype(bf16)
    grad_hidden_shift = jnp.sum(pre_low.astype(f32), axis=0)
    far_one = swap(dot_nt(pre_low[part_rows:], up_weight).astype(bf16), "core")
    grad_one = resid_grad_two + dot_nt(pre_low[:part_rows], up_weight) + far_one.astype(f32)

    resid_grad_one, gain_grad_one, shift_grad_one = norm_backward(
        grad_one, normed_one, inverse_one, gain_rows[0]
    )
    out_shift_grad = jnp.sum(resid_grad_one, axis=0)
    attn_low = resid_grad_one.astype(bf16)
    block_twin = swap(block_low, "core")
    heads_grad = lax.dot_general(
        out_weight, attn_low, (((0,), (1,)), ((), ())), preferred_element_type=f32
    ).astype(bf16)
    grad_out = lax.dot_general(
        attn_low, heads_own, (((0,), (1,)), ((), ())), preferred_element_type=f32
    ).astype(bf16)
    heads_grad = heads_grad.reshape(4, group_width, part_rows)
    pieces = [heads_grad[place] for place in quarter_places]
    pieces = lax.optimization_barrier(
        (*pieces, grad_out, ffn_low, ffn_twin, pre_low, block_twin)
    )
    ffn_low, ffn_twin, pre_low, block_twin = pieces[5:]
    ffn_both = jnp.concatenate([ffn_low, ffn_twin], axis=0)
    attended_grad = in_quarters(exchange(pieces[:4]))

    def halves(array):
        return [array[:, :hidden], array[:, hidden:]]

    grad_down = [dot_tn(ffn_both, part).astype(bf16) for part in halves(active)]
    grad_up = [dot_tn(hidden_both, part).astype(bf16) for part in halves(pre_low)]

    up_grad = jnp.zeros((4, hidden), f32)
    for j in range(2):
        up_grad = lax.dynamic_update_slice(
            up_grad,
            grad_hidden_shift[None, j * hidden : (j + 1) * hidden],
            (2 * jnp.where(j == 0, half, 1 - half) + core, 0),
        )
    first = jnp.where((side == 0) & (core == 0), 1.0, 0.0)
    pieces = [
        gain_grad_one,
        gain_grad_two,
        out_shift_grad,
        down_shift_grad,
        shift_grad_one,
        shift_grad_two,
        up_grad.reshape(-1),
        pool_vectors[3],
        pool_vectors[0] * first,
        pool_vectors[2],
        pool_vectors[1] * first,
        (grad_dense * first).reshape(-1),
        (grad_head[:, :16] * first).reshape(-1),
    ]
    sizes = [piece.size for piece in pieces]
    starts = [sum(sizes[:i]) for i in range(len(sizes) + 1)]
    packed = 2 * hidden + stu_width + group_width
    small = jnp.concatenate(pieces)
    small = jnp.pad(small, (0, -small.size % (shards * packed)))
    small_rows = small.size // (shards * packed)
    small = small.reshape(shards, small_rows, packed)
    small = jnp.pad(small, ((0, 0), (0, 16 - small_rows), (0, 0)))
    small = (small + swap(small, "core")).astype(bf16)

    half_out = 2 * group_width
    proj_low = grad_proj.astype(bf16)
    out_sum = grad_out[:, :half_out].astype(f32) + swap(grad_out[:, half_out:], "core").astype(f32)
    out_sum = out_sum.astype(bf16)
    proj_sum = (proj_low.astype(f32) + swap(proj_low, "core").astype(f32)).astype(bf16)
    out_sum = after(out_sum, attended_grad, block_other)
    block_far = swap(after(block_other, out_sum), "core")
    kept, sent = [
        packed_pieces(
            shard, crossed, shards, grad_up[j], grad_down[j], proj_sum, out_sum, small, j
        )
        for j in range(2)
    ]

    def reduced(k, got, last):
        total = kept[k].astype(f32) + got.astype(f32)
        if last is not None:
            total = total + last.astype(f32)
        return total.astype(bf16)

    qkv_grad = blank((qkv_width, 4 * part_rows), bf16)
    qkv_grad = after(qkv_grad, *sent)
    got = [swap(sent[0], "half"), swap(sent[1], "half")]
    qkv_grad = attn_backward(
        table, qkv, attended_grad, sums_0, qkv_grad, 0, heads, tree_blocks
    )
    kept = lax.optimization_barrier((qkv_grad, *kept))[1:]
    totals = [reduced(0, got[0], None)]
    passed = ring(totals[0])
    got.append(swap(after(sent[2], totals[0]), "half"))
    qkv_grad = after(qkv_grad, totals[0])
    qkv_grad = attn_backward(
        table, qkv, attended_grad, sums_1, qkv_grad, 1, heads, tree_blocks
    )
    totals.append(reduced(1, after(got[1], qkv_grad), passed))
    passed = ring(totals[1])
    got.append(swap(after(sent[3], totals[1]), "half"))
    qkv_grad = after(qkv_grad, totals[1])
    qkv_grad = attn_backward(
        table, qkv, attended_grad, sums_2, qkv_grad, 2, heads, tree_blocks
    )
    totals.append(reduced(2, after(got[2], qkv_grad), passed))
    passed = ring(totals[2])
    qkv_grad = after(qkv_grad, totals[2])

    def to_rows(columns):
        return lax.dot_general(
            columns, qkv_weight, (((0,), (1,)), ((), ())), preferred_element_type=f32
        ).astype(bf16)

    sent_grad = to_rows(qkv_grad[:, row_count:])
    near_grad = swap(sent_grad, "core")
    kept_grad = to_rows(after(qkv_grad, sent_grad)[:, :row_count])
    far_rows = kept_grad[part_rows:].astype(f32) + near_grad[part_rows:].astype(f32)
    far_rows = far_rows.astype(bf16)
    chunk = part_rows // 2
    spans = [slice(0, chunk), slice(chunk, part_rows)]

    grad_in = lax.dot_general(
        tree_rows, after(qkv_grad, far_rows), (((0,), (1,)), ((), ())), preferred_element_type=f32
    )
    grad_in = grad_in.astype(bf16).reshape(shards, 2, slab // 2, qkv_width)
    kept_in = lax.dynamic_index_in_dim(grad_in, half, 1, keepdims=False)
    sent_in = lax.dynamic_index_in_dim(grad_in, 1 - half, 1, keepdims=False)
    bias_sums = jnp.sum(qkv_grad.astype(f32), axis=1).astype(bf16)
    bias_rows = bias_sums.reshape(shards, 1, qkv_width // shards)
    bias_rows = jnp.pad(bias_rows, ((0, 0), (0, 15), (0, qkv_width - qkv_width // shards)))
    far_first = swap(far_rows[spans[0]], "side")
    sent_in, far_rows, far_first = lax.optimization_barrier(
        (jnp.concatenate([sent_in, bias_rows], axis=1), far_rows, far_first)
    )
    far_second = swap(far_rows[spans[1]], "side")
    got_in = swap(sent_in, "half")
    kept_in = jnp.concatenate([kept_in, bias_rows], axis=1)

    def at_in(k):
        place = (shard - k) % shards
        return at(kept_in, place).astype(f32) + at(got_in, place).astype(f32)

    def tokens_part(i, far):
        near = kept_grad[:part_rows][spans[i]].astype(f32)
        near = near + near_grad[:part_rows][spans[i]].astype(f32)
        return (resid_grad_one[spans[i]] + near + far.astype(f32)).astype(bf16)

    tokens_grad = blank((2, 2, part_rows, model), f32)
    total = reduced(3, got[3], passed)
    got_in, far_second, total = lax.optimization_barrier((got_in, far_second, total))
    chip_in = (kept_in.astype(f32) + got_in.astype(f32)).astype(bf16)
    rows_low, rows_high = [tokens_part(i, far) for i, far in enumerate((far_first, far_second))]
    rows_all = jnp.concatenate([rows_low, rows_high], axis=0)
    chip_in, rows_all, total = lax.optimization_barrier((chip_in, rows_all, total))
    other_all = swap(rows_all, "half")
    total_far = swap(total, "side")
    parts_in = [at(chip_in, shard)]
    for k in range(1, shards):
        pairs = [(i, (i + k) % shards) for i in range(shards)]
        sent_part = at(chip_in, (shard + k) % shards)
        parts_in.append(lax.ppermute(sent_part, "shard", pairs))
    block_out = placed(
        blank((2, 2, part_rows, model), bf16), 0, after(block_low, rows_all), block_other, [block_twin, block_far]
    )
    gathered = lax.optimization_barrier(
        (other_all, total_far, *parts_in, rows_all, total, block_out)
    )
    other_all, total_far, parts_in = gathered[0], gathered[1], gathered[2 : 2 + shards]
    rows_all, total, block_out = gathered[2 + shards :]
    block_out = block_out.reshape(2, row_count, model)
    part = sum(piece.astype(f32) for piece in parts_in)
    total = total.astype(f32) + total_far.astype(f32)
    if trees > 1:
        total = lax.psum(total, "tree")
        part = lax.psum(part, "tree")
    part = part.astype(bf16)
    half_slab = slab // 2
    part_twin = swap(part[:half_slab], "half")
    twins = [swap(rows_all, "core"), swap(other_all, "core")]
    bias_part = jnp.pad(part[half_slab : half_slab + 1], ((0, 0), (0, packed - qkv_width)))
    small = jnp.concatenate([total[slab : slab + small_rows], bias_part.astype(f32)], axis=0)
    small = jnp.pad(small, ((0, 16 - small.shape[0]), (0, 0))).astype(bf16)[None]

    def joined(own, other, bit):
        low = (shard // bit) % 2 == 0
        return jnp.concatenate([jnp.where(low, own, other), jnp.where(low, other, own)], axis=0)

    small_other = over_shards(small, 1)
    part_twin, twins[0], twins[1], part, small, small_other = lax.optimization_barrier(
        (part_twin, *twins, part, small, small_other)
    )
    small = joined(small, small_other, 1)
    step = 2
    while step < shards:
        small = joined(small, over_shards(small, step), step)
        step *= 2
    tokens_grad = placed(tokens_grad, 0, rows_all, other_all, twins)
    tokens_grad = tokens_grad.reshape(2, row_count, model)
    small = small.astype(f32)
    bias_own = small[:, small_rows, : qkv_width // shards].reshape(1, qkv_width)
    small = small[:, :small_rows].reshape(-1)

    group_in = jnp.concatenate(
        [
            jnp.where(half == 0, part[:half_slab], part_twin),
            jnp.where(half == 0, part_twin, part[:half_slab]),
            jnp.pad(bias_own.astype(bf16), ((0, 15), (0, 0))),
        ],
        axis=0,
    )
    group_in = jnp.where(side == half, group_in, swap(group_in, "side")).astype(f32)
    grad_in_own = group_in[:slab].reshape(slab, 3, group_width).transpose(1, 0, 2)
    bias_own = group_in[slab]

    def taken(low, high):
        return small[starts[low] : starts[high]]

    position = 2 * half + core
    return (
        block_out,
        tokens_grad,
        grad_in_own,
        jnp.stack([bias_own[:group_width], bias_own[2 * group_width : qkv_width]]),
        total[:slab, 2 * hidden + stu_width :].T,
        total[:slab, :hidden],
        lax.dynamic_slice_in_dim(taken(6, 7), position * hidden, hidden, 0),
        total[:slab, hidden : 2 * hidden].T,
        taken(0, 2).reshape(2, model),
        taken(2, 6).reshape(4, model),
        total[:slab, 2 * hidden : 2 * hidden + stu_width],
        taken(7, 9).reshape(2, stu_width),
        taken(9, 10),
        taken(11, 12).reshape(stu_width, stu_width),
        taken(12, 13).reshape(stu_width, 16)[:, :class_count],
        taken(10, 11)[:class_count],
    )


def solution(mesh):
    shape = dict(mesh.shape)
    split = Mesh(
        mesh.devices.reshape(shape["shard"], shape["ctx"] // 2, 2, 2, shape["tp"] // 2),
        ("shard", "tree", "side", "half", "core"),
    )
    ctx = ("tree", "side")
    tp = ("half", "core")
    rows = ("shard",) + ctx
    in_specs = (
        P(None, rows, None),
        P(None, rows, None),
        P(None, None, "shard"),
        P(None, rows),
        P(None, "shard", tp),
        P(None, tp),
        P(tp, "shard"),
        P("shard", tp),
        P(tp),
        P(tp, "shard"),
        P(),
        P(),
        P("shard", None),
        P(),
        P(),
        P(),
        P(),
        P(),
    )
    out_specs = (
        P(None, rows, None),
        P(None, rows, None),
        P(None, "shard", tp),
        P(None, tp),
        P(tp, "shard"),
        P("shard", tp),
        P(tp),
        P(tp, "shard"),
        P(),
        P(),
        P("shard", None),
        P(),
        P(),
        P(),
        P(),
        P(),
    )
    return jax.shard_map(body, mesh=split, in_specs=in_specs, out_specs=out_specs, check_vma=False)
```

```python
import functools

import jax
import jax.numpy as jnp
from jax import lax
from jax.experimental import pallas as pl
from jax.experimental.pallas import tpu as pltpu
from jax.sharding import Mesh
from jax.sharding import PartitionSpec as P

HEAD_DIM = 64
POOL_HEADS = 2
TRUNK = 8
BLOCK = 128
PAIR = 2 * BLOCK

NORM_EPSILON = 1e-05
MASK_VALUE = -1e30

f32 = jnp.float32
bf16 = jnp.bfloat16


def swap(value, axis):
    return lax.ppermute(value, axis, [(0, 1), (1, 0)])


def diagonal(value):
    return lax.ppermute(value, ("side", "core"), [(0, 3), (3, 0), (1, 2), (2, 1)])


def ring(value):
    count = lax.axis_size("shard")
    return lax.ppermute(value, "shard", [(i, (i + 1) % count) for i in range(count)])


def over_shards(value, step):
    pairs = [(i, i ^ step) for i in range(lax.axis_size("shard"))]
    return lax.ppermute(value, "shard", pairs)


def after(value, *others):
    return lax.optimization_barrier((value,) + others)[0]


def blank(shape, dtype):
    return pl.pallas_call(
        lambda out: None,
        out_shape=jax.ShapeDtypeStruct(shape, dtype),
        out_specs=pl.BlockSpec(memory_space=pl.ANY),
        name="blank",
    )()


def dot_nn(left, right):
    return lax.dot_general(left, right, (((1,), (0,)), ((), ())), preferred_element_type=f32)


def dot_tn(left, right):
    return lax.dot_general(left, right, (((0,), (0,)), ((), ())), preferred_element_type=f32)


def dot_nt(left, right):
    return lax.dot_general(left, right, (((1,), (1,)), ((), ())), preferred_element_type=f32)


def exact(left, right, dims):
    return lax.dot_general(
        left, right, (dims, ((), ())), precision=lax.Precision.HIGHEST, preferred_element_type=f32
    )


def norm_forward(resid, gain, shift):
    center = resid - jnp.mean(resid, axis=-1, keepdims=True)
    inverse = lax.rsqrt(jnp.mean(center * center, axis=-1, keepdims=True) + NORM_EPSILON)
    normed = center * inverse
    return (normed * gain + shift, normed, inverse)


def norm_backward(grad_out, normed, inverse, gain):
    scaled = grad_out * gain
    grad_in = inverse * (
        scaled
        - jnp.mean(scaled, axis=-1, keepdims=True)
        - normed * jnp.mean(scaled * normed, axis=-1, keepdims=True)
    )
    return (grad_in, jnp.sum(grad_out * normed, axis=0), jnp.sum(grad_out, axis=0))


def block_rows(index):
    return pl.ds(pl.multiple_of(index * BLOCK, BLOCK), BLOCK)


def split_head(head, width, qkv, qs, ks, vs):
    first = head * HEAD_DIM
    qs[...] = qkv[:, first : first + HEAD_DIM] * bf16(HEAD_DIM**-0.5)
    ks[...] = qkv[:, width + first : width + first + HEAD_DIM]
    vs[...] = qkv[:, 2 * width + first : 2 * width + first + HEAD_DIM]


def tile_scores(keys, trunk_keys, queries, rows, masked):
    parts = [dot_nt(trunk_keys, queries)]
    if masked is not None:
        parts.append(dot_nt(keys[rows[0], :], queries[:BLOCK]))
        parts.append(dot_nt(keys[rows[1], :], queries[BLOCK:]))
        parts.append(dot_nt(keys[rows[2], :], queries) + masked)
    return parts


def over_keys(reduce, join, parts):
    result = reduce(parts[0], axis=0, keepdims=True)
    if len(parts) > 1:
        own = [reduce(parts[1], axis=0, keepdims=True), reduce(parts[2], axis=0, keepdims=True)]
        result = join(result, jnp.concatenate(own, axis=1))
        result = join(result, reduce(parts[3], axis=0, keepdims=True))
    return result


def for_parts(row, count):
    return [row, row[:, :BLOCK], row[:, BLOCK:], row][:count]


def tile_softmax(parts):
    tops = for_parts(over_keys(jnp.max, jnp.maximum, parts), len(parts))
    exps = [jnp.exp(part - top) for part, top in zip(parts, tops)]
    return exps, tops[0], over_keys(jnp.sum, jnp.add, exps)


def tile_places(tab, tile, blocks):
    first, second = tab[2 * tile], tab[2 * tile + 1]
    rows = [block_rows(first), block_rows(second), block_rows(tab[blocks + tile])]
    masked = jnp.where(tab[blocks + blocks // 2 + tile] == 2, 0.0, MASK_VALUE).astype(f32)
    return (first, second), rows, masked


def tile_loops(blocks, run):
    def trunk_step(pair, carry):
        run(2 * pair, False)
        run(2 * pair + 1, False)
        return carry

    def step(pair, carry):
        run(2 * pair, True)
        run(2 * pair + 1, True)
        return carry

    lax.fori_loop(0, TRUNK // 4, trunk_step, 0)
    lax.fori_loop(TRUNK // 4, blocks // 4, step, 0)


def place_of(index, part_blocks):
    quarter = index // part_blocks
    return quarter, block_rows(index - quarter * part_blocks)


def attn_fwd_kernel(head, heads, blocks, tab, qkv, before, out, log_sums, *scratch):
    del before
    qs, ks, vs, kt, vtt, result, sem = scratch
    part_blocks = blocks // 4
    split_head(head, heads * HEAD_DIM, qkv, qs, ks, vs)
    for j in range(TRUNK):
        rows = block_rows(tab[j])
        kt[j * BLOCK : (j + 1) * BLOCK, :] = ks[rows, :]
        vtt[:, j * BLOCK : (j + 1) * BLOCK] = vs[rows, :].T

    def run(tile, beside):
        pair, rows, masked = tile_places(tab, tile, blocks)
        queries = jnp.concatenate([qs[rows[0], :], qs[rows[1], :]], axis=0)
        parts = tile_scores(ks, kt[...], queries, rows, masked if beside else None)
        exps, top, total = tile_softmax(parts)
        log_sums[pl.ds(tile, 1), :] = top + jnp.log(total)
        exps = [part.astype(bf16) for part in exps]
        acc = dot_nn(vtt[...], exps[0])
        if beside:
            own = [dot_tn(vs[rows[0], :], exps[1]), dot_tn(vs[rows[1], :], exps[2])]
            acc = acc + jnp.concatenate(own, axis=1) + dot_tn(vs[rows[2], :], exps[3])
        acc = (acc / total).astype(bf16)
        for i in range(2):
            quarter, columns = place_of(pair[i], part_blocks)
            result[quarter, :, columns] = acc[:, i * BLOCK : (i + 1) * BLOCK]

    tile_loops(blocks, run)
    span = pl.ds(head * HEAD_DIM, HEAD_DIM)
    copy = pltpu.make_async_copy(result, out.at[:, span, :], sem)
    copy.start()
    copy.wait()


def attn_bwd_kernel(
    head, heads, blocks, tab, qkv, dot, log_sums, before, out, *scratch
):
    del before
    qs, ks, vs, kt, vt, ktt, dkt, dvt, dka, dva, result, sem = scratch
    part_blocks = blocks // 4
    split_head(head, heads * HEAD_DIM, qkv, qs, ks, vs)
    for j in range(TRUNK):
        rows = block_rows(tab[j])
        span = slice(j * BLOCK, (j + 1) * BLOCK)
        kt[span, :] = ks[rows, :]
        vt[span, :] = vs[rows, :]
        ktt[:, span] = ks[rows, :].T
    dkt[...] = jnp.zeros_like(dkt)
    dvt[...] = jnp.zeros_like(dvt)
    dka[...] = jnp.zeros_like(dka)
    dva[...] = jnp.zeros_like(dva)
    lanes = slice(head * HEAD_DIM, (head + 1) * HEAD_DIM)

    def run(tile, beside):
        pair, rows, masked = tile_places(tab, tile, blocks)
        queries = jnp.concatenate([qs[rows[0], :], qs[rows[1], :]], axis=0)
        places = [place_of(index, part_blocks) for index in pair]
        grads = jnp.concatenate([dot[q, lanes, columns] for q, columns in places], axis=1)
        parts = tile_scores(ks, kt[...], queries, rows, masked if beside else None)
        count = len(parts)
        row_sums = for_parts(log_sums[pl.ds(tile, 1), :], count)
        probs = [jnp.exp(part - row_sum) for part, row_sum in zip(parts, row_sums)]
        grad_parts = [dot_nn(vt[...], grads)]
        if beside:
            grad_parts.append(dot_nn(vs[rows[0], :], grads[:, :BLOCK]))
            grad_parts.append(dot_nn(vs[rows[1], :], grads[:, BLOCK:]))
            grad_parts.append(dot_nn(vs[rows[2], :], grads))
        products = [p * g for p, g in zip(probs, grad_parts)]
        deltas = for_parts(over_keys(jnp.sum, jnp.add, products), count)
        score_grads = [(p * (g - d)).astype(bf16) for p, g, d in zip(probs, grad_parts, deltas)]
        probs = [p.astype(bf16) for p in probs]
        dvt[...] += dot_nt(probs[0], grads)
        dkt[...] += dot_nn(score_grads[0], queries)
        query_grad = dot_nn(ktt[...], score_grads[0])
        if beside:
            dva[rows[0], :] += dot_nt(probs[1], grads[:, :BLOCK])
            dva[rows[1], :] += dot_nt(probs[2], grads[:, BLOCK:])
            dva[rows[2], :] += dot_nt(probs[3], grads)
            dka[rows[0], :] += dot_nn(score_grads[1], queries[:BLOCK])
            dka[rows[1], :] += dot_nn(score_grads[2], queries[BLOCK:])
            dka[rows[2], :] += dot_nn(score_grads[3], queries)
            own = [
                dot_tn(ks[rows[0], :], score_grads[1]),
                dot_tn(ks[rows[1], :], score_grads[2]),
            ]
            query_grad = query_grad + jnp.concatenate(own, axis=1)
            query_grad = query_grad + dot_tn(ks[rows[2], :], score_grads[3])
        query_grad = (query_grad * HEAD_DIM**-0.5).astype(bf16)
        result[0, :, rows[0]] = query_grad[:, :BLOCK]
        result[0, :, rows[1]] = query_grad[:, BLOCK:]

    tile_loops(blocks, run)
    for j in range(TRUNK):
        rows = block_rows(tab[j])
        span = slice(j * BLOCK, (j + 1) * BLOCK)
        dka[rows, :] = dkt[span, :]
        dva[rows, :] = dvt[span, :]
    result[1] = dka[...].T.astype(bf16)
    result[2] = dva[...].T.astype(bf16)
    copies = [
        pltpu.make_async_copy(
            result.at[i], out.at[pl.ds((i * heads + head) * HEAD_DIM, HEAD_DIM), :], sem.at[i]
        )
        for i in range(3)
    ]
    for copy in copies:
        copy.start()
    for copy in copies:
        copy.wait()


def attn_forward(table, qkv, before, head, heads, blocks):
    rows = qkv.shape[0]
    trunk = TRUNK * BLOCK
    return pl.pallas_call(
        functools.partial(attn_fwd_kernel, head, heads, blocks),
        out_shape=(
            jax.ShapeDtypeStruct(before.shape, bf16),
            jax.ShapeDtypeStruct((16, PAIR), f32),
        ),
        in_specs=[
            pl.BlockSpec(memory_space=pltpu.SMEM),
            pl.BlockSpec(memory_space=pltpu.VMEM),
            pl.BlockSpec(memory_space=pl.ANY),
        ],
        out_specs=(
            pl.BlockSpec(memory_space=pl.ANY),
            pl.BlockSpec(memory_space=pltpu.VMEM),
        ),
        input_output_aliases={2: 0},
        scratch_shapes=[pltpu.VMEM((rows, HEAD_DIM), bf16)] * 3
        + [pltpu.VMEM((trunk, HEAD_DIM), bf16), pltpu.VMEM((HEAD_DIM, trunk), bf16)]
        + [pltpu.VMEM((4, HEAD_DIM, rows // 4), bf16), pltpu.SemaphoreType.DMA],
        compiler_params=pltpu.CompilerParams(vmem_limit_bytes=32 << 20),
        cost_estimate=pl.CostEstimate(
            flops=6 * rows * trunk * BLOCK,
            bytes_accessed=8 * rows * HEAD_DIM,
            transcendentals=0,
        ),
        name="tree_attention",
    )(table, qkv, before)


def attn_backward(table, qkv, out_grad, log_sums, before, head, heads, blocks):
    rows = qkv.shape[0]
    trunk = TRUNK * BLOCK
    return pl.pallas_call(
        functools.partial(attn_bwd_kernel, head, heads, blocks),
        out_shape=jax.ShapeDtypeStruct(before.shape, bf16),
        in_specs=[
            pl.BlockSpec(memory_space=pltpu.SMEM),
            pl.BlockSpec(memory_space=pltpu.VMEM),
            pl.BlockSpec(memory_space=pltpu.VMEM),
            pl.BlockSpec(memory_space=pltpu.VMEM),
            pl.BlockSpec(memory_space=pl.ANY),
        ],
        out_specs=pl.BlockSpec(memory_space=pl.ANY),
        input_output_aliases={4: 0},
        scratch_shapes=[pltpu.VMEM((rows, HEAD_DIM), bf16)] * 3
        + [pltpu.VMEM((trunk, HEAD_DIM), bf16)] * 2
        + [pltpu.VMEM((HEAD_DIM, trunk), bf16)]
        + [pltpu.VMEM((trunk, HEAD_DIM), f32)] * 2
        + [pltpu.VMEM((rows, HEAD_DIM), f32)] * 2
        + [pltpu.VMEM((3, HEAD_DIM, rows), bf16), pltpu.SemaphoreType.DMA((3,))],
        compiler_params=pltpu.CompilerParams(vmem_limit_bytes=40 << 20),
        cost_estimate=pl.CostEstimate(
            flops=16 * rows * trunk * BLOCK,
            bytes_accessed=14 * rows * HEAD_DIM,
            transcendentals=0,
        ),
        name="tree_attention_grad",
    )(table, qkv, out_grad, log_sums, before)


def attention_table(path):
    blocks = path.shape[1]
    place = jnp.arange(blocks, dtype=jnp.int32)
    kind = (path[1] != path[0]).astype(jnp.int32) + (path[2] != path[1]).astype(jnp.int32)
    key = kind * 65536 + jnp.where(kind == 2, path[1] * 32, 0) + place
    rank = jnp.sum((key[None, :] < key[:, None]).astype(jnp.int32), axis=1)
    branch = jnp.sum(
        jnp.where((kind[None, :] == 1) & (path[2][None, :] == path[1][:, None]), place[None, :], 0),
        axis=1,
    )
    slot = (rank[None, :] == place[:, None]).astype(jnp.int32)
    columns = jnp.stack([place, jnp.where(kind == 2, branch, 0), kind])
    sorted_columns = jnp.sum(slot[None] * columns[:, None, :], axis=2)
    return jnp.concatenate([sorted_columns[0], sorted_columns[1, ::2], sorted_columns[2, ::2]])


def assemble_kernel(count, spans, flags, *refs):
    pieces, outs = refs[: 2 * count], refs[2 * count :]
    slab = pieces[0].shape[0]
    for j in range(2):
        for k in range(count):
            place = lax.rem(flags[0] + (count - k), count)
            rows = pl.ds(pl.multiple_of(place * slab, 16), slab)
            piece = pieces[j * count + k]
            for out, (lanes, kind) in zip(outs, spans):
                width = lanes.stop - lanes.start
                if kind == 1 or j == 0 and kind == 0:
                    out[rows, j * width : (j + 1) * width] = piece[:, lanes]
                for crossed in range(2 if kind == 2 else 0):

                    @pl.when(flags[1] == crossed)
                    def _():
                        first = (j ^ crossed) * width
                        out[rows, first : first + width] = piece[:, lanes]


def assembled(shard, crossed, own, twin, spans):
    count = len(own)
    rows = count * own[0].shape[0]
    vmem = pl.BlockSpec(memory_space=pltpu.VMEM)
    shapes = [
        jax.ShapeDtypeStruct((rows, (lanes.stop - lanes.start) * (2 if kind else 1)), bf16)
        for lanes, kind in spans
    ]
    return pl.pallas_call(
        functools.partial(assemble_kernel, count, spans),
        out_shape=shapes,
        in_specs=[pl.BlockSpec(memory_space=pltpu.SMEM)] + [vmem] * (2 * count),
        out_specs=[vmem] * len(spans),
        compiler_params=pltpu.CompilerParams(vmem_limit_bytes=24 << 20),
        cost_estimate=pl.CostEstimate(
            flops=0, bytes_accessed=4 * sum(piece.size for piece in own + twin), transcendentals=0
        ),
        name="assembled_weights",
    )(jnp.stack([shard, crossed]).astype(jnp.int32), *own, *twin)


def pack_kernel(count, j, flags, up, down, proj, out, small, *pieces):
    slab = up.shape[0] // count
    group = pieces[0].shape[1] - up.shape[1] - down.shape[1] - proj.shape[1]
    for k in range(count):
        place = lax.rem(flags[0] + (count - k - 1), count)
        rows = pl.ds(pl.multiple_of(place * slab, 16), slab)
        first = 0
        for source in (up, down, proj):
            pieces[k][:slab, first : first + source.shape[1]] = source[rows, :]
            first += source.shape[1]
        for crossed in range(2):

            @pl.when(flags[1] == crossed)
            def _():
                lane = (j ^ crossed) * group
                pieces[k][:slab, first:] = out[rows, lane : lane + group]

        pieces[k][slab:, :] = small[place]


def packed_pieces(shard, crossed, count, up, down, proj, out, small, j):
    rows = up.shape[0] // count + small.shape[1]
    width = small.shape[2]
    vmem = pl.BlockSpec(memory_space=pltpu.VMEM)
    return pl.pallas_call(
        functools.partial(pack_kernel, count, j),
        out_shape=[jax.ShapeDtypeStruct((rows, width), bf16)] * count,
        in_specs=[pl.BlockSpec(memory_space=pltpu.SMEM)] + [vmem] * 5,
        out_specs=[vmem] * count,
        compiler_params=pltpu.CompilerParams(vmem_limit_bytes=24 << 20),
        cost_estimate=pl.CostEstimate(
            flops=0, bytes_accessed=4 * count * rows * width, transcendentals=0
        ),
        name="packed_gradients",
    )(jnp.stack([shard, crossed]).astype(jnp.int32), up, down, proj, out, small)


def place_kernel(start, places, first, second, third, fourth, before, out, wide, sem):
    del before
    rows = first.shape[0]
    half, core = places[0], places[1]
    spots = [(half, core), (1 - half, core), (half, 1 - core), (1 - half, 1 - core)]
    copies = []
    for i, piece in enumerate((first, second, third, fourth)):
        wide[i] = piece[...].astype(wide.dtype)
        row, column = spots[i]
        target = out.at[row, column, pl.ds(start, rows), :]
        copy = pltpu.make_async_copy(wide.at[i], target, sem.at[i])
        copy.start()
        copies.append(copy)
    for copy in copies:
        copy.wait()


def place_rows(places, pieces, before, start):
    rows, width = pieces[0].shape
    vmem = pl.BlockSpec(memory_space=pltpu.VMEM)
    return pl.pallas_call(
        functools.partial(place_kernel, start),
        out_shape=jax.ShapeDtypeStruct(before.shape, before.dtype),
        in_specs=[pl.BlockSpec(memory_space=pltpu.SMEM)]
        + [vmem] * 4
        + [pl.BlockSpec(memory_space=pl.ANY)],
        out_specs=pl.BlockSpec(memory_space=pl.ANY),
        input_output_aliases={5: 0},
        scratch_shapes=[
            pltpu.VMEM((4, rows, width), before.dtype),
            pltpu.SemaphoreType.DMA((4,)),
        ],
        compiler_params=pltpu.CompilerParams(vmem_limit_bytes=24 << 20),
        cost_estimate=pl.CostEstimate(
            flops=0, bytes_accessed=24 * rows * width, transcendentals=0
        ),
        name="placed_rows",
    )(places, *pieces, before)


def student_kernel(part_blocks, labels, rows, weight, shift, query, student, weights, stats):
    width = weight.shape[1]
    pool_dim = width // POOL_HEADS
    value = dot_nn(rows[...], weight[...]) + shift[...]
    student[...] = value
    lane = lax.broadcasted_iota(jnp.int32, (1, width), 1)
    first_head = lane < pool_dim
    product = value * query[...]
    scores = [
        jnp.sum(product[:, e * pool_dim : (e + 1) * pool_dim], axis=1, keepdims=True)
        for e in range(POOL_HEADS)
    ]
    stats[...] = jnp.zeros_like(stats)
    for block in range(part_blocks):
        span = slice(block * BLOCK, (block + 1) * BLOCK)
        peaks = [jnp.max(score[span], axis=0, keepdims=True) for score in scores]
        exps = [jnp.exp(score[span] - peak) for score, peak in zip(scores, peaks)]
        masses = [jnp.sum(part, axis=0, keepdims=True) for part in exps]
        lanes = jnp.where(first_head, exps[0], exps[1])
        weights[span, :] = lanes
        stats[block : block + 1, :width] = jnp.sum(lanes * value[span], axis=0, keepdims=True)
        label = jnp.full((1, width), labels[block], jnp.int32).astype(f32)
        tail = jnp.where(lane == 4, label, 0.0)
        for place, part in enumerate(peaks + masses):
            tail = jnp.where(lane == place, part, tail)
        stats[block : block + 1, width:] = tail


def student_stats(labels, rows, weight, shift, query, part_blocks):
    count = rows.shape[0]
    width = weight.shape[1]
    vmem = pl.BlockSpec(memory_space=pltpu.VMEM)
    return pl.pallas_call(
        functools.partial(student_kernel, part_blocks),
        out_shape=(
            jax.ShapeDtypeStruct((count, width), f32),
            jax.ShapeDtypeStruct((count, width), f32),
            jax.ShapeDtypeStruct((8, 2 * width), f32),
        ),
        in_specs=[pl.BlockSpec(memory_space=pltpu.SMEM)] + [vmem] * 4,
        out_specs=(vmem,) * 3,
        cost_estimate=pl.CostEstimate(
            flops=2 * rows.size * width, bytes_accessed=2 * rows.size, transcendentals=count
        ),
        name="student_stats",
    )(labels, rows, weight, shift, query)


def pool_kernel(
    part_blocks,
    own,
    near,
    across,
    corner,
    member,
    leaf,
    dense,
    head,
    dense_shift,
    cls_shift,
    student,
    weights,
    query,
    student_low,
    grad_dense,
    grad_head,
    vectors,
):
    width = dense.shape[0]
    pool_dim = width // POOL_HEADS
    pool_scale = pool_dim ** (-0.5)
    stats = jnp.concatenate([own[...], near[...], across[...], corner[...]], axis=0)
    moment = stats[:, :width]
    seen = member[...] > 0.0
    is_leaf = leaf[...] > 0.0
    coeffs = []
    pooled = []
    for e in range(POOL_HEADS):
        peak = stats[:, width + e : width + e + 1]
        mass = stats[:, width + POOL_HEADS + e : width + POOL_HEADS + e + 1]
        top = jnp.max(jnp.where(seen, peak, MASK_VALUE), axis=0, keepdims=True)
        factor = jnp.where(seen, jnp.exp(jnp.where(seen, peak - top, MASK_VALUE)), 0.0)
        total = jnp.sum(factor * mass, axis=0, keepdims=True)
        total = jnp.where(total > 0.0, total, 1.0)
        coeff = factor / total
        coeffs.append(coeff)
        lanes = slice(e * pool_dim, (e + 1) * pool_dim)
        pooled.append(exact(coeff, moment[:, lanes], ((0,), (0,))))
    pooled = jnp.concatenate(pooled, axis=1)
    dense_out = jnp.tanh(exact(pooled, dense[...], ((1,), (0,))) + dense_shift[...])
    logits = exact(dense_out, head[...], ((1,), (0,))) + cls_shift[...]
    logits = logits - jnp.max(logits, axis=1, keepdims=True)
    chances = jnp.exp(logits)
    chances = chances / jnp.sum(chances, axis=1, keepdims=True)
    label = stats[:, width + 2 * POOL_HEADS : width + 2 * POOL_HEADS + 1]
    classes = lax.broadcasted_iota(jnp.int32, (1, width), 1).astype(f32)
    onehot = jnp.where(label == classes, 1.0, 0.0)
    grad_logits = jnp.where(is_leaf, chances - onehot, 0.0)
    grad_head[...] = exact(dense_out, grad_logits, ((0,), (0,)))
    grad_pre = exact(grad_logits, head[...], ((1,), (1,))) * (1.0 - dense_out * dense_out)
    grad_dense[...] = exact(pooled, grad_pre, ((0,), (0,)))
    grad_pooled = exact(grad_pre, dense[...], ((1,), (1,)))
    product = grad_pooled * pooled
    spread = []
    offset = []
    for e in range(POOL_HEADS):
        lanes = slice(e * pool_dim, (e + 1) * pool_dim)
        spread.append(exact(coeffs[e], grad_pooled[:, lanes], ((1,), (0,))))
        inner = jnp.sum(product[:, lanes], axis=1, keepdims=True)
        inner = jnp.broadcast_to(inner, (inner.shape[0], pool_dim))
        offset.append(exact(coeffs[e], inner, ((1,), (0,))))
    spread = jnp.concatenate(spread, axis=1)
    offset = jnp.concatenate(offset, axis=1)
    grad_query = jnp.zeros((1, width), f32)
    grad_shift = jnp.zeros((1, width), f32)
    first_head = lax.broadcasted_iota(jnp.int32, (1, width), 1) < pool_dim
    for block in range(part_blocks):
        span = slice(block * BLOCK, (block + 1) * BLOCK)
        value = student[span, :]
        weight = weights[span, :]
        row = spread[block : block + 1]
        product = value * row
        inner = jnp.where(
            first_head,
            jnp.sum(product[:, :pool_dim], axis=1, keepdims=True),
            jnp.sum(product[:, pool_dim:], axis=1, keepdims=True),
        )
        grad_score = weight * (inner - offset[block : block + 1])
        grad_query = grad_query + jnp.sum(grad_score * value, axis=0, keepdims=True)
        low = (weight * row + grad_score * query[...]).astype(bf16)
        student_low[span, :] = low
        grad_shift = grad_shift + jnp.sum(low.astype(f32), axis=0, keepdims=True)
    vectors[0:1, :] = jnp.sum(grad_pre, axis=0, keepdims=True)
    vectors[1:2, :] = jnp.sum(grad_logits, axis=0, keepdims=True)
    vectors[2:3, :] = grad_query * pool_scale
    vectors[3:4, :] = grad_shift
    vectors[4:8, :] = jnp.zeros((4, width), f32)


def pool_classifier(part_blocks, *operands):
    student = operands[-3]
    width = student.shape[1]
    return pl.pallas_call(
        functools.partial(pool_kernel, part_blocks),
        out_shape=(
            jax.ShapeDtypeStruct(student.shape, bf16),
            jax.ShapeDtypeStruct((width, width), f32),
            jax.ShapeDtypeStruct((width, width), f32),
            jax.ShapeDtypeStruct((8, width), f32),
        ),
        cost_estimate=pl.CostEstimate(
            flops=2000 * width * width, bytes_accessed=16 * student.size, transcendentals=0
        ),
        name="pool_classifier",
    )(*operands)


def body(
    tokens,
    cotangent,
    block_path,
    labels,
    w_attn_in,
    attn_bias,
    w_attn_out,
    w_up,
    up_bias,
    w_down,
    norm_gain,
    layer_bias,
    stu_proj,
    stu_bias,
    pool_query,
    stu_dense,
    stu_head,
    class_bias,
):
    row_count, model = tokens.shape[1:]
    own_blocks = labels.shape[1]
    tree_blocks = 2 * own_blocks
    group_width = w_attn_in.shape[2]
    heads = group_width // HEAD_DIM
    slab = w_up.shape[0]
    hidden = w_up.shape[1]
    shards = lax.axis_size("shard")
    trees = lax.axis_size("tree")
    stu_width = stu_proj.shape[1]
    pool_dim = stu_width // POOL_HEADS
    pool_scale = pool_dim ** (-0.5)
    class_count = class_bias.shape[0]
    part_rows = row_count // 2
    part_blocks = own_blocks // 2

    shard = lax.axis_index("shard")
    tree = lax.axis_index("tree")
    side = lax.axis_index("side")
    half = lax.axis_index("half")
    core = lax.axis_index("core")

    shift_rows = layer_bias.astype(f32)
    gain_rows = norm_gain.astype(f32)
    stu_shifts = stu_bias.astype(f32)
    pool_vec = pool_query.astype(f32)

    def by_shard(pieces):
        result = blank((shards,) + pieces[0].shape, pieces[0].dtype)
        for k, piece in enumerate(pieces):
            result = lax.dynamic_update_index_in_dim(result, piece, (shard - k) % shards, 0)
        return result

    def rows_of(array, part):
        place = (half, part * part_rows, 0)
        return lax.dynamic_slice(array, place, (1, part_rows, model))[0]

    own_part = rows_of(tokens, core)
    other_part = swap(own_part, "side")
    own_rest = rows_of(after(tokens, own_part), 1 - core)

    qkv_width = 3 * group_width
    bias_row = jnp.concatenate([attn_bias[0], jnp.zeros((group_width,), bf16), attn_bias[1]])
    up_rows = jnp.pad(up_bias.reshape(2, hidden // 2), ((0, 0), (0, qkv_width - hidden // 2)))
    qkv_message = jnp.concatenate(
        [
            w_attn_in.transpose(1, 0, 2).reshape(slab, qkv_width),
            bias_row[None],
            up_rows,
            jnp.zeros((13, qkv_width), bf16),
        ],
        axis=0,
    )
    qkv_twin = swap(after(qkv_message, own_part), "half")
    twin_bias = qkv_twin[slab + 1 : slab + 3, : hidden // 2].reshape(hidden)
    qkv_message = jnp.where(side == half, qkv_message, qkv_twin)
    qkv_bias = qkv_message[slab].astype(f32)
    qkv_pieces = [qkv_message]
    for k in range(1, shards):
        qkv_pieces.append(ring(qkv_pieces[-1]))
    other_twin = swap(after(other_part, qkv_pieces[2]), "core")
    tree_rows = jnp.concatenate([own_part, other_part, own_rest, other_twin], axis=0)
    qkv_weight = by_shard([piece[:slab] for piece in qkv_pieces]).reshape(model, qkv_width)

    stu_lanes = slice(hidden, hidden + stu_width)
    out_lanes = slice(hidden + stu_width, hidden + stu_width + group_width)
    message_one = jnp.concatenate([w_up, stu_proj, w_attn_out.T], axis=1)
    message_two = w_down.T
    own_one = [after(message_one, qkv_pieces[-1], other_twin)]
    own_one.append(ring(own_one[0]))
    twin_one = [swap(after(message_one, qkv_message), "half")]

    paths = lax.dynamic_index_in_dim(block_path, half, 0, keepdims=False)
    paths = lax.dynamic_slice_in_dim(paths, tree * tree_blocks, tree_blocks, 1)
    paths = after(paths, qkv_pieces[1])
    quarters = paths.reshape(3, 2, 2, part_blocks)
    quarters = jnp.where(side == 0, quarters, quarters[:, ::-1])
    quarters = jnp.where(core == 0, quarters, quarters[:, :, ::-1])
    table = attention_table(quarters.swapaxes(1, 2).reshape(3, tree_blocks))

    quarters = jnp.pad(quarters, ((0, 0),) * 3 + ((0, 8 - part_blocks),), constant_values=-1)
    quarters = quarters.reshape(3, 32)
    is_leaf = (quarters[1] != quarters[2]).astype(f32)
    member = jnp.any(quarters[2][:, None, None] == quarters.T[None, :, :], axis=2).astype(f32)
    member = member * is_leaf[None, :]
    leaf_column = is_leaf[:, None]
    lane_pad = stu_width - class_count
    dense_full = stu_dense.astype(f32)
    head_padded = jnp.pad(stu_head.astype(f32), ((0, 0), (0, lane_pad)))
    cls_padded = jnp.pad(
        class_bias.astype(f32)[None, :], ((0, 0), (0, lane_pad)), constant_values=MASK_VALUE
    )
    own_labels = lax.dynamic_slice(labels, (half, core * part_blocks), (1, part_blocks))[0]
    dense_shift = stu_bias[1:2].astype(f32)
    proj_shift = stu_bias[0:1].astype(f32)
    scaled_query = (pool_vec * pool_scale)[None, :]
    prepared = lax.optimization_barrier(
        (
            tree_rows,
            member,
            leaf_column,
            dense_full,
            head_padded,
            cls_padded,
            own_labels,
            dense_shift,
            proj_shift,
            scaled_query,
        )
    )
    tree_rows, member, leaf_column, dense_full, head_padded, cls_padded = prepared[:6]
    own_labels, dense_shift, proj_shift, scaled_query = prepared[6:]

    qkv = (dot_nn(tree_rows, qkv_weight) + qkv_bias).astype(bf16)
    attended = blank((4, group_width, part_rows), bf16)
    attended, sums_0 = attn_forward(table, qkv, attended, 0, heads, tree_blocks)
    twin_two = [swap(after(message_two, twin_one[0]), "half")]
    one = after(own_one[1], attended)
    own_one.append(ring(one))
    twin_one.append(swap(one, "half"))
    attended = after(attended, twin_one[0], twin_two[0])
    attended, sums_1 = attn_forward(table, qkv, attended, 1, heads, tree_blocks)
    one = after(own_one[2], attended)
    own_one.append(ring(one))
    twin_one.append(swap(one, "half"))
    attended = after(attended, twin_one[1])
    attended, sums_2 = attn_forward(table, qkv, attended, 2, heads, tree_blocks)
    twin_one.append(swap(after(own_one[3], attended), "half"))
    own_two = [after(message_two, attended)]
    own_two.append(ring(own_two[0]))
    attended = after(attended, twin_one[2])

    def exchange(pieces):
        return [
            pieces[0],
            swap(pieces[1], "core"),
            swap(pieces[2], "side"),
            diagonal(pieces[3]),
        ]

    def at(array, place):
        return lax.dynamic_index_in_dim(array, place, 0, keepdims=False)

    def placed(pieces, places):
        result = blank((len(pieces),) + pieces[0].shape, pieces[0].dtype)
        for piece, place in zip(pieces, places):
            result = lax.dynamic_update_index_in_dim(result, piece, place, 0)
        return result

    quarter_places = [0, 2, 1, 3]
    crossed = jnp.where(side == half, 0, 1)

    def in_quarters(pieces):
        kept, near, across, corner = pieces
        return jnp.stack([kept, across, near, corner])

    crossing = exchange([attended[place] for place in quarter_places])
    own_two.append(ring(after(own_two[1], crossing[1])))
    own_one[0] = after(own_one[0], *crossing[1:], own_two[2])
    heads_own = in_quarters(crossing)
    heads_own = heads_own.reshape(4 * group_width, part_rows)
    heads_own = after(heads_own, twin_one[3])
    up_weight, stu_weight, out_half = assembled(
        shard,
        crossed,
        own_one,
        twin_one,
        [(slice(0, hidden), 1), (stu_lanes, 0), (out_lanes, 2)],
    )
    twin_two.append(swap(after(own_two[1], up_weight), "half"))
    own_two.append(ring(after(own_two[2], up_weight)))
    out_weight = jnp.concatenate([out_half, swap(out_half, "core")], axis=1)
    twin_two.append(swap(after(own_two[2], up_weight), "half"))
    out_weight = after(out_weight, twin_two[1], twin_two[2], own_two[3])
    twin_two.append(swap(after(own_two[3], out_weight), "half"))
    hidden_shift = jnp.concatenate([up_bias, twin_bias]).astype(f32)

    attn = lax.dot_general(
        heads_own, out_weight, (((0,), (1,)), ((), ())), preferred_element_type=f32
    )
    resid_one = own_part.astype(f32) + (attn + shift_rows[0])
    hidden_one, normed_one, inverse_one = norm_forward(resid_one, gain_rows[0], shift_rows[2])
    hidden_low = hidden_one.astype(bf16)

    hidden_both = jnp.concatenate([hidden_low, swap(hidden_low, "core")], axis=0)
    pre_act = dot_nn(hidden_both, up_weight) + hidden_shift
    normal_cdf = 0.5 * (1.0 + lax.erf(pre_act * 0.7071067811865476))
    active = (pre_act * normal_cdf).astype(bf16)
    slope = normal_cdf + pre_act * jnp.exp(-0.5 * pre_act * pre_act) * 0.3989422804014327
    slope = lax.optimization_barrier(slope.astype(bf16))
    own_two[0] = after(own_two[0], active)
    (down_weight,) = assembled(shard, crossed, own_two, twin_two, [(slice(0, hidden), 1)])
    ffn_far = swap(dot_nt(active[part_rows:], down_weight).astype(bf16), "core")
    ffn = dot_nt(active[:part_rows], down_weight) + ffn_far.astype(f32)
    hidden_two, normed_two, inverse_two = norm_forward(
        hidden_one + ffn + shift_rows[1], gain_rows[1], shift_rows[3]
    )
    block_low = hidden_two.astype(bf16)

    def everywhere(rows, other):
        return rows, other, [swap(rows, "core"), swap(other, "core")]

    def placed(result, start, rows, other, twins):
        places = jnp.stack([half, core]).astype(jnp.int32)
        return place_rows(places, [rows, other] + twins, result, start)

    block_other = swap(block_low, "half")

    student, weights, stats = student_stats(
        own_labels, block_low, stu_weight, proj_shift, scaled_query, part_blocks
    )
    student_low, grad_dense, grad_head, pool_vectors = pool_classifier(
        part_blocks,
        *exchange([stats] * 4),
        member,
        leaf_column,
        dense_full,
        head_padded,
        dense_shift,
        cls_padded,
        student,
        weights,
        scaled_query,
    )
    grad_proj = dot_tn(block_low, student_low)

    upstream = lax.dynamic_slice(
        cotangent, (half, core * part_rows, 0), (1, part_rows, model)
    )[0].astype(f32)
    grad_two = upstream + dot_nt(student_low, stu_weight)
    resid_grad_two, gain_grad_two, shift_grad_two = norm_backward(
        grad_two, normed_two, inverse_two, gain_rows[1]
    )
    down_shift_grad = jnp.sum(resid_grad_two, axis=0)
    ffn_low = resid_grad_two.astype(bf16)
    ffn_twin = swap(ffn_low, "core")
    ffn_both = jnp.concatenate([ffn_low, ffn_twin], axis=0)
    pre_low = (dot_nn(ffn_both, down_weight) * slope).astype(bf16)
    grad_hidden_shift = jnp.sum(pre_low.astype(f32), axis=0)
    far_one = swap(dot_nt(pre_low[part_rows:], up_weight).astype(bf16), "core")
    grad_one = resid_grad_two + dot_nt(pre_low[:part_rows], up_weight) + far_one.astype(f32)

    resid_grad_one, gain_grad_one, shift_grad_one = norm_backward(
        grad_one, normed_one, inverse_one, gain_rows[0]
    )
    out_shift_grad = jnp.sum(resid_grad_one, axis=0)
    attn_low = resid_grad_one.astype(bf16)
    block_twin = swap(block_low, "core")
    heads_grad = lax.dot_general(
        out_weight, attn_low, (((0,), (1,)), ((), ())), preferred_element_type=f32
    ).astype(bf16)
    grad_out = lax.dot_general(
        attn_low, heads_own, (((0,), (1,)), ((), ())), preferred_element_type=f32
    ).astype(bf16)
    heads_grad = heads_grad.reshape(4, group_width, part_rows)
    pieces = [heads_grad[place] for place in quarter_places]
    pieces = lax.optimization_barrier(
        (*pieces, grad_out, ffn_low, ffn_twin, pre_low, block_twin)
    )
    ffn_low, ffn_twin, pre_low, block_twin = pieces[5:]
    ffn_both = jnp.concatenate([ffn_low, ffn_twin], axis=0)
    attended_grad = in_quarters(exchange(pieces[:4]))

    def halves(array):
        return [array[:, :hidden], array[:, hidden:]]

    grad_down = [dot_tn(ffn_both, part).astype(bf16) for part in halves(active)]
    grad_up = [dot_tn(hidden_both, part).astype(bf16) for part in halves(pre_low)]

    up_grad = jnp.zeros((4, hidden), f32)
    for j in range(2):
        up_grad = lax.dynamic_update_slice(
            up_grad,
            grad_hidden_shift[None, j * hidden : (j + 1) * hidden],
            (2 * jnp.where(j == 0, half, 1 - half) + core, 0),
        )
    first = jnp.where((side == 0) & (core == 0), 1.0, 0.0)
    pieces = [
        gain_grad_one,
        gain_grad_two,
        out_shift_grad,
        down_shift_grad,
        shift_grad_one,
        shift_grad_two,
        up_grad.reshape(-1),
        pool_vectors[3],
        pool_vectors[0] * first,
        pool_vectors[2],
        pool_vectors[1] * first,
        (grad_dense * first).reshape(-1),
        (grad_head[:, :16] * first).reshape(-1),
    ]
    sizes = [piece.size for piece in pieces]
    starts = [sum(sizes[:i]) for i in range(len(sizes) + 1)]
    packed = 2 * hidden + stu_width + group_width
    small = jnp.concatenate(pieces)
    small = jnp.pad(small, (0, -small.size % (shards * packed)))
    small_rows = small.size // (shards * packed)
    small = small.reshape(shards, small_rows, packed)
    small = jnp.pad(small, ((0, 0), (0, 16 - small_rows), (0, 0)))
    small = (small + swap(small, "core")).astype(bf16)

    half_out = 2 * group_width
    proj_low = grad_proj.astype(bf16)
    out_sum = grad_out[:, :half_out].astype(f32) + swap(grad_out[:, half_out:], "core").astype(f32)
    out_sum = out_sum.astype(bf16)
    proj_sum = (proj_low.astype(f32) + swap(proj_low, "core").astype(f32)).astype(bf16)
    out_sum = after(out_sum, attended_grad, block_other)
    block_far = swap(after(block_other, out_sum), "core")
    kept, sent = [
        packed_pieces(
            shard, crossed, shards, grad_up[j], grad_down[j], proj_sum, out_sum, small, j
        )
        for j in range(2)
    ]

    def reduced(k, got, last):
        total = kept[k].astype(f32) + got.astype(f32)
        if last is not None:
            total = total + last.astype(f32)
        return total.astype(bf16)

    qkv_grad = blank((qkv_width, 4 * part_rows), bf16)
    qkv_grad = after(qkv_grad, *sent)
    got = [swap(sent[0], "half"), swap(sent[1], "half")]
    qkv_grad = attn_backward(
        table, qkv, attended_grad, sums_0, qkv_grad, 0, heads, tree_blocks
    )
    kept = lax.optimization_barrier((qkv_grad, *kept))[1:]
    totals = [reduced(0, got[0], None)]
    passed = ring(totals[0])
    got.append(swap(after(sent[2], totals[0]), "half"))
    qkv_grad = after(qkv_grad, totals[0])
    qkv_grad = attn_backward(
        table, qkv, attended_grad, sums_1, qkv_grad, 1, heads, tree_blocks
    )
    totals.append(reduced(1, after(got[1], qkv_grad), passed))
    passed = ring(totals[1])
    got.append(swap(after(sent[3], totals[1]), "half"))
    qkv_grad = after(qkv_grad, totals[1])
    qkv_grad = attn_backward(
        table, qkv, attended_grad, sums_2, qkv_grad, 2, heads, tree_blocks
    )
    totals.append(reduced(2, after(got[2], qkv_grad), passed))
    passed = ring(totals[2])
    qkv_grad = after(qkv_grad, totals[2])

    def to_rows(columns):
        return lax.dot_general(
            columns, qkv_weight, (((0,), (1,)), ((), ())), preferred_element_type=f32
        ).astype(bf16)

    sent_grad = to_rows(qkv_grad[:, row_count:])
    near_grad = swap(sent_grad, "core")
    kept_grad = to_rows(after(qkv_grad, sent_grad)[:, :row_count])
    far_rows = kept_grad[part_rows:].astype(f32) + near_grad[part_rows:].astype(f32)
    far_rows = far_rows.astype(bf16)
    chunk = part_rows // 2
    spans = [slice(0, chunk), slice(chunk, part_rows)]

    grad_in = lax.dot_general(
        tree_rows, after(qkv_grad, far_rows), (((0,), (1,)), ((), ())), preferred_element_type=f32
    )
    grad_in = grad_in.astype(bf16).reshape(shards, 2, slab // 2, qkv_width)
    kept_in = lax.dynamic_index_in_dim(grad_in, half, 1, keepdims=False)
    sent_in = lax.dynamic_index_in_dim(grad_in, 1 - half, 1, keepdims=False)
    bias_sums = jnp.sum(qkv_grad.astype(f32), axis=1).astype(bf16)
    bias_rows = bias_sums.reshape(shards, 1, qkv_width // shards)
    bias_rows = jnp.pad(bias_rows, ((0, 0), (0, 15), (0, qkv_width - qkv_width // shards)))
    far_first = swap(far_rows[spans[0]], "side")
    sent_in, far_rows, far_first = lax.optimization_barrier(
        (jnp.concatenate([sent_in, bias_rows], axis=1), far_rows, far_first)
    )
    far_second = swap(far_rows[spans[1]], "side")
    got_in = swap(sent_in, "half")
    kept_in = jnp.concatenate([kept_in, bias_rows], axis=1)

    def at_in(k):
        place = (shard - k) % shards
        return at(kept_in, place).astype(f32) + at(got_in, place).astype(f32)

    def tokens_part(i, far):
        near = kept_grad[:part_rows][spans[i]].astype(f32)
        near = near + near_grad[:part_rows][spans[i]].astype(f32)
        return (resid_grad_one[spans[i]] + near + far.astype(f32)).astype(bf16)

    tokens_grad = blank((2, 2, part_rows, model), f32)
    total = reduced(3, got[3], passed)
    got_in, far_second, total = lax.optimization_barrier((got_in, far_second, total))
    chip_in = (kept_in.astype(f32) + got_in.astype(f32)).astype(bf16)
    rows_low, rows_high = [tokens_part(i, far) for i, far in enumerate((far_first, far_second))]
    rows_all = jnp.concatenate([rows_low, rows_high], axis=0)
    chip_in, rows_all, total = lax.optimization_barrier((chip_in, rows_all, total))
    other_all = swap(rows_all, "half")
    total_far = swap(total, "side")
    parts_in = [at(chip_in, shard)]
    for k in range(1, shards):
        pairs = [(i, (i + k) % shards) for i in range(shards)]
        sent_part = at(chip_in, (shard + k) % shards)
        parts_in.append(lax.ppermute(sent_part, "shard", pairs))
    block_out = placed(
        blank((2, 2, part_rows, model), bf16), 0, after(block_low, rows_all), block_other, [block_twin, block_far]
    )
    gathered = lax.optimization_barrier(
        (other_all, total_far, *parts_in, rows_all, total, block_out)
    )
    other_all, total_far, parts_in = gathered[0], gathered[1], gathered[2 : 2 + shards]
    rows_all, total, block_out = gathered[2 + shards :]
    block_out = block_out.reshape(2, row_count, model)
    part = sum(piece.astype(f32) for piece in parts_in)
    total = total.astype(f32) + total_far.astype(f32)
    if trees > 1:
        total = lax.psum(total, "tree")
        part = lax.psum(part, "tree")
    part = part.astype(bf16)
    half_slab = slab // 2
    part_twin = swap(part[:half_slab], "half")
    twins = [swap(rows_all, "core"), swap(other_all, "core")]
    bias_part = jnp.pad(part[half_slab : half_slab + 1], ((0, 0), (0, packed - qkv_width)))
    small = jnp.concatenate([total[slab : slab + small_rows], bias_part.astype(f32)], axis=0)
    small = jnp.pad(small, ((0, 16 - small.shape[0]), (0, 0))).astype(bf16)[None]

    def joined(own, other, bit):
        low = (shard // bit) % 2 == 0
        return jnp.concatenate([jnp.where(low, own, other), jnp.where(low, other, own)], axis=0)

    small_other = over_shards(small, 1)
    part_twin, twins[0], twins[1], part, small, small_other = lax.optimization_barrier(
        (part_twin, *twins, part, small, small_other)
    )
    small = joined(small, small_other, 1)
    step = 2
    while step < shards:
        small = joined(small, over_shards(small, step), step)
        step *= 2
    tokens_grad = placed(tokens_grad, 0, rows_all, other_all, twins)
    tokens_grad = tokens_grad.reshape(2, row_count, model)
    small = small.astype(f32)
    bias_own = small[:, small_rows, : qkv_width // shards].reshape(1, qkv_width)
    small = small[:, :small_rows].reshape(-1)

    group_in = jnp.concatenate(
        [
            jnp.where(half == 0, part[:half_slab], part_twin),
            jnp.where(half == 0, part_twin, part[:half_slab]),
            jnp.pad(bias_own.astype(bf16), ((0, 15), (0, 0))),
        ],
        axis=0,
    )
    group_in = jnp.where(side == half, group_in, swap(group_in, "side")).astype(f32)
    grad_in_own = group_in[:slab].reshape(slab, 3, group_width).transpose(1, 0, 2)
    bias_own = group_in[slab]

    def taken(low, high):
        return small[starts[low] : starts[high]]

    position = 2 * half + core
    return (
        block_out,
        tokens_grad,
        grad_in_own,
        jnp.stack([bias_own[:group_width], bias_own[2 * group_width : qkv_width]]),
        total[:slab, 2 * hidden + stu_width :].T,
        total[:slab, :hidden],
        lax.dynamic_slice_in_dim(taken(6, 7), position * hidden, hidden, 0),
        total[:slab, hidden : 2 * hidden].T,
        taken(0, 2).reshape(2, model),
        taken(2, 6).reshape(4, model),
        total[:slab, 2 * hidden : 2 * hidden + stu_width],
        taken(7, 9).reshape(2, stu_width),
        taken(9, 10),
        taken(11, 12).reshape(stu_width, stu_width),
        taken(12, 13).reshape(stu_width, 16)[:, :class_count],
        taken(10, 11)[:class_count],
    )


def solution(mesh):
    shape = dict(mesh.shape)
    split = Mesh(
        mesh.devices.reshape(shape["shard"], shape["ctx"] // 2, 2, 2, shape["tp"] // 2),
        ("shard", "tree", "side", "half", "core"),
    )
    ctx = ("tree", "side")
    tp = ("half", "core")
    rows = ("shard",) + ctx
    in_specs = (
        P(None, rows, None),
        P(None, rows, None),
        P(None, None, "shard"),
        P(None, rows),
        P(None, "shard", tp),
        P(None, tp),
        P(tp, "shard"),
        P("shard", tp),
        P(tp),
        P(tp, "shard"),
        P(),
        P(),
        P("shard", None),
        P(),
        P(),
        P(),
        P(),
        P(),
    )
    out_specs = (
        P(None, rows, None),
        P(None, rows, None),
        P(None, "shard", tp),
        P(None, tp),
        P(tp, "shard"),
        P("shard", tp),
        P(tp),
        P(tp, "shard"),
        P(),
        P(),
        P("shard", None),
        P(),
        P(),
        P(),
        P(),
        P(),
    )
    return jax.shard_map(body, mesh=split, in_specs=in_specs, out_specs=out_specs, check_vma=False)
```

```python
import functools

import jax
import jax.numpy as jnp
from jax import lax
from jax.experimental import pallas as pl
from jax.experimental.pallas import tpu as pltpu
from jax.sharding import Mesh
from jax.sharding import PartitionSpec as P

HEAD_DIM = 64
POOL_HEADS = 2
TRUNK = 8
BLOCK = 128
PAIR = 2 * BLOCK

NORM_EPSILON = 1e-05
MASK_VALUE = -1e30

f32 = jnp.float32
bf16 = jnp.bfloat16


def swap(value, axis):
    return lax.ppermute(value, axis, [(0, 1), (1, 0)])


def diagonal(value):
    return lax.ppermute(value, ("side", "core"), [(0, 3), (3, 0), (1, 2), (2, 1)])


def ring(value):
    count = lax.axis_size("shard")
    return lax.ppermute(value, "shard", [(i, (i + 1) % count) for i in range(count)])


def over_shards(value, step):
    pairs = [(i, i ^ step) for i in range(lax.axis_size("shard"))]
    return lax.ppermute(value, "shard", pairs)


def after(value, *others):
    return lax.optimization_barrier((value,) + others)[0]


def blank(shape, dtype):
    return pl.pallas_call(
        lambda out: None,
        out_shape=jax.ShapeDtypeStruct(shape, dtype),
        out_specs=pl.BlockSpec(memory_space=pl.ANY),
        name="blank",
    )()


def dot_nn(left, right):
    return lax.dot_general(left, right, (((1,), (0,)), ((), ())), preferred_element_type=f32)


def dot_tn(left, right):
    return lax.dot_general(left, right, (((0,), (0,)), ((), ())), preferred_element_type=f32)


def dot_nt(left, right):
    return lax.dot_general(left, right, (((1,), (1,)), ((), ())), preferred_element_type=f32)


def exact(left, right, dims):
    return lax.dot_general(
        left, right, (dims, ((), ())), precision=lax.Precision.HIGHEST, preferred_element_type=f32
    )


def norm_forward(resid, gain, shift):
    center = resid - jnp.mean(resid, axis=-1, keepdims=True)
    inverse = lax.rsqrt(jnp.mean(center * center, axis=-1, keepdims=True) + NORM_EPSILON)
    normed = center * inverse
    return (normed * gain + shift, normed, inverse)


def norm_backward(grad_out, normed, inverse, gain):
    scaled = grad_out * gain
    grad_in = inverse * (
        scaled
        - jnp.mean(scaled, axis=-1, keepdims=True)
        - normed * jnp.mean(scaled * normed, axis=-1, keepdims=True)
    )
    return (grad_in, jnp.sum(grad_out * normed, axis=0), jnp.sum(grad_out, axis=0))


def block_rows(index):
    return pl.ds(pl.multiple_of(index * BLOCK, BLOCK), BLOCK)


def split_head(head, width, qkv, qs, ks, vs):
    first = head * HEAD_DIM
    qs[...] = qkv[:, first : first + HEAD_DIM] * bf16(HEAD_DIM**-0.5)
    ks[...] = qkv[:, width + first : width + first + HEAD_DIM]
    vs[...] = qkv[:, 2 * width + first : 2 * width + first + HEAD_DIM]


def tile_scores(keys, trunk_keys, queries, rows, masked):
    parts = [dot_nt(trunk_keys, queries)]
    if masked is not None:
        parts.append(dot_nt(keys[rows[0], :], queries[:BLOCK]))
        parts.append(dot_nt(keys[rows[1], :], queries[BLOCK:]))
        parts.append(dot_nt(keys[rows[2], :], queries) + masked)
    return parts


def over_keys(reduce, join, parts):
    result = reduce(parts[0], axis=0, keepdims=True)
    if len(parts) > 1:
        own = [reduce(parts[1], axis=0, keepdims=True), reduce(parts[2], axis=0, keepdims=True)]
        result = join(result, jnp.concatenate(own, axis=1))
        result = join(result, reduce(parts[3], axis=0, keepdims=True))
    return result


def for_parts(row, count):
    return [row, row[:, :BLOCK], row[:, BLOCK:], row][:count]


def tile_softmax(parts):
    tops = for_parts(over_keys(jnp.max, jnp.maximum, parts), len(parts))
    exps = [jnp.exp(part - top) for part, top in zip(parts, tops)]
    return exps, tops[0], over_keys(jnp.sum, jnp.add, exps)


def tile_places(tab, tile, blocks):
    first, second = tab[2 * tile], tab[2 * tile + 1]
    rows = [block_rows(first), block_rows(second), block_rows(tab[blocks + tile])]
    masked = jnp.where(tab[blocks + blocks // 2 + tile] == 2, 0.0, MASK_VALUE).astype(f32)
    return (first, second), rows, masked


def tile_loops(blocks, run):
    def trunk_step(pair, carry):
        run(2 * pair, False)
        run(2 * pair + 1, False)
        return carry

    def step(pair, carry):
        run(2 * pair, True)
        run(2 * pair + 1, True)
        return carry

    lax.fori_loop(0, TRUNK // 4, trunk_step, 0)
    lax.fori_loop(TRUNK // 4, blocks // 4, step, 0)


def place_of(index, part_blocks):
    quarter = index // part_blocks
    return quarter, block_rows(index - quarter * part_blocks)


def attn_fwd_kernel(head, heads, blocks, tab, qkv, before, out, log_sums, *scratch):
    del before
    qs, ks, vs, kt, vtt, result, sem = scratch
    part_blocks = blocks // 4
    split_head(head, heads * HEAD_DIM, qkv, qs, ks, vs)
    for j in range(TRUNK):
        rows = block_rows(tab[j])
        kt[j * BLOCK : (j + 1) * BLOCK, :] = ks[rows, :]
        vtt[:, j * BLOCK : (j + 1) * BLOCK] = vs[rows, :].T

    def run(tile, beside):
        pair, rows, masked = tile_places(tab, tile, blocks)
        queries = jnp.concatenate([qs[rows[0], :], qs[rows[1], :]], axis=0)
        parts = tile_scores(ks, kt[...], queries, rows, masked if beside else None)
        exps, top, total = tile_softmax(parts)
        log_sums[pl.ds(tile, 1), :] = top + jnp.log(total)
        exps = [part.astype(bf16) for part in exps]
        acc = dot_nn(vtt[...], exps[0])
        if beside:
            own = [dot_tn(vs[rows[0], :], exps[1]), dot_tn(vs[rows[1], :], exps[2])]
            acc = acc + jnp.concatenate(own, axis=1) + dot_tn(vs[rows[2], :], exps[3])
        acc = (acc / total).astype(bf16)
        for i in range(2):
            quarter, columns = place_of(pair[i], part_blocks)
            result[quarter, :, columns] = acc[:, i * BLOCK : (i + 1) * BLOCK]

    tile_loops(blocks, run)
    span = pl.ds(head * HEAD_DIM, HEAD_DIM)
    copy = pltpu.make_async_copy(result, out.at[:, span, :], sem)
    copy.start()
    copy.wait()


def attn_bwd_kernel(
    head, heads, blocks, tab, qkv, dot, log_sums, before, out, *scratch
):
    del before
    qs, ks, vs, kt, vt, ktt, dkt, dvt, dka, dva, result, sem = scratch
    part_blocks = blocks // 4
    split_head(head, heads * HEAD_DIM, qkv, qs, ks, vs)
    for j in range(TRUNK):
        rows = block_rows(tab[j])
        span = slice(j * BLOCK, (j + 1) * BLOCK)
        kt[span, :] = ks[rows, :]
        vt[span, :] = vs[rows, :]
        ktt[:, span] = ks[rows, :].T
    dkt[...] = jnp.zeros_like(dkt)
    dvt[...] = jnp.zeros_like(dvt)
    dka[...] = jnp.zeros_like(dka)
    dva[...] = jnp.zeros_like(dva)
    lanes = slice(head * HEAD_DIM, (head + 1) * HEAD_DIM)

    def run(tile, beside):
        pair, rows, masked = tile_places(tab, tile, blocks)
        queries = jnp.concatenate([qs[rows[0], :], qs[rows[1], :]], axis=0)
        places = [place_of(index, part_blocks) for index in pair]
        grads = jnp.concatenate([dot[q, lanes, columns] for q, columns in places], axis=1)
        parts = tile_scores(ks, kt[...], queries, rows, masked if beside else None)
        count = len(parts)
        row_sums = for_parts(log_sums[pl.ds(tile, 1), :], count)
        probs = [jnp.exp(part - row_sum) for part, row_sum in zip(parts, row_sums)]
        grad_parts = [dot_nn(vt[...], grads)]
        if beside:
            grad_parts.append(dot_nn(vs[rows[0], :], grads[:, :BLOCK]))
            grad_parts.append(dot_nn(vs[rows[1], :], grads[:, BLOCK:]))
            grad_parts.append(dot_nn(vs[rows[2], :], grads))
        products = [p * g for p, g in zip(probs, grad_parts)]
        deltas = for_parts(over_keys(jnp.sum, jnp.add, products), count)
        score_grads = [(p * (g - d)).astype(bf16) for p, g, d in zip(probs, grad_parts, deltas)]
        probs = [p.astype(bf16) for p in probs]
        dvt[...] += dot_nt(probs[0], grads)
        dkt[...] += dot_nn(score_grads[0], queries)
        query_grad = dot_nn(ktt[...], score_grads[0])
        if beside:
            dva[rows[0], :] += dot_nt(probs[1], grads[:, :BLOCK])
            dva[rows[1], :] += dot_nt(probs[2], grads[:, BLOCK:])
            dva[rows[2], :] += dot_nt(probs[3], grads)
            dka[rows[0], :] += dot_nn(score_grads[1], queries[:BLOCK])
            dka[rows[1], :] += dot_nn(score_grads[2], queries[BLOCK:])
            dka[rows[2], :] += dot_nn(score_grads[3], queries)
            own = [
                dot_tn(ks[rows[0], :], score_grads[1]),
                dot_tn(ks[rows[1], :], score_grads[2]),
            ]
            query_grad = query_grad + jnp.concatenate(own, axis=1)
            query_grad = query_grad + dot_tn(ks[rows[2], :], score_grads[3])
        query_grad = (query_grad * HEAD_DIM**-0.5).astype(bf16)
        result[0, :, rows[0]] = query_grad[:, :BLOCK]
        result[0, :, rows[1]] = query_grad[:, BLOCK:]

    tile_loops(blocks, run)
    for j in range(TRUNK):
        rows = block_rows(tab[j])
        span = slice(j * BLOCK, (j + 1) * BLOCK)
        dka[rows, :] = dkt[span, :]
        dva[rows, :] = dvt[span, :]
    result[1] = dka[...].T.astype(bf16)
    result[2] = dva[...].T.astype(bf16)
    copies = [
        pltpu.make_async_copy(
            result.at[i], out.at[pl.ds((i * heads + head) * HEAD_DIM, HEAD_DIM), :], sem.at[i]
        )
        for i in range(3)
    ]
    for copy in copies:
        copy.start()
    for copy in copies:
        copy.wait()


def attn_forward(table, qkv, before, head, heads, blocks):
    rows = qkv.shape[0]
    trunk = TRUNK * BLOCK
    return pl.pallas_call(
        functools.partial(attn_fwd_kernel, head, heads, blocks),
        out_shape=(
            jax.ShapeDtypeStruct(before.shape, bf16),
            jax.ShapeDtypeStruct((16, PAIR), f32),
        ),
        in_specs=[
            pl.BlockSpec(memory_space=pltpu.SMEM),
            pl.BlockSpec(memory_space=pltpu.VMEM),
            pl.BlockSpec(memory_space=pl.ANY),
        ],
        out_specs=(
            pl.BlockSpec(memory_space=pl.ANY),
            pl.BlockSpec(memory_space=pltpu.VMEM),
        ),
        input_output_aliases={2: 0},
        scratch_shapes=[pltpu.VMEM((rows, HEAD_DIM), bf16)] * 3
        + [pltpu.VMEM((trunk, HEAD_DIM), bf16), pltpu.VMEM((HEAD_DIM, trunk), bf16)]
        + [pltpu.VMEM((4, HEAD_DIM, rows // 4), bf16), pltpu.SemaphoreType.DMA],
        compiler_params=pltpu.CompilerParams(vmem_limit_bytes=32 << 20),
        cost_estimate=pl.CostEstimate(
            flops=6 * rows * trunk * BLOCK,
            bytes_accessed=8 * rows * HEAD_DIM,
            transcendentals=0,
        ),
        name="tree_attention",
    )(table, qkv, before)


def attn_backward(table, qkv, out_grad, log_sums, before, head, heads, blocks):
    rows = qkv.shape[0]
    trunk = TRUNK * BLOCK
    return pl.pallas_call(
        functools.partial(attn_bwd_kernel, head, heads, blocks),
        out_shape=jax.ShapeDtypeStruct(before.shape, bf16),
        in_specs=[
            pl.BlockSpec(memory_space=pltpu.SMEM),
            pl.BlockSpec(memory_space=pltpu.VMEM),
            pl.BlockSpec(memory_space=pltpu.VMEM),
            pl.BlockSpec(memory_space=pltpu.VMEM),
            pl.BlockSpec(memory_space=pl.ANY),
        ],
        out_specs=pl.BlockSpec(memory_space=pl.ANY),
        input_output_aliases={4: 0},
        scratch_shapes=[pltpu.VMEM((rows, HEAD_DIM), bf16)] * 3
        + [pltpu.VMEM((trunk, HEAD_DIM), bf16)] * 2
        + [pltpu.VMEM((HEAD_DIM, trunk), bf16)]
        + [pltpu.VMEM((trunk, HEAD_DIM), f32)] * 2
        + [pltpu.VMEM((rows, HEAD_DIM), f32)] * 2
        + [pltpu.VMEM((3, HEAD_DIM, rows), bf16), pltpu.SemaphoreType.DMA((3,))],
        compiler_params=pltpu.CompilerParams(vmem_limit_bytes=40 << 20),
        cost_estimate=pl.CostEstimate(
            flops=16 * rows * trunk * BLOCK,
            bytes_accessed=14 * rows * HEAD_DIM,
            transcendentals=0,
        ),
        name="tree_attention_grad",
    )(table, qkv, out_grad, log_sums, before)


def attention_table(path):
    blocks = path.shape[1]
    place = jnp.arange(blocks, dtype=jnp.int32)
    kind = (path[1] != path[0]).astype(jnp.int32) + (path[2] != path[1]).astype(jnp.int32)
    key = kind * 65536 + jnp.where(kind == 2, path[1] * 32, 0) + place
    rank = jnp.sum((key[None, :] < key[:, None]).astype(jnp.int32), axis=1)
    branch = jnp.sum(
        jnp.where((kind[None, :] == 1) & (path[2][None, :] == path[1][:, None]), place[None, :], 0),
        axis=1,
    )
    slot = (rank[None, :] == place[:, None]).astype(jnp.int32)
    columns = jnp.stack([place, jnp.where(kind == 2, branch, 0), kind])
    sorted_columns = jnp.sum(slot[None] * columns[:, None, :], axis=2)
    return jnp.concatenate([sorted_columns[0], sorted_columns[1, ::2], sorted_columns[2, ::2]])


def assemble_kernel(count, spans, flags, *refs):
    pieces, outs = refs[: 2 * count], refs[2 * count :]
    slab = pieces[0].shape[0]
    for j in range(2):
        for k in range(count):
            place = lax.rem(flags[0] + (count - k), count)
            rows = pl.ds(pl.multiple_of(place * slab, 16), slab)
            piece = pieces[j * count + k]
            for out, (lanes, kind) in zip(outs, spans):
                width = lanes.stop - lanes.start
                if kind == 1 or j == 0 and kind == 0:
                    out[rows, j * width : (j + 1) * width] = piece[:, lanes]
                for crossed in range(2 if kind == 2 else 0):

                    @pl.when(flags[1] == crossed)
                    def _():
                        first = (j ^ crossed) * width
                        out[rows, first : first + width] = piece[:, lanes]


def assembled(shard, crossed, own, twin, spans):
    count = len(own)
    rows = count * own[0].shape[0]
    vmem = pl.BlockSpec(memory_space=pltpu.VMEM)
    shapes = [
        jax.ShapeDtypeStruct((rows, (lanes.stop - lanes.start) * (2 if kind else 1)), bf16)
        for lanes, kind in spans
    ]
    return pl.pallas_call(
        functools.partial(assemble_kernel, count, spans),
        out_shape=shapes,
        in_specs=[pl.BlockSpec(memory_space=pltpu.SMEM)] + [vmem] * (2 * count),
        out_specs=[vmem] * len(spans),
        compiler_params=pltpu.CompilerParams(vmem_limit_bytes=24 << 20),
        cost_estimate=pl.CostEstimate(
            flops=0, bytes_accessed=4 * sum(piece.size for piece in own + twin), transcendentals=0
        ),
        name="assembled_weights",
    )(jnp.stack([shard, crossed]).astype(jnp.int32), *own, *twin)


def pack_kernel(count, j, flags, up, down, proj, out, small, *pieces):
    slab = up.shape[0] // count
    group = pieces[0].shape[1] - up.shape[1] - down.shape[1] - proj.shape[1]
    for k in range(count):
        place = lax.rem(flags[0] + (count - k - 1), count)
        rows = pl.ds(pl.multiple_of(place * slab, 16), slab)
        first = 0
        for source in (up, down, proj):
            pieces[k][:slab, first : first + source.shape[1]] = source[rows, :]
            first += source.shape[1]
        for crossed in range(2):

            @pl.when(flags[1] == crossed)
            def _():
                lane = (j ^ crossed) * group
                pieces[k][:slab, first:] = out[rows, lane : lane + group]

        pieces[k][slab:, :] = small[place]


def packed_pieces(shard, crossed, count, up, down, proj, out, small, j):
    rows = up.shape[0] // count + small.shape[1]
    width = small.shape[2]
    vmem = pl.BlockSpec(memory_space=pltpu.VMEM)
    return pl.pallas_call(
        functools.partial(pack_kernel, count, j),
        out_shape=[jax.ShapeDtypeStruct((rows, width), bf16)] * count,
        in_specs=[pl.BlockSpec(memory_space=pltpu.SMEM)] + [vmem] * 5,
        out_specs=[vmem] * count,
        compiler_params=pltpu.CompilerParams(vmem_limit_bytes=24 << 20),
        cost_estimate=pl.CostEstimate(
            flops=0, bytes_accessed=4 * count * rows * width, transcendentals=0
        ),
        name="packed_gradients",
    )(jnp.stack([shard, crossed]).astype(jnp.int32), up, down, proj, out, small)


def place_kernel(start, places, first, second, third, fourth, before, out, wide, sem):
    del before
    rows = first.shape[0]
    half, core = places[0], places[1]
    spots = [(half, core), (1 - half, core), (half, 1 - core), (1 - half, 1 - core)]
    copies = []
    for i, piece in enumerate((first, second, third, fourth)):
        wide[i] = piece[...].astype(wide.dtype)
        row, column = spots[i]
        target = out.at[row, column, pl.ds(start, rows), :]
        copy = pltpu.make_async_copy(wide.at[i], target, sem.at[i])
        copy.start()
        copies.append(copy)
    for copy in copies:
        copy.wait()


def place_rows(places, pieces, before, start):
    rows, width = pieces[0].shape
    vmem = pl.BlockSpec(memory_space=pltpu.VMEM)
    return pl.pallas_call(
        functools.partial(place_kernel, start),
        out_shape=jax.ShapeDtypeStruct(before.shape, before.dtype),
        in_specs=[pl.BlockSpec(memory_space=pltpu.SMEM)]
        + [vmem] * 4
        + [pl.BlockSpec(memory_space=pl.ANY)],
        out_specs=pl.BlockSpec(memory_space=pl.ANY),
        input_output_aliases={5: 0},
        scratch_shapes=[
            pltpu.VMEM((4, rows, width), before.dtype),
            pltpu.SemaphoreType.DMA((4,)),
        ],
        compiler_params=pltpu.CompilerParams(vmem_limit_bytes=24 << 20),
        cost_estimate=pl.CostEstimate(
            flops=0, bytes_accessed=24 * rows * width, transcendentals=0
        ),
        name="placed_rows",
    )(places, *pieces, before)


def student_kernel(part_blocks, labels, rows, weight, shift, query, student, weights, stats):
    width = weight.shape[1]
    pool_dim = width // POOL_HEADS
    value = dot_nn(rows[...], weight[...]) + shift[...]
    student[...] = value
    lane = lax.broadcasted_iota(jnp.int32, (1, width), 1)
    first_head = lane < pool_dim
    product = value * query[...]
    scores = [
        jnp.sum(product[:, e * pool_dim : (e + 1) * pool_dim], axis=1, keepdims=True)
        for e in range(POOL_HEADS)
    ]
    stats[...] = jnp.zeros_like(stats)
    for block in range(part_blocks):
        span = slice(block * BLOCK, (block + 1) * BLOCK)
        peaks = [jnp.max(score[span], axis=0, keepdims=True) for score in scores]
        exps = [jnp.exp(score[span] - peak) for score, peak in zip(scores, peaks)]
        masses = [jnp.sum(part, axis=0, keepdims=True) for part in exps]
        lanes = jnp.where(first_head, exps[0], exps[1])
        weights[span, :] = lanes
        stats[block : block + 1, :width] = jnp.sum(lanes * value[span], axis=0, keepdims=True)
        label = jnp.full((1, width), labels[block], jnp.int32).astype(f32)
        tail = jnp.where(lane == 4, label, 0.0)
        for place, part in enumerate(peaks + masses):
            tail = jnp.where(lane == place, part, tail)
        stats[block : block + 1, width:] = tail


def student_stats(labels, rows, weight, shift, query, part_blocks):
    count = rows.shape[0]
    width = weight.shape[1]
    vmem = pl.BlockSpec(memory_space=pltpu.VMEM)
    return pl.pallas_call(
        functools.partial(student_kernel, part_blocks),
        out_shape=(
            jax.ShapeDtypeStruct((count, width), f32),
            jax.ShapeDtypeStruct((count, width), f32),
            jax.ShapeDtypeStruct((8, 2 * width), f32),
        ),
        in_specs=[pl.BlockSpec(memory_space=pltpu.SMEM)] + [vmem] * 4,
        out_specs=(vmem,) * 3,
        cost_estimate=pl.CostEstimate(
            flops=2 * rows.size * width, bytes_accessed=2 * rows.size, transcendentals=count
        ),
        name="student_stats",
    )(labels, rows, weight, shift, query)


def pool_kernel(
    part_blocks,
    own,
    near,
    across,
    corner,
    member,
    leaf,
    dense,
    head,
    dense_shift,
    cls_shift,
    student,
    weights,
    query,
    student_low,
    grad_dense,
    grad_head,
    vectors,
):
    width = dense.shape[0]
    pool_dim = width // POOL_HEADS
    pool_scale = pool_dim ** (-0.5)
    stats = jnp.concatenate([own[...], near[...], across[...], corner[...]], axis=0)
    moment = stats[:, :width]
    seen = member[...] > 0.0
    is_leaf = leaf[...] > 0.0
    coeffs = []
    pooled = []
    for e in range(POOL_HEADS):
        peak = stats[:, width + e : width + e + 1]
        mass = stats[:, width + POOL_HEADS + e : width + POOL_HEADS + e + 1]
        top = jnp.max(jnp.where(seen, peak, MASK_VALUE), axis=0, keepdims=True)
        factor = jnp.where(seen, jnp.exp(jnp.where(seen, peak - top, MASK_VALUE)), 0.0)
        total = jnp.sum(factor * mass, axis=0, keepdims=True)
        total = jnp.where(total > 0.0, total, 1.0)
        coeff = factor / total
        coeffs.append(coeff)
        lanes = slice(e * pool_dim, (e + 1) * pool_dim)
        pooled.append(exact(coeff, moment[:, lanes], ((0,), (0,))))
    pooled = jnp.concatenate(pooled, axis=1)
    dense_out = jnp.tanh(exact(pooled, dense[...], ((1,), (0,))) + dense_shift[...])
    logits = exact(dense_out, head[...], ((1,), (0,))) + cls_shift[...]
    logits = logits - jnp.max(logits, axis=1, keepdims=True)
    chances = jnp.exp(logits)
    chances = chances / jnp.sum(chances, axis=1, keepdims=True)
    label = stats[:, width + 2 * POOL_HEADS : width + 2 * POOL_HEADS + 1]
    classes = lax.broadcasted_iota(jnp.int32, (1, width), 1).astype(f32)
    onehot = jnp.where(label == classes, 1.0, 0.0)
    grad_logits = jnp.where(is_leaf, chances - onehot, 0.0)
    grad_head[...] = exact(dense_out, grad_logits, ((0,), (0,)))
    grad_pre = exact(grad_logits, head[...], ((1,), (1,))) * (1.0 - dense_out * dense_out)
    grad_dense[...] = exact(pooled, grad_pre, ((0,), (0,)))
    grad_pooled = exact(grad_pre, dense[...], ((1,), (1,)))
    product = grad_pooled * pooled
    spread = []
    offset = []
    for e in range(POOL_HEADS):
        lanes = slice(e * pool_dim, (e + 1) * pool_dim)
        spread.append(exact(coeffs[e], grad_pooled[:, lanes], ((1,), (0,))))
        inner = jnp.sum(product[:, lanes], axis=1, keepdims=True)
        inner = jnp.broadcast_to(inner, (inner.shape[0], pool_dim))
        offset.append(exact(coeffs[e], inner, ((1,), (0,))))
    spread = jnp.concatenate(spread, axis=1)
    offset = jnp.concatenate(offset, axis=1)
    grad_query = jnp.zeros((1, width), f32)
    grad_shift = jnp.zeros((1, width), f32)
    first_head = lax.broadcasted_iota(jnp.int32, (1, width), 1) < pool_dim
    for block in range(part_blocks):
        span = slice(block * BLOCK, (block + 1) * BLOCK)
        value = student[span, :]
        weight = weights[span, :]
        row = spread[block : block + 1]
        product = value * row
        inner = jnp.where(
            first_head,
            jnp.sum(product[:, :pool_dim], axis=1, keepdims=True),
            jnp.sum(product[:, pool_dim:], axis=1, keepdims=True),
        )
        grad_score = weight * (inner - offset[block : block + 1])
        grad_query = grad_query + jnp.sum(grad_score * value, axis=0, keepdims=True)
        low = (weight * row + grad_score * query[...]).astype(bf16)
        student_low[span, :] = low
        grad_shift = grad_shift + jnp.sum(low.astype(f32), axis=0, keepdims=True)
    vectors[0:1, :] = jnp.sum(grad_pre, axis=0, keepdims=True)
    vectors[1:2, :] = jnp.sum(grad_logits, axis=0, keepdims=True)
    vectors[2:3, :] = grad_query * pool_scale
    vectors[3:4, :] = grad_shift
    vectors[4:8, :] = jnp.zeros((4, width), f32)


def pool_classifier(part_blocks, *operands):
    student = operands[-3]
    width = student.shape[1]
    return pl.pallas_call(
        functools.partial(pool_kernel, part_blocks),
        out_shape=(
            jax.ShapeDtypeStruct(student.shape, bf16),
            jax.ShapeDtypeStruct((width, width), f32),
            jax.ShapeDtypeStruct((width, width), f32),
            jax.ShapeDtypeStruct((8, width), f32),
        ),
        cost_estimate=pl.CostEstimate(
            flops=2000 * width * width, bytes_accessed=16 * student.size, transcendentals=0
        ),
        name="pool_classifier",
    )(*operands)


def body(
    tokens,
    cotangent,
    block_path,
    labels,
    w_attn_in,
    attn_bias,
    w_attn_out,
    w_up,
    up_bias,
    w_down,
    norm_gain,
    layer_bias,
    stu_proj,
    stu_bias,
    pool_query,
    stu_dense,
    stu_head,
    class_bias,
):
    row_count, model = tokens.shape[1:]
    own_blocks = labels.shape[1]
    tree_blocks = 2 * own_blocks
    group_width = w_attn_in.shape[2]
    heads = group_width // HEAD_DIM
    slab = w_up.shape[0]
    hidden = w_up.shape[1]
    shards = lax.axis_size("shard")
    trees = lax.axis_size("tree")
    stu_width = stu_proj.shape[1]
    pool_dim = stu_width // POOL_HEADS
    pool_scale = pool_dim ** (-0.5)
    class_count = class_bias.shape[0]
    part_rows = row_count // 2
    part_blocks = own_blocks // 2

    shard = lax.axis_index("shard")
    tree = lax.axis_index("tree")
    side = lax.axis_index("side")
    half = lax.axis_index("half")
    core = lax.axis_index("core")

    shift_rows = layer_bias.astype(f32)
    gain_rows = norm_gain.astype(f32)
    stu_shifts = stu_bias.astype(f32)
    pool_vec = pool_query.astype(f32)

    def by_shard(pieces):
        result = blank((shards,) + pieces[0].shape, pieces[0].dtype)
        for k, piece in enumerate(pieces):
            result = lax.dynamic_update_index_in_dim(result, piece, (shard - k) % shards, 0)
        return result

    def rows_of(array, part):
        place = (half, part * part_rows, 0)
        return lax.dynamic_slice(array, place, (1, part_rows, model))[0]

    own_part = rows_of(tokens, core)
    other_part = swap(own_part, "side")
    own_rest = rows_of(after(tokens, own_part), 1 - core)

    qkv_width = 3 * group_width
    bias_row = jnp.concatenate([attn_bias[0], jnp.zeros((group_width,), bf16), attn_bias[1]])
    up_rows = jnp.pad(up_bias.reshape(2, hidden // 2), ((0, 0), (0, qkv_width - hidden // 2)))
    qkv_message = jnp.concatenate(
        [
            w_attn_in.transpose(1, 0, 2).reshape(slab, qkv_width),
            bias_row[None],
            up_rows,
            jnp.zeros((13, qkv_width), bf16),
        ],
        axis=0,
    )
    qkv_twin = swap(after(qkv_message, own_part), "half")
    twin_bias = qkv_twin[slab + 1 : slab + 3, : hidden // 2].reshape(hidden)
    qkv_message = jnp.where(side == half, qkv_message, qkv_twin)
    qkv_bias = qkv_message[slab].astype(f32)
    qkv_pieces = [qkv_message]
    for k in range(1, shards):
        qkv_pieces.append(ring(qkv_pieces[-1]))
    other_twin = swap(after(other_part, qkv_pieces[2]), "core")
    tree_rows = jnp.concatenate([own_part, other_part, own_rest, other_twin], axis=0)
    qkv_weight = by_shard([piece[:slab] for piece in qkv_pieces]).reshape(model, qkv_width)

    stu_lanes = slice(hidden, hidden + stu_width)
    out_lanes = slice(hidden + stu_width, hidden + stu_width + group_width)
    message_one = jnp.concatenate([w_up, stu_proj, w_attn_out.T], axis=1)
    message_two = w_down.T
    own_one = [after(message_one, qkv_pieces[-1], other_twin)]
    own_one.append(ring(own_one[0]))
    twin_one = [swap(after(message_one, qkv_message), "half")]

    paths = lax.dynamic_index_in_dim(block_path, half, 0, keepdims=False)
    paths = lax.dynamic_slice_in_dim(paths, tree * tree_blocks, tree_blocks, 1)
    paths = after(paths, qkv_pieces[1])
    quarters = paths.reshape(3, 2, 2, part_blocks)
    quarters = jnp.where(side == 0, quarters, quarters[:, ::-1])
    quarters = jnp.where(core == 0, quarters, quarters[:, :, ::-1])
    table = attention_table(quarters.swapaxes(1, 2).reshape(3, tree_blocks))

    quarters = jnp.pad(quarters, ((0, 0),) * 3 + ((0, 8 - part_blocks),), constant_values=-1)
    quarters = quarters.reshape(3, 32)
    is_leaf = (quarters[1] != quarters[2]).astype(f32)
    member = jnp.any(quarters[2][:, None, None] == quarters.T[None, :, :], axis=2).astype(f32)
    member = member * is_leaf[None, :]
    leaf_column = is_leaf[:, None]
    lane_pad = stu_width - class_count
    dense_full = stu_dense.astype(f32)
    head_padded = jnp.pad(stu_head.astype(f32), ((0, 0), (0, lane_pad)))
    cls_padded = jnp.pad(
        class_bias.astype(f32)[None, :], ((0, 0), (0, lane_pad)), constant_values=MASK_VALUE
    )
    own_labels = lax.dynamic_slice(labels, (half, core * part_blocks), (1, part_blocks))[0]
    dense_shift = stu_bias[1:2].astype(f32)
    proj_shift = stu_bias[0:1].astype(f32)
    scaled_query = (pool_vec * pool_scale)[None, :]
    prepared = lax.optimization_barrier(
        (
            tree_rows,
            member,
            leaf_column,
            dense_full,
            head_padded,
            cls_padded,
            own_labels,
            dense_shift,
            proj_shift,
            scaled_query,
        )
    )
    tree_rows, member, leaf_column, dense_full, head_padded, cls_padded = prepared[:6]
    own_labels, dense_shift, proj_shift, scaled_query = prepared[6:]

    qkv = (dot_nn(tree_rows, qkv_weight) + qkv_bias).astype(bf16)
    attended = blank((4, group_width, part_rows), bf16)
    attended, sums_0 = attn_forward(table, qkv, attended, 0, heads, tree_blocks)
    twin_two = [swap(after(message_two, twin_one[0]), "half")]
    one = after(own_one[1], attended)
    own_one.append(ring(one))
    twin_one.append(swap(one, "half"))
    attended = after(attended, twin_one[0], twin_two[0])
    attended, sums_1 = attn_forward(table, qkv, attended, 1, heads, tree_blocks)
    one = after(own_one[2], attended)
    own_one.append(ring(one))
    twin_one.append(swap(one, "half"))
    attended = after(attended, twin_one[1])
    attended, sums_2 = attn_forward(table, qkv, attended, 2, heads, tree_blocks)
    twin_one.append(swap(after(own_one[3], attended), "half"))
    own_two = [after(message_two, attended)]
    own_two.append(ring(own_two[0]))
    attended = after(attended, twin_one[2])

    def exchange(pieces):
        return [
            pieces[0],
            swap(pieces[1], "core"),
            swap(pieces[2], "side"),
            diagonal(pieces[3]),
        ]

    def at(array, place):
        return lax.dynamic_index_in_dim(array, place, 0, keepdims=False)

    def placed(pieces, places):
        result = blank((len(pieces),) + pieces[0].shape, pieces[0].dtype)
        for piece, place in zip(pieces, places):
            result = lax.dynamic_update_index_in_dim(result, piece, place, 0)
        return result

    quarter_places = [0, 2, 1, 3]
    crossed = jnp.where(side == half, 0, 1)

    def in_quarters(pieces):
        kept, near, across, corner = pieces
        return jnp.stack([kept, across, near, corner])

    crossing = exchange([attended[place] for place in quarter_places])
    own_two.append(ring(after(own_two[1], crossing[1])))
    own_one[0] = after(own_one[0], *crossing[1:], own_two[2])
    heads_own = in_quarters(crossing)
    heads_own = heads_own.reshape(4 * group_width, part_rows)
    heads_own = after(heads_own, twin_one[3])
    up_weight, stu_weight, out_half = assembled(
        shard,
        crossed,
        own_one,
        twin_one,
        [(slice(0, hidden), 1), (stu_lanes, 0), (out_lanes, 2)],
    )
    twin_two.append(swap(after(own_two[1], up_weight), "half"))
    own_two.append(ring(after(own_two[2], up_weight)))
    out_weight = jnp.concatenate([out_half, swap(out_half, "core")], axis=1)
    twin_two.append(swap(after(own_two[2], up_weight), "half"))
    out_weight = after(out_weight, twin_two[1], twin_two[2], own_two[3])
    twin_two.append(swap(after(own_two[3], out_weight), "half"))
    hidden_shift = jnp.concatenate([up_bias, twin_bias]).astype(f32)

    attn = lax.dot_general(
        heads_own, out_weight, (((0,), (1,)), ((), ())), preferred_element_type=f32
    )
    resid_one = own_part.astype(f32) + (attn + shift_rows[0])
    hidden_one, normed_one, inverse_one = norm_forward(resid_one, gain_rows[0], shift_rows[2])
    hidden_low = hidden_one.astype(bf16)
    normed_one = lax.optimization_barrier(normed_one.astype(bf16)).astype(f32)

    hidden_both = jnp.concatenate([hidden_low, swap(hidden_low, "core")], axis=0)
    pre_act = dot_nn(hidden_both, up_weight) + hidden_shift
    normal_cdf = 0.5 * (1.0 + lax.erf(pre_act * 0.7071067811865476))
    active = (pre_act * normal_cdf).astype(bf16)
    slope = normal_cdf + pre_act * jnp.exp(-0.5 * pre_act * pre_act) * 0.3989422804014327
    slope = lax.optimization_barrier(slope.astype(bf16))
    own_two[0] = after(own_two[0], active)
    (down_weight,) = assembled(shard, crossed, own_two, twin_two, [(slice(0, hidden), 1)])
    ffn_far = swap(dot_nt(active[part_rows:], down_weight).astype(bf16), "core")
    ffn = dot_nt(active[:part_rows], down_weight) + ffn_far.astype(f32)
    hidden_two, normed_two, inverse_two = norm_forward(
        hidden_one + ffn + shift_rows[1], gain_rows[1], shift_rows[3]
    )
    block_low = hidden_two.astype(bf16)
    normed_two = lax.optimization_barrier(normed_two.astype(bf16)).astype(f32)

    def everywhere(rows, other):
        return rows, other, [swap(rows, "core"), swap(other, "core")]

    def placed(result, start, rows, other, twins):
        places = jnp.stack([half, core]).astype(jnp.int32)
        return place_rows(places, [rows, other] + twins, result, start)

    block_other = swap(block_low, "half")

    student, weights, stats = student_stats(
        own_labels, block_low, stu_weight, proj_shift, scaled_query, part_blocks
    )
    student_low, grad_dense, grad_head, pool_vectors = pool_classifier(
        part_blocks,
        *exchange([stats] * 4),
        member,
        leaf_column,
        dense_full,
        head_padded,
        dense_shift,
        cls_padded,
        student,
        weights,
        scaled_query,
    )
    grad_proj = dot_tn(block_low, student_low)

    upstream = lax.dynamic_slice(
        cotangent, (half, core * part_rows, 0), (1, part_rows, model)
    )[0].astype(f32)
    grad_two = upstream + dot_nt(student_low, stu_weight)
    resid_grad_two, gain_grad_two, shift_grad_two = norm_backward(
        grad_two, normed_two, inverse_two, gain_rows[1]
    )
    down_shift_grad = jnp.sum(resid_grad_two, axis=0)
    ffn_low = resid_grad_two.astype(bf16)
    ffn_twin = swap(ffn_low, "core")
    ffn_both = jnp.concatenate([ffn_low, ffn_twin], axis=0)
    pre_low = (dot_nn(ffn_both, down_weight) * slope).astype(bf16)
    grad_hidden_shift = jnp.sum(pre_low.astype(f32), axis=0)
    far_one = swap(dot_nt(pre_low[part_rows:], up_weight).astype(bf16), "core")
    grad_one = resid_grad_two + dot_nt(pre_low[:part_rows], up_weight) + far_one.astype(f32)

    resid_grad_one, gain_grad_one, shift_grad_one = norm_backward(
        grad_one, normed_one, inverse_one, gain_rows[0]
    )
    out_shift_grad = jnp.sum(resid_grad_one, axis=0)
    attn_low = resid_grad_one.astype(bf16)
    block_twin = swap(block_low, "core")
    heads_grad = lax.dot_general(
        out_weight, attn_low, (((0,), (1,)), ((), ())), preferred_element_type=f32
    ).astype(bf16)
    grad_out = lax.dot_general(
        attn_low, heads_own, (((0,), (1,)), ((), ())), preferred_element_type=f32
    ).astype(bf16)
    heads_grad = heads_grad.reshape(4, group_width, part_rows)
    pieces = [heads_grad[place] for place in quarter_places]
    pieces = lax.optimization_barrier(
        (*pieces, grad_out, ffn_low, ffn_twin, pre_low, block_twin)
    )
    ffn_low, ffn_twin, pre_low, block_twin = pieces[5:]
    ffn_both = jnp.concatenate([ffn_low, ffn_twin], axis=0)
    attended_grad = in_quarters(exchange(pieces[:4]))

    def halves(array):
        return [array[:, :hidden], array[:, hidden:]]

    grad_down = [dot_tn(ffn_both, part).astype(bf16) for part in halves(active)]
    grad_up = [dot_tn(hidden_both, part).astype(bf16) for part in halves(pre_low)]

    up_grad = jnp.zeros((4, hidden), f32)
    for j in range(2):
        up_grad = lax.dynamic_update_slice(
            up_grad,
            grad_hidden_shift[None, j * hidden : (j + 1) * hidden],
            (2 * jnp.where(j == 0, half, 1 - half) + core, 0),
        )
    first = jnp.where((side == 0) & (core == 0), 1.0, 0.0)
    pieces = [
        gain_grad_one,
        gain_grad_two,
        out_shift_grad,
        down_shift_grad,
        shift_grad_one,
        shift_grad_two,
        up_grad.reshape(-1),
        pool_vectors[3],
        pool_vectors[0] * first,
        pool_vectors[2],
        pool_vectors[1] * first,
        (grad_dense * first).reshape(-1),
        (grad_head[:, :16] * first).reshape(-1),
    ]
    sizes = [piece.size for piece in pieces]
    starts = [sum(sizes[:i]) for i in range(len(sizes) + 1)]
    packed = 2 * hidden + stu_width + group_width
    small = jnp.concatenate(pieces)
    small = jnp.pad(small, (0, -small.size % (shards * packed)))
    small_rows = small.size // (shards * packed)
    small = small.reshape(shards, small_rows, packed)
    small = jnp.pad(small, ((0, 0), (0, 16 - small_rows), (0, 0)))
    small = (small + swap(small, "core")).astype(bf16)

    half_out = 2 * group_width
    proj_low = grad_proj.astype(bf16)
    out_sum = grad_out[:, :half_out].astype(f32) + swap(grad_out[:, half_out:], "core").astype(f32)
    out_sum = out_sum.astype(bf16)
    proj_sum = (proj_low.astype(f32) + swap(proj_low, "core").astype(f32)).astype(bf16)
    out_sum = after(out_sum, attended_grad, block_other)
    block_far = swap(after(block_other, out_sum), "core")
    kept, sent = [
        packed_pieces(
            shard, crossed, shards, grad_up[j], grad_down[j], proj_sum, out_sum, small, j
        )
        for j in range(2)
    ]

    def reduced(k, got, last):
        total = kept[k].astype(f32) + got.astype(f32)
        if last is not None:
            total = total + last.astype(f32)
        return total.astype(bf16)

    qkv_grad = blank((qkv_width, 4 * part_rows), bf16)
    qkv_grad = after(qkv_grad, *sent)
    got = [swap(sent[0], "half"), swap(sent[1], "half")]
    qkv_grad = attn_backward(
        table, qkv, attended_grad, sums_0, qkv_grad, 0, heads, tree_blocks
    )
    kept = lax.optimization_barrier((qkv_grad, *kept))[1:]
    totals = [reduced(0, got[0], None)]
    passed = ring(totals[0])
    got.append(swap(after(sent[2], totals[0]), "half"))
    qkv_grad = after(qkv_grad, totals[0])
    qkv_grad = attn_backward(
        table, qkv, attended_grad, sums_1, qkv_grad, 1, heads, tree_blocks
    )
    totals.append(reduced(1, after(got[1], qkv_grad), passed))
    passed = ring(totals[1])
    got.append(swap(after(sent[3], totals[1]), "half"))
    qkv_grad = after(qkv_grad, totals[1])
    qkv_grad = attn_backward(
        table, qkv, attended_grad, sums_2, qkv_grad, 2, heads, tree_blocks
    )
    totals.append(reduced(2, after(got[2], qkv_grad), passed))
    passed = ring(totals[2])
    qkv_grad = after(qkv_grad, totals[2])

    def to_rows(columns):
        return lax.dot_general(
            columns, qkv_weight, (((0,), (1,)), ((), ())), preferred_element_type=f32
        ).astype(bf16)

    sent_grad = to_rows(qkv_grad[:, row_count:])
    near_grad = swap(sent_grad, "core")
    kept_grad = to_rows(after(qkv_grad, sent_grad)[:, :row_count])
    far_rows = kept_grad[part_rows:].astype(f32) + near_grad[part_rows:].astype(f32)
    far_rows = far_rows.astype(bf16)
    chunk = part_rows // 2
    spans = [slice(0, chunk), slice(chunk, part_rows)]

    grad_in = lax.dot_general(
        tree_rows, after(qkv_grad, far_rows), (((0,), (1,)), ((), ())), preferred_element_type=f32
    )
    grad_in = grad_in.astype(bf16).reshape(shards, 2, slab // 2, qkv_width)
    kept_in = lax.dynamic_index_in_dim(grad_in, half, 1, keepdims=False)
    sent_in = lax.dynamic_index_in_dim(grad_in, 1 - half, 1, keepdims=False)
    bias_sums = jnp.sum(qkv_grad.astype(f32), axis=1).astype(bf16)
    bias_rows = bias_sums.reshape(shards, 1, qkv_width // shards)
    bias_rows = jnp.pad(bias_rows, ((0, 0), (0, 15), (0, qkv_width - qkv_width // shards)))
    far_first = swap(far_rows[spans[0]], "side")
    sent_in, far_rows, far_first = lax.optimization_barrier(
        (jnp.concatenate([sent_in, bias_rows], axis=1), far_rows, far_first)
    )
    far_second = swap(far_rows[spans[1]], "side")
    got_in = swap(sent_in, "half")
    kept_in = jnp.concatenate([kept_in, bias_rows], axis=1)

    def at_in(k):
        place = (shard - k) % shards
        return at(kept_in, place).astype(f32) + at(got_in, place).astype(f32)

    def tokens_part(i, far):
        near = kept_grad[:part_rows][spans[i]].astype(f32)
        near = near + near_grad[:part_rows][spans[i]].astype(f32)
        return (resid_grad_one[spans[i]] + near + far.astype(f32)).astype(bf16)

    tokens_grad = blank((2, 2, part_rows, model), f32)
    total = reduced(3, got[3], passed)
    got_in, far_second, total = lax.optimization_barrier((got_in, far_second, total))
    chip_in = (kept_in.astype(f32) + got_in.astype(f32)).astype(bf16)
    rows_low, rows_high = [tokens_part(i, far) for i, far in enumerate((far_first, far_second))]
    rows_all = jnp.concatenate([rows_low, rows_high], axis=0)
    chip_in, rows_all, total = lax.optimization_barrier((chip_in, rows_all, total))
    other_all = swap(rows_all, "half")
    total_far = swap(total, "side")
    parts_in = [at(chip_in, shard)]
    for k in range(1, shards):
        pairs = [(i, (i + k) % shards) for i in range(shards)]
        sent_part = at(chip_in, (shard + k) % shards)
        parts_in.append(lax.ppermute(sent_part, "shard", pairs))
    block_out = placed(
        blank((2, 2, part_rows, model), bf16), 0, after(block_low, rows_all), block_other, [block_twin, block_far]
    )
    gathered = lax.optimization_barrier(
        (other_all, total_far, *parts_in, rows_all, total, block_out)
    )
    other_all, total_far, parts_in = gathered[0], gathered[1], gathered[2 : 2 + shards]
    rows_all, total, block_out = gathered[2 + shards :]
    block_out = block_out.reshape(2, row_count, model)
    part = sum(piece.astype(f32) for piece in parts_in)
    total = total.astype(f32) + total_far.astype(f32)
    if trees > 1:
        total = lax.psum(total, "tree")
        part = lax.psum(part, "tree")
    part = part.astype(bf16)
    half_slab = slab // 2
    part_twin = swap(part[:half_slab], "half")
    twins = [swap(rows_all, "core"), swap(other_all, "core")]
    bias_part = jnp.pad(part[half_slab : half_slab + 1], ((0, 0), (0, packed - qkv_width)))
    small = jnp.concatenate([total[slab : slab + small_rows], bias_part.astype(f32)], axis=0)
    small = jnp.pad(small, ((0, 16 - small.shape[0]), (0, 0))).astype(bf16)[None]

    def joined(own, other, bit):
        low = (shard // bit) % 2 == 0
        return jnp.concatenate([jnp.where(low, own, other), jnp.where(low, other, own)], axis=0)

    small_other = over_shards(small, 1)
    part_twin, twins[0], twins[1], part, small, small_other = lax.optimization_barrier(
        (part_twin, *twins, part, small, small_other)
    )
    small = joined(small, small_other, 1)
    step = 2
    while step < shards:
        small = joined(small, over_shards(small, step), step)
        step *= 2
    tokens_grad = placed(tokens_grad, 0, rows_all, other_all, twins)
    tokens_grad = tokens_grad.reshape(2, row_count, model)
    small = small.astype(f32)
    bias_own = small[:, small_rows, : qkv_width // shards].reshape(1, qkv_width)
    small = small[:, :small_rows].reshape(-1)

    group_in = jnp.concatenate(
        [
            jnp.where(half == 0, part[:half_slab], part_twin),
            jnp.where(half == 0, part_twin, part[:half_slab]),
            jnp.pad(bias_own.astype(bf16), ((0, 15), (0, 0))),
        ],
        axis=0,
    )
    group_in = jnp.where(side == half, group_in, swap(group_in, "side")).astype(f32)
    grad_in_own = group_in[:slab].reshape(slab, 3, group_width).transpose(1, 0, 2)
    bias_own = group_in[slab]

    def taken(low, high):
        return small[starts[low] : starts[high]]

    position = 2 * half + core
    return (
        block_out,
        tokens_grad,
        grad_in_own,
        jnp.stack([bias_own[:group_width], bias_own[2 * group_width : qkv_width]]),
        total[:slab, 2 * hidden + stu_width :].T,
        total[:slab, :hidden],
        lax.dynamic_slice_in_dim(taken(6, 7), position * hidden, hidden, 0),
        total[:slab, hidden : 2 * hidden].T,
        taken(0, 2).reshape(2, model),
        taken(2, 6).reshape(4, model),
        total[:slab, 2 * hidden : 2 * hidden + stu_width],
        taken(7, 9).reshape(2, stu_width),
        taken(9, 10),
        taken(11, 12).reshape(stu_width, stu_width),
        taken(12, 13).reshape(stu_width, 16)[:, :class_count],
        taken(10, 11)[:class_count],
    )


def solution(mesh):
    shape = dict(mesh.shape)
    split = Mesh(
        mesh.devices.reshape(shape["shard"], shape["ctx"] // 2, 2, 2, shape["tp"] // 2),
        ("shard", "tree", "side", "half", "core"),
    )
    ctx = ("tree", "side")
    tp = ("half", "core")
    rows = ("shard",) + ctx
    in_specs = (
        P(None, rows, None),
        P(None, rows, None),
        P(None, None, "shard"),
        P(None, rows),
        P(None, "shard", tp),
        P(None, tp),
        P(tp, "shard"),
        P("shard", tp),
        P(tp),
        P(tp, "shard"),
        P(),
        P(),
        P("shard", None),
        P(),
        P(),
        P(),
        P(),
        P(),
    )
    out_specs = (
        P(None, rows, None),
        P(None, rows, None),
        P(None, "shard", tp),
        P(None, tp),
        P(tp, "shard"),
        P("shard", tp),
        P(tp),
        P(tp, "shard"),
        P(),
        P(),
        P("shard", None),
        P(),
        P(),
        P(),
        P(),
        P(),
    )
    return jax.shard_map(body, mesh=split, in_specs=in_specs, out_specs=out_specs, check_vma=False)
```
